32 devices in a mesh: row: 4 (over y, core), col: 8 (over z, x).
Axes of the slice: x: 2, y: 2, z: 4, core: 2. Of those that a mesh axis runs over, the one named last changes fastest.
Arguments:
- spectra: float32 [2, 16, 1024, 512], P(None, None, ('col', 'row')), as said below
- pair_mask: int32 [4, 8], P('row', 'col'), may hold values 0 or 1
- band_range: int32 [2], replicated, may hold values from 0 to 512, as said below
Outputs:
- correlations: bfloat16 [1024, 1024, 201], P('row', 'col')
The draws below stay inside these ranges and needn't reach their ends.
Inputs may be any that keep to these rules, and one draw needn't show every extreme that they name: `spectra`: every channel's spectrum carries its own amplitude. band_range[0] < band_range[1].
All inputs are finite; a program needn't handle non-finite values. No bound on the sum of `pair_mask` on one device may be relied on, other than what follows from the above.
Results may differ from the reference program's by a relative error of at most 0.0061.
Values may be sent and summed in bfloat16 or wider, within the bound.
No kernel may reach another device: no remote copies, remote signals or barrier semaphores. Data moves between devices by JAX's collectives and lax.ppermute only.
A program may use at most 320 MiB of HBM per device.

```python
import math
import jax
import jax.numpy as jnp
from jax import lax

CB = 128
W = 16
FB = 512
LAGS = 201
NFFT = 15000
F0 = 60
CHANNELS = 1024
N_ROW = 4
N_COL = 8


def draw_spectra(key, part):
    first, second, third = jax.random.split(key, 3)
    shape_full = (2, W, CHANNELS, FB)
    base = jax.random.normal(first, shape_full, jnp.float32)
    channel_scale = jnp.exp(jax.random.uniform(second, (1, 1, CHANNELS, 1), jnp.float32, 0.0, math.log(10.0)))
    freq_scale = jnp.exp(jax.random.uniform(third, (1, W, 1, FB), jnp.float32, math.log(0.3), math.log(3.0)))
    return base * channel_scale * freq_scale


def draw_band_range(key, part):
    first, second = jax.random.split(key, 2)
    lower = jax.random.randint(first, (1,), 0, FB // 8 + 1, jnp.int32)
    upper = jax.random.randint(second, (1,), FB - FB // 8, FB + 1, jnp.int32)
    return jnp.concatenate([lower, upper]).astype(jnp.int32)


def with_ends(array, rng, least, top_value):
    index_at = [jax.random.randint(jax.random.fold_in(rng, axis), (), 0, length) for axis, length in enumerate(array.shape)]
    widest = array.shape.index(max(array.shape))
    beside = index_at[:widest] + [(index_at[widest] + 1) % array.shape[widest]] + index_at[widest + 1:]
    return array.at[tuple(index_at)].set(least).at[tuple(beside)].set(top_value)


def setup_inputs(seed: int = 0) -> dict:
    key_of = jax.random.split(jax.random.key(seed), 4)
    return {
        "spectra": draw_spectra(jax.random.fold_in(key_of[3], 71), 0),
        "pair_mask": with_ends((jax.random.randint(key_of[1], (N_ROW, N_COL), 0, 4) < 3).astype(jnp.int32), jax.random.fold_in(key_of[1], 1), 0, 1),
        "band_range": draw_band_range(jax.random.fold_in(key_of[3], 71), 0),
    }


EPS = 1e-06

def whiten(spectra):
    power_mean = lax.optimization_barrier(jnp.mean(spectra[0] * spectra[0] + spectra[1] * spectra[1], axis=-1, keepdims=True))
    return (spectra * lax.rsqrt(power_mean + EPS)).astype(jnp.bfloat16)

def make_table(band_range):
    freq_index = jnp.arange(FB, dtype=jnp.int32)
    lag_index = jnp.arange(LAGS, dtype=jnp.int32) - LAGS // 2
    turns = jnp.mod((F0 + freq_index)[:, None] * lag_index[None, :], NFFT)
    theta = turns.astype(jnp.float32) * (2.0 * math.pi / NFFT)
    inband = ((freq_index >= band_range[0]) & (freq_index < band_range[1])).astype(jnp.float32)[:, None]
    return jnp.concatenate([inband * jnp.cos(theta), -inband * jnp.sin(theta)], axis=0).astype(jnp.bfloat16)

def pair_block(row_block, col_block, lag_table):
    rows_wide = row_block.astype(jnp.float32)
    cols_wide = col_block.astype(jnp.float32)
    real_part = jnp.einsum('wap,wbp->abp', rows_wide[0], cols_wide[0]) + jnp.einsum('wap,wbp->abp', rows_wide[1], cols_wide[1])
    imag_part = jnp.einsum('wap,wbp->abp', rows_wide[1], cols_wide[0]) - jnp.einsum('wap,wbp->abp', rows_wide[0], cols_wide[1])
    cross = jnp.stack([real_part, imag_part], axis=2).astype(jnp.bfloat16)
    cross = lax.optimization_barrier(cross)
    height = rows_wide.shape[2]
    flat = cross.reshape(height * CB, 2 * FB).astype(jnp.float32)
    table_wide = lax.optimization_barrier(lag_table).astype(jnp.float32)
    summed = jnp.dot(flat, table_wide, preferred_element_type=jnp.float32)
    return (summed * (1.0 / math.sqrt(W * FB))).astype(jnp.bfloat16).reshape(height, CB, LAGS)

def reference(spectra, pair_mask, band_range):
    whitened = whiten(spectra)
    lag_table = make_table(band_range)
    blocks_per_row = N_COL // N_ROW
    row_width = CB * blocks_per_row

    def one_row(row_id):
        row_block = lax.dynamic_slice_in_dim(whitened, row_id * row_width, row_width, 2)

        def one_col(col_id):
            col_block = lax.dynamic_slice_in_dim(whitened, col_id * CB, CB, 2)
            request = (pair_mask[row_id, col_id] == 1) & (col_id >= row_id * blocks_per_row)
            return lax.cond(request, lambda: pair_block(row_block, col_block, lag_table), lambda: jnp.zeros((row_width, CB, LAGS), jnp.bfloat16))
        blocks = lax.map(one_col, jnp.arange(N_COL, dtype=jnp.int32))
        return jnp.transpose(blocks, (1, 0, 2, 3)).reshape(row_width, CHANNELS, LAGS)
    rows_out = lax.map(one_row, jnp.arange(N_ROW, dtype=jnp.int32))
    return rows_out.reshape(CHANNELS, CHANNELS, LAGS)
```

```python
import functools
import math

import jax
import jax.numpy as jnp
from jax import lax
from jax.experimental import pallas as pl
from jax.experimental.pallas import tpu as pltpu
from jax.sharding import PartitionSpec as P

W = 16
FB = 512
LAGS = 201
NFFT = 15000
F0 = 60
EPS = 1e-06

SEGMENTS = 4
ROWS = FB // SEGMENTS
PAIRS = ROWS // 2
LAG_PAD = 208


def whiten_kernel(*refs, width, parts):
    x_refs, out_refs, scratch = refs[:SEGMENTS], refs[SEGMENTS : SEGMENTS + parts], refs[-1]

    def channel(c, carry):
        tiles = [x_ref[pl.ds(c, 2 * W, stride=width), :] for x_ref in x_refs]
        total = sum(v[:W] * v[:W] + v[W:] * v[W:] for v in tiles)
        power = jnp.sum(total, axis=-1, keepdims=True) * (1.0 / FB)
        scale = lax.rsqrt(power + EPS)
        scale = jnp.concatenate([scale, scale], axis=0)
        stacked = jnp.concatenate([v * scale for v in tiles], axis=0)
        scratch[pl.ds(c, ROWS, stride=width), :] = stacked.T
        return carry

    lax.fori_loop(0, width, channel, 0, unroll=2)
    step = width // parts
    full = scratch[...].reshape(ROWS, width, 128).astype(jnp.bfloat16)
    for g in range(parts):
        out_refs[g][...] = full[:, g * step : (g + 1) * step, :]


def whiten(spectra, parts):
    width = spectra.shape[2]
    step = width // parts
    lines = 2 * W * width
    flat = spectra.reshape(lines, FB)
    return pl.pallas_call(
        functools.partial(whiten_kernel, width=width, parts=parts),
        out_shape=[jax.ShapeDtypeStruct((ROWS, step, 128), jnp.bfloat16)] * parts,
        grid=(1,),
        in_specs=[pl.BlockSpec((lines, ROWS), functools.partial(lambda q, i: (0, q), q)) for q in range(SEGMENTS)],
        out_specs=[pl.BlockSpec((ROWS, step, 128), lambda i: (0, 0, 0))] * parts,
        scratch_shapes=[pltpu.VMEM((ROWS * width, 128), jnp.float32)],
        compiler_params=pltpu.CompilerParams(vmem_limit_bytes=40 << 20),
        name="whiten",
    )(*[flat] * SEGMENTS)


def weights_kernel(offset_ref, *refs, count, step):
    in_refs, out_ref, scratch = refs[:count], refs[count], refs[count + 1]
    for i in range(count):
        at = pl.multiple_of(offset_ref[i], step)
        scratch[:, pl.ds(at, step), :] = in_refs[i][...].astype(jnp.float32)

    def row(t, carry):
        for s in range(2):
            real = scratch[2 * t + s].T
            pieces = []
            for q in range(SEGMENTS):
                lo = q * 2 * W
                pieces += [-real[lo + W : lo + 2 * W], real[lo : lo + W]]
            imag = jnp.concatenate(pieces, axis=0)
            both = jnp.concatenate([real, imag], axis=1).astype(jnp.bfloat16)
            out_ref[t, s * 128 : (s + 1) * 128, :] = both
        return carry

    lax.fori_loop(0, out_ref.shape[0], row, 0, unroll=2)


def weights(offsets, shards):
    count = len(shards)
    step = shards[0].shape[1]
    tiles = 4
    return pl.pallas_call(
        functools.partial(weights_kernel, count=count, step=step),
        out_shape=jax.ShapeDtypeStruct((PAIRS, 256, 256), jnp.bfloat16),
        grid_spec=pltpu.PrefetchScalarGridSpec(
            num_scalar_prefetch=1,
            grid=(tiles,),
            in_specs=[pl.BlockSpec((ROWS // tiles, step, 128), lambda i, o: (i, 0, 0))] * count,
            out_specs=pl.BlockSpec((PAIRS // tiles, 256, 256), lambda i, o: (i, 0, 0)),
            scratch_shapes=[pltpu.VMEM((ROWS // tiles, count * step, 128), jnp.float32)],
        ),
        compiler_params=pltpu.CompilerParams(vmem_limit_bytes=40 << 20),
        name="weights",
    )(offsets, *shards)


def pair_kernel(meta_ref, *refs, count, step, unroll_sum, unroll_lag):
    x_refs = refs[:count]
    w_ref, t_ref, _, out_ref = refs[count : count + 4]
    xbuf, wide, wbuf, tbuf, cross, lags, stage, sems = refs[count + 4 :]
    height = count * step

    @pl.when(meta_ref[0] == 1)
    def _():
        copies = [
            pltpu.make_async_copy(x_refs[i], xbuf.at[:, i * step : (i + 1) * step, :], sems.at[i])
            for i in range(count)
        ]
        copies.append(pltpu.make_async_copy(w_ref, wbuf, sems.at[count]))
        copies.append(pltpu.make_async_copy(t_ref, tbuf, sems.at[count + 1]))
        for copy in copies:
            copy.start()
        for copy in copies[:count]:
            copy.wait()
        wide[...] = xbuf[...].astype(jnp.float32).reshape(ROWS * height, 128)
        for copy in copies[count:]:
            copy.wait()

        sub = lax.broadcasted_iota(jnp.int32, (8, 128), 0)
        segment = lax.broadcasted_iota(jnp.int32, (8, 128), 1) // (2 * W)
        masks = (segment == sub, segment == sub - SEGMENTS)

        def window_sums(h, carry):
            halves = []
            for u in range(2):
                pair = 2 * h + u
                rows = []
                for a in range(height):
                    halves_of_k = [
                        jnp.where(masks[s], wide[pl.ds((2 * pair + s) * height + a, 8, stride=0), :], 0.0)
                        for s in range(2)
                    ]
                    rows.append(jnp.concatenate(halves_of_k, axis=1))
                left = jnp.concatenate(rows, axis=0).astype(jnp.bfloat16)
                sums = jnp.dot(left, wbuf[pair], preferred_element_type=jnp.float32)
                halves.append(sums.reshape(height, 8, 256))
            both = jnp.concatenate(halves, axis=1).astype(jnp.bfloat16)
            cross[:, pl.ds(pl.multiple_of(h * 16, 16), 16), :] = both
            return carry

        lax.fori_loop(0, PAIRS // 2, window_sums, 0, unroll=unroll_sum)

        def lag_sums(h, carry):
            first, second = cross[2 * h], cross[2 * h + 1]
            real = jnp.concatenate([first[:, :128], second[:, :128]], axis=1)
            imag = jnp.concatenate([first[:, 128:], second[:, 128:]], axis=1)
            right = jnp.concatenate([real, imag], axis=0)
            out = jnp.dot(tbuf[...], right, preferred_element_type=jnp.float32)
            out = out * (1.0 / math.sqrt(W * FB))
            lags[pl.ds(2 * h, LAG_PAD, stride=height), :] = out[:, :128]
            lags[pl.ds(2 * h + 1, LAG_PAD, stride=height), :] = out[:, 128:]
            return carry

        lax.fori_loop(0, height // 2, lag_sums, 0, unroll=unroll_lag)
        full = lags[...].reshape(LAG_PAD, height, 128)[:LAGS].astype(jnp.bfloat16)
        stage[...] = full
        backs = [
            pltpu.make_async_copy(
                stage.at[:, i * step : (i + 1) * step, :],
                out_ref.at[:, pl.ds(pl.multiple_of(meta_ref[1 + i], step), step), :],
                sems.at[i],
            )
            for i in range(count)
        ]
        for back in backs:
            back.start()
        for back in backs:
            back.wait()


def pair_block(meta, shards, right, table, out, unroll_sum=2, unroll_lag=2):
    count = len(shards)
    step = shards[0].shape[1]
    height = count * step
    anywhere = pl.BlockSpec(memory_space=pl.ANY)
    return pl.pallas_call(
        functools.partial(pair_kernel, count=count, step=step, unroll_sum=unroll_sum, unroll_lag=unroll_lag),
        out_shape=jax.ShapeDtypeStruct(out.shape, out.dtype),
        grid_spec=pltpu.PrefetchScalarGridSpec(
            num_scalar_prefetch=1,
            grid=(),
            in_specs=[anywhere] * (count + 3),
            out_specs=anywhere,
            scratch_shapes=[
                pltpu.VMEM((ROWS, height, 128), jnp.bfloat16),
                pltpu.VMEM((ROWS * height, 128), jnp.float32),
                pltpu.VMEM((PAIRS, 256, 256), jnp.bfloat16),
                pltpu.VMEM((LAG_PAD, 2 * FB), jnp.bfloat16),
                pltpu.VMEM((height, FB, 256), jnp.bfloat16),
                pltpu.VMEM((LAG_PAD * height, 128), jnp.float32),
                pltpu.VMEM((LAGS, height, 128), jnp.bfloat16),
                pltpu.SemaphoreType.DMA((count + 2,)),
            ],
        ),
        input_output_aliases={count + 3: 0},
        compiler_params=pltpu.CompilerParams(vmem_limit_bytes=60 << 20),
        cost_estimate=pl.CostEstimate(
            flops=2 * height * FB * 256 * 8 * 32 + 2 * height * 128 * 2 * FB * LAG_PAD,
            bytes_accessed=PAIRS * 256 * 256 * 2 + 2 * height * 128 * LAGS,
            transcendentals=0,
        ),
        name="pair_block",
    )(meta, *shards, right, table, out)


def make_table(band_range):
    order = jnp.arange(FB, dtype=jnp.int32)
    freq_index = (order % SEGMENTS) * ROWS + order // SEGMENTS
    lag_index = jnp.arange(LAG_PAD, dtype=jnp.int32) - LAGS // 2
    turns = jnp.mod((F0 + freq_index)[None, :] * lag_index[:, None], NFFT)
    theta = turns.astype(jnp.float32) * (2.0 * math.pi / NFFT)
    inband = ((freq_index >= band_range[0]) & (freq_index < band_range[1])).astype(jnp.float32)[None, :]
    return jnp.concatenate([inband * jnp.cos(theta), -inband * jnp.sin(theta)], axis=1).astype(jnp.bfloat16)


def bystander_body(whitened, request, table, out):
    (shard,) = whitened
    width = shard.shape[1]
    row_count = lax.axis_size("row")
    blocks_per_row = lax.axis_size("col") // row_count
    column = lax.all_gather(shard, "row", axis=1, tiled=True)
    strided = lax.all_gather(shard, "col", axis=0)
    grouped = strided.reshape(row_count, blocks_per_row, ROWS, width, 128)
    moved = lax.all_to_all(grouped, "row", split_axis=0, concat_axis=0)
    block = jnp.transpose(moved, (2, 1, 0, 3, 4)).reshape(ROWS, blocks_per_row * row_count * width, 128)
    right = weights(jnp.zeros((1,), jnp.int32), [column])
    group = min(64, block.shape[1])
    for at in range(0, block.shape[1], group):
        meta = jnp.stack([request, jnp.int32(at)])
        out = pair_block(meta, [block[:, at : at + group]], right, table, out)
    return out


def relay_body(whitened, request, table, out, row_count, blocks_per_row):
    (shard,) = whitened
    width = shard.shape[1]
    row_id = lax.axis_index("row")
    col_id = lax.axis_index("col")
    plane = col_id // blocks_per_row
    side = col_id % blocks_per_row
    depth = plane - row_id
    devices = [(r, p, x) for r in range(row_count) for p in range(row_count) for x in range(blocks_per_row)]

    def number(r, p, x):
        return (r * row_count + p) * blocks_per_row + x

    def move(value, pairs):
        return lax.ppermute(value, ("row", "col"), [(number(*a), number(*b)) for a, b in pairs])

    def core_flip(value):
        return move(value, [((r, p, x), (r ^ 1, p, x)) for r, p, x in devices])

    def chip_flip(value):
        return move(value, [((r, p, x), (r ^ 2, p, x)) for r, p, x in devices])

    across = chip_flip(shard)
    own = [shard, core_flip(shard), across, core_flip(across)]
    count = len(own)
    offsets = jnp.stack([(row_id ^ k) * width for k in range(count)])
    right = weights(offsets, own)
    came = None
    for s in range(count + row_count - 1):
        busy = [(r, p, x) for r, p, x in devices if p >= r and 0 <= s - (p - r) < count]
        if s == 0:
            front = own[0]
        elif s < count:
            front = jnp.where(depth == 0, own[s], came)
        else:
            front = came
        came = move(front, [((r, p, x), (r, p + 1, x)) for r, p, x in busy if p + 1 < row_count])
        other = move(front, [((r, p, x), (r, p, 1 - x)) for r, p, x in busy])
        k = s - depth
        valid = jnp.where((k >= 0) & (k < count), request, 0)
        source = row_id ^ jnp.clip(k, 0, count - 1)
        meta = jnp.stack(
            [valid, (side * row_count + source) * width, ((1 - side) * row_count + source) * width]
        ).astype(jnp.int32)
        out = pair_block(meta, [front, other], right, table, out, 4, 4)
    return out


def body(spectra, pair_mask, band_range):
    row_id = lax.axis_index("row")
    col_id = lax.axis_index("col")
    row_count = lax.axis_size("row")
    blocks_per_row = lax.axis_size("col") // row_count
    width = spectra.shape[2]
    whitened = whiten(spectra, 1)
    request = ((pair_mask[0, 0] == 1) & (col_id >= row_id * blocks_per_row)).astype(jnp.int32)
    table = make_table(band_range)
    out = jnp.zeros((LAGS, blocks_per_row * row_count * width, row_count * width), jnp.bfloat16)
    if row_count == 4 and blocks_per_row == 2:
        out = relay_body(whitened, request, table, out, row_count, blocks_per_row)
    else:
        out = bystander_body(whitened, request, table, out)
    return jnp.transpose(out, (1, 2, 0))


def solution(mesh):
    return jax.shard_map(
        body,
        mesh=mesh,
        in_specs=(P(None, None, ("col", "row"), None), P("row", "col"), P()),
        out_specs=P("row", "col", None),
        check_vma=False,
    )
```

```python
import functools
import math

import jax
import jax.numpy as jnp
from jax import lax
from jax.experimental import pallas as pl
from jax.experimental.pallas import tpu as pltpu
from jax.sharding import Mesh
from jax.sharding import PartitionSpec as P

W = 16
FB = 512
LAGS = 201
NFFT = 15000
F0 = 60
EPS = 1e-06

SEGMENTS = 4
ROWS = FB // SEGMENTS
PAIRS = ROWS // 2
LAG_PAD = 208


def whiten_kernel(*refs, width, parts):
    x_refs, whole_ref, out_refs, scratch = refs[:SEGMENTS], refs[SEGMENTS], refs[SEGMENTS + 1 : -1], refs[-1]

    def channel(c, carry):
        tiles = [x_ref[pl.ds(c, 2 * W, stride=width), :] for x_ref in x_refs]
        total = sum(v[:W] * v[:W] + v[W:] * v[W:] for v in tiles)
        power = jnp.sum(total, axis=-1, keepdims=True) * (1.0 / FB)
        scale = lax.rsqrt(power + EPS)
        scale = jnp.concatenate([scale, scale], axis=0)
        stacked = jnp.concatenate([v * scale for v in tiles], axis=0)
        scratch[pl.ds(c, ROWS, stride=width), :] = stacked.T
        return carry

    lax.fori_loop(0, width, channel, 0, unroll=2)
    step = width // parts
    full = scratch[...].reshape(ROWS, width, 128).astype(jnp.bfloat16)
    whole_ref[...] = full
    for g, out_ref in enumerate(out_refs):
        out_ref[...] = full[:, g * step : (g + 1) * step, :]


def whiten(spectra, parts):
    width = spectra.shape[2]
    widths = [width] + ([width // parts] * parts if parts > 1 else [])
    lines = 2 * W * width
    flat = spectra.reshape(lines, FB)
    return pl.pallas_call(
        functools.partial(whiten_kernel, width=width, parts=parts),
        out_shape=[jax.ShapeDtypeStruct((ROWS, n, 128), jnp.bfloat16) for n in widths],
        grid=(1,),
        in_specs=[pl.BlockSpec((lines, ROWS), functools.partial(lambda q, i: (0, q), q)) for q in range(SEGMENTS)],
        out_specs=[pl.BlockSpec((ROWS, n, 128), lambda i: (0, 0, 0)) for n in widths],
        scratch_shapes=[pltpu.VMEM((ROWS * width, 128), jnp.float32)],
        compiler_params=pltpu.CompilerParams(vmem_limit_bytes=40 << 20),
        name="whiten",
    )(*[flat] * SEGMENTS)


def weights_kernel(offset_ref, *refs, count, step):
    in_refs, out_ref, scratch = refs[:count], refs[count], refs[count + 1]
    for i in range(count):
        at = pl.multiple_of(offset_ref[i], step)
        scratch[:, pl.ds(at, step), :] = in_refs[i][...].astype(jnp.float32)

    def row(t, carry):
        for s in range(2):
            real = scratch[2 * t + s].T
            pieces = []
            for q in range(SEGMENTS):
                lo = q * 2 * W
                pieces += [-real[lo + W : lo + 2 * W], real[lo : lo + W]]
            imag = jnp.concatenate(pieces, axis=0)
            both = jnp.concatenate([real, imag], axis=1).astype(jnp.bfloat16)
            out_ref[t, s * 128 : (s + 1) * 128, :] = both
        return carry

    lax.fori_loop(0, out_ref.shape[0], row, 0, unroll=2)


def weights(offsets, shards):
    count = len(shards)
    step = shards[0].shape[1]
    tiles = 4
    return pl.pallas_call(
        functools.partial(weights_kernel, count=count, step=step),
        out_shape=jax.ShapeDtypeStruct((PAIRS, 256, 256), jnp.bfloat16),
        grid_spec=pltpu.PrefetchScalarGridSpec(
            num_scalar_prefetch=1,
            grid=(tiles,),
            in_specs=[pl.BlockSpec((ROWS // tiles, step, 128), lambda i, o: (i, 0, 0))] * count,
            out_specs=pl.BlockSpec((PAIRS // tiles, 256, 256), lambda i, o: (i, 0, 0)),
            scratch_shapes=[pltpu.VMEM((ROWS // tiles, count * step, 128), jnp.float32)],
        ),
        compiler_params=pltpu.CompilerParams(vmem_limit_bytes=40 << 20),
        name="weights",
    )(offsets, *shards)


def pair_kernel(meta_ref, *refs, count, step, unroll_sum, unroll_lag, pitch):
    x_refs = refs[:count]
    w_ref, t_ref, _, out_ref = refs[count : count + 4]
    xbuf, wide, wbuf, tbuf, cross, lags, stage, sems = refs[count + 4 :]
    height = count * step

    @pl.when(meta_ref[0] == 1)
    def _():
        copies = [
            pltpu.make_async_copy(x_refs[i], xbuf.at[:, i * step : (i + 1) * step, :], sems.at[i])
            for i in range(count)
        ]
        copies.append(pltpu.make_async_copy(w_ref, wbuf, sems.at[count]))
        copies.append(pltpu.make_async_copy(t_ref, tbuf, sems.at[count + 1]))
        for copy in copies:
            copy.start()
        for copy in copies[:count]:
            copy.wait()
        wide[...] = xbuf[...].astype(jnp.float32).reshape(ROWS * height, 128)
        for copy in copies[count:]:
            copy.wait()

        sub = lax.broadcasted_iota(jnp.int32, (8, 128), 0)
        segment = lax.broadcasted_iota(jnp.int32, (8, 128), 1) // (2 * W)
        masks = (segment == sub, segment == sub - SEGMENTS)

        def window_sums(h, carry):
            halves = []
            for u in range(2):
                pair = 2 * h + u
                rows = []
                for a in range(height):
                    halves_of_k = [
                        jnp.where(masks[s], wide[pl.ds((2 * pair + s) * height + a, 8, stride=0), :], 0.0)
                        for s in range(2)
                    ]
                    rows.append(jnp.concatenate(halves_of_k, axis=1))
                left = jnp.concatenate(rows, axis=0).astype(jnp.bfloat16)
                sums = jnp.dot(left, wbuf[pair], preferred_element_type=jnp.float32)
                halves.append(sums.reshape(height, 8, 256))
            both = jnp.concatenate(halves, axis=1).astype(jnp.bfloat16)
            cross[:, pl.ds(pl.multiple_of(h * 16, 16), 16), :] = both
            return carry

        lax.fori_loop(0, PAIRS // 2, window_sums, 0, unroll=unroll_sum)

        def lag_sums(h, carry):
            first, second = cross[2 * h], cross[2 * h + 1]
            real = jnp.concatenate([first[:, :128], second[:, :128]], axis=1)
            imag = jnp.concatenate([first[:, 128:], second[:, 128:]], axis=1)
            right = jnp.concatenate([real, imag], axis=0)
            out = jnp.dot(tbuf[...], right, preferred_element_type=jnp.float32)
            out = out * (1.0 / math.sqrt(W * FB))
            lags[pl.ds(2 * h, LAG_PAD, stride=pitch), :] = out[:, :128]
            lags[pl.ds(2 * h + 1, LAG_PAD, stride=pitch), :] = out[:, 128:]
            return carry

        lax.fori_loop(0, height // 2, lag_sums, 0, unroll=unroll_lag)
        full = lags[...].reshape(LAG_PAD, pitch, 128)[:LAGS, :height].astype(jnp.bfloat16)
        stage[...] = full
        backs = [
            pltpu.make_async_copy(
                stage.at[:, i * step : (i + 1) * step, :],
                out_ref.at[:, pl.ds(pl.multiple_of(meta_ref[1 + i], step), step), :],
                sems.at[i],
            )
            for i in range(count)
        ]
        for back in backs:
            back.start()
        for back in backs:
            back.wait()


def pair_block(meta, shards, right, table, out, unroll_sum=8, unroll_lag=8, pad=8):
    count = len(shards)
    step = shards[0].shape[1]
    height = count * step
    anywhere = pl.BlockSpec(memory_space=pl.ANY)
    return pl.pallas_call(
        functools.partial(pair_kernel, count=count, step=step, unroll_sum=unroll_sum, unroll_lag=unroll_lag, pitch=height+pad),
        out_shape=jax.ShapeDtypeStruct(out.shape, out.dtype),
        grid_spec=pltpu.PrefetchScalarGridSpec(
            num_scalar_prefetch=1,
            grid=(),
            in_specs=[anywhere] * (count + 3),
            out_specs=anywhere,
            scratch_shapes=[
                pltpu.VMEM((ROWS, height, 128), jnp.bfloat16),
                pltpu.VMEM((ROWS * height, 128), jnp.float32),
                pltpu.VMEM((PAIRS, 256, 256), jnp.bfloat16),
                pltpu.VMEM((LAG_PAD, 2 * FB), jnp.bfloat16),
                pltpu.VMEM((height, FB, 256), jnp.bfloat16),
                pltpu.VMEM((LAG_PAD * (height + pad), 128), jnp.float32),
                pltpu.VMEM((LAGS, height, 128), jnp.bfloat16),
                pltpu.SemaphoreType.DMA((count + 2,)),
            ],
        ),
        input_output_aliases={count + 3: 0},
        compiler_params=pltpu.CompilerParams(vmem_limit_bytes=60 << 20),
        cost_estimate=pl.CostEstimate(
            flops=2 * height * FB * 256 * 8 * 32 + 2 * height * 128 * 2 * FB * LAG_PAD,
            bytes_accessed=PAIRS * 256 * 256 * 2 + 2 * height * 128 * LAGS,
            transcendentals=0,
        ),
        name="pair_block",
    )(meta, *shards, right, table, out)


def make_table(band_range):
    order = jnp.arange(FB, dtype=jnp.int32)
    freq_index = (order % SEGMENTS) * ROWS + order // SEGMENTS
    lag_index = jnp.arange(LAG_PAD, dtype=jnp.int32) - LAGS // 2
    turns = jnp.mod((F0 + freq_index)[None, :] * lag_index[:, None], NFFT)
    theta = turns.astype(jnp.float32) * (2.0 * math.pi / NFFT)
    inband = ((freq_index >= band_range[0]) & (freq_index < band_range[1])).astype(jnp.float32)[None, :]
    return jnp.concatenate([inband * jnp.cos(theta), -inband * jnp.sin(theta)], axis=1).astype(jnp.bfloat16)


def gather_rows(parts, plane_axis, row_axis, side_axis):
    rows = lax.axis_size(row_axis)
    sides = lax.axis_size(side_axis)
    row_id = lax.axis_index(row_axis)
    side_id = lax.axis_index(side_axis)
    axes = (row_axis, plane_axis, side_axis)
    gathered = [lax.all_gather(part, plane_axis, axis=0) for part in parts]
    out = []
    for planes in gathered:
        pieces = [lax.dynamic_index_in_dim(planes, row_id ^ t, 0, keepdims=False) for t in range(rows)]
        held = []
        for flip in range(sides):
            for t in range(rows):
                piece = pieces[t]
                if t or flip:
                    pairs = [
                        ((r * rows + p) * sides + x, ((r ^ t) * rows + p) * sides + (x ^ flip))
                        for r in range(rows)
                        for p in range(rows)
                        for x in range(sides)
                        if p >= r ^ t
                    ]
                    piece = lax.ppermute(piece, axes, pairs)
                held.append((piece, row_id ^ t, side_id ^ flip))
        out.append(held)
    return out


def column_weights(shard, plane_axis, row_axis, side_axis):
    rows = lax.axis_size(row_axis)
    row_id = lax.axis_index(row_axis)
    width = shard.shape[1]
    axes = (row_axis,)
    own = [shard]
    for t in range(1, rows):
        low = t & -t
        if t == low:
            own.append(lax.ppermute(shard, axes, [(r, r ^ t) for r in range(rows)]))
        else:
            own.append(lax.ppermute(own[t ^ low], axes, [(r, r ^ low) for r in range(rows)]))
    offsets = jnp.stack([(row_id ^ t) * width for t in range(rows)]).astype(jnp.int32)
    return weights(offsets, own)


def direct_body(spectra, request, table, out):
    rows = lax.axis_size("row")
    sides = lax.axis_size("side")
    width = spectra.shape[2]
    parts = 2
    step = width // parts
    whole, *pieces = whiten(spectra, parts)
    held = gather_rows(pieces, "plane", "row", "side")
    right = column_weights(whole, "plane", "row", "side")
    for g in range(parts):
        for group in GROUPS:
            members = [held[g][i] for i in group]
            places = [(x * rows + r) * width + g * step for _, r, x in members]
            meta = jnp.stack([request, *places]).astype(jnp.int32)
            out = pair_block(meta, [m[0] for m in members], right, table, out)
    return out


GROUPS = ((0, 1, 4, 5), (2, 3, 6, 7))


def gather_body(spectra, request, table, out):
    shard = whiten(spectra, 1)[0]
    width = shard.shape[1]
    rows = lax.axis_size("row")
    sides = lax.axis_size("side")
    column = lax.all_gather(shard, "row", axis=1, tiled=True)
    grouped = lax.all_gather(shard, ("plane", "side"), axis=0).reshape(rows, sides, ROWS, width, 128)
    moved = lax.all_to_all(grouped, "row", split_axis=0, concat_axis=0)
    block = jnp.transpose(moved, (2, 1, 0, 3, 4)).reshape(ROWS, sides * rows * width, 128)
    right = weights(jnp.zeros((1,), jnp.int32), [column])
    group = min(64, block.shape[1])
    for at in range(0, block.shape[1], group):
        meta = jnp.stack([request, jnp.int32(at)])
        out = pair_block(meta, [block[:, at : at + group]], right, table, out)
    return out


def body(spectra, pair_mask, band_range):
    rows = lax.axis_size("row")
    sides = lax.axis_size("side")
    width = spectra.shape[2]
    request = ((pair_mask[0, 0] == 1) & (lax.axis_index("plane") >= lax.axis_index("row"))).astype(jnp.int32)
    table = make_table(band_range)
    out = jnp.zeros((LAGS, sides * rows * width, rows * width), jnp.bfloat16)
    if (rows, sides) == (4, 2) and width % 32 == 0:
        out = direct_body(spectra, request, table, out)
    else:
        out = gather_body(spectra, request, table, out)
    return jnp.transpose(out, (1, 2, 0))


def solution(mesh):
    rows, cols = mesh.devices.shape
    cut = Mesh(mesh.devices.reshape(rows, rows, cols // rows), ("row", "plane", "side"))
    return jax.shard_map(
        body,
        mesh=cut,
        in_specs=(P(None, None, ("plane", "side", "row"), None), P("row", ("plane", "side")), P()),
        out_specs=P("row", ("plane", "side"), None),
        check_vma=False,
    )
```

```python
import functools
import math

import jax
import jax.numpy as jnp
from jax import lax
from jax.experimental import pallas as pl
from jax.experimental.pallas import tpu as pltpu
from jax.sharding import Mesh
from jax.sharding import PartitionSpec as P

W = 16
FB = 512
LAGS = 201
NFFT = 15000
F0 = 60
EPS = 1e-06

SEGMENTS = 4
ROWS = FB // SEGMENTS
PAIRS = ROWS // 2
LAG_PAD = 208


def whiten_kernel(*refs, width, parts):
    x_refs, whole_ref, out_refs, scratch = refs[:SEGMENTS], refs[SEGMENTS], refs[SEGMENTS + 1 : -1], refs[-1]

    def channel(c, carry):
        tiles = [x_ref[pl.ds(c, 2 * W, stride=width), :] for x_ref in x_refs]
        total = sum(v[:W] * v[:W] + v[W:] * v[W:] for v in tiles)
        power = jnp.sum(total, axis=-1, keepdims=True) * (1.0 / FB)
        scale = lax.rsqrt(power + EPS)
        scale = jnp.concatenate([scale, scale], axis=0)
        stacked = jnp.concatenate([v * scale for v in tiles], axis=0)
        scratch[pl.ds(c, ROWS, stride=width), :] = stacked.T
        return carry

    lax.fori_loop(0, width, channel, 0, unroll=2)
    step = width // parts
    full = scratch[...].reshape(ROWS, width, 128).astype(jnp.bfloat16)
    whole_ref[...] = full
    for g, out_ref in enumerate(out_refs):
        out_ref[...] = full[:, g * step : (g + 1) * step, :]


def whiten(spectra, parts):
    width = spectra.shape[2]
    widths = [width] + ([width // parts] * parts if parts > 1 else [])
    lines = 2 * W * width
    flat = spectra.reshape(lines, FB)
    return pl.pallas_call(
        functools.partial(whiten_kernel, width=width, parts=parts),
        out_shape=[jax.ShapeDtypeStruct((ROWS, n, 128), jnp.bfloat16) for n in widths],
        grid=(1,),
        in_specs=[pl.BlockSpec((lines, ROWS), functools.partial(lambda q, i: (0, q), q)) for q in range(SEGMENTS)],
        out_specs=[pl.BlockSpec((ROWS, n, 128), lambda i: (0, 0, 0)) for n in widths],
        scratch_shapes=[pltpu.VMEM((ROWS * width, 128), jnp.float32)],
        compiler_params=pltpu.CompilerParams(vmem_limit_bytes=40 << 20),
        name="whiten",
    )(*[flat] * SEGMENTS)


def weights_kernel(offset_ref, *refs, count, step):
    in_refs, out_ref, scratch = refs[:count], refs[count], refs[count + 1]
    for i in range(count):
        at = pl.multiple_of(offset_ref[i], step)
        scratch[:, pl.ds(at, step), :] = in_refs[i][...].astype(jnp.float32)

    def row(t, carry):
        for s in range(2):
            real = scratch[2 * t + s].T
            pieces = []
            for q in range(SEGMENTS):
                lo = q * 2 * W
                pieces += [-real[lo + W : lo + 2 * W], real[lo : lo + W]]
            imag = jnp.concatenate(pieces, axis=0)
            both = jnp.concatenate([real, imag], axis=1).astype(jnp.bfloat16)
            out_ref[t, s * 128 : (s + 1) * 128, :] = both
        return carry

    lax.fori_loop(0, out_ref.shape[0], row, 0, unroll=2)


def weights(offsets, shards):
    count = len(shards)
    step = shards[0].shape[1]
    tiles = 4
    return pl.pallas_call(
        functools.partial(weights_kernel, count=count, step=step),
        out_shape=jax.ShapeDtypeStruct((PAIRS, 256, 256), jnp.bfloat16),
        grid_spec=pltpu.PrefetchScalarGridSpec(
            num_scalar_prefetch=1,
            grid=(tiles,),
            in_specs=[pl.BlockSpec((ROWS // tiles, step, 128), lambda i, o: (i, 0, 0))] * count,
            out_specs=pl.BlockSpec((PAIRS // tiles, 256, 256), lambda i, o: (i, 0, 0)),
            scratch_shapes=[pltpu.VMEM((ROWS // tiles, count * step, 128), jnp.float32)],
        ),
        compiler_params=pltpu.CompilerParams(vmem_limit_bytes=40 << 20),
        name="weights",
    )(offsets, *shards)


def pair_kernel(meta_ref, *refs, count, height, unroll_sum, unroll_lag, pitch):
    x_refs = refs[:count]
    w_ref, t_ref, _, out_ref = refs[count : count + 4]
    xbuf, wide, wbuf, tbuf, cross, lags, stage, sems = refs[count + 4 :]

    @pl.when(meta_ref[0] >= 0)
    def _():
        for i in range(count):

            @pl.when(meta_ref[0] == i)
            def _(i=i):
                pltpu.make_async_copy(x_refs[i], xbuf, sems.at[0]).start()

        others = [
            pltpu.make_async_copy(w_ref, wbuf, sems.at[1]),
            pltpu.make_async_copy(t_ref, tbuf, sems.at[2]),
        ]
        for copy in others:
            copy.start()
        pltpu.make_async_copy(x_refs[0], xbuf, sems.at[0]).wait()
        wide[...] = xbuf[...].astype(jnp.float32).reshape(ROWS * height, 128)
        for copy in others:
            copy.wait()

        sub = lax.broadcasted_iota(jnp.int32, (8, 128), 0)
        segment = lax.broadcasted_iota(jnp.int32, (8, 128), 1) // (2 * W)
        masks = (segment == sub, segment == sub - SEGMENTS)

        def window_sums(h, carry):
            halves = []
            for u in range(2):
                pair = 2 * h + u
                rows = []
                for a in range(height):
                    halves_of_k = [
                        jnp.where(masks[s], wide[pl.ds((2 * pair + s) * height + a, 8, stride=0), :], 0.0)
                        for s in range(2)
                    ]
                    rows.append(jnp.concatenate(halves_of_k, axis=1))
                left = jnp.concatenate(rows, axis=0).astype(jnp.bfloat16)
                sums = jnp.dot(left, wbuf[pair], preferred_element_type=jnp.float32)
                halves.append(sums.reshape(height, 8, 256))
            both = jnp.concatenate(halves, axis=1).astype(jnp.bfloat16)
            cross[:, pl.ds(pl.multiple_of(h * 16, 16), 16), :] = both
            return carry

        lax.fori_loop(0, PAIRS // 2, window_sums, 0, unroll=unroll_sum)

        def lag_sums(h, carry):
            first, second = cross[2 * h], cross[2 * h + 1]
            real = jnp.concatenate([first[:, :128], second[:, :128]], axis=1)
            imag = jnp.concatenate([first[:, 128:], second[:, 128:]], axis=1)
            right = jnp.concatenate([real, imag], axis=0)
            out = jnp.dot(tbuf[...], right, preferred_element_type=jnp.float32)
            out = out * (1.0 / math.sqrt(W * FB))
            lags[pl.ds(2 * h, LAG_PAD, stride=pitch), :] = out[:, :128]
            lags[pl.ds(2 * h + 1, LAG_PAD, stride=pitch), :] = out[:, 128:]
            return carry

        lax.fori_loop(0, height // 2, lag_sums, 0, unroll=unroll_lag)
        stage[...] = lags[...].reshape(LAG_PAD, pitch, 128)[:LAGS, :height].astype(jnp.bfloat16)
        at = pl.multiple_of(meta_ref[1], height)
        back = pltpu.make_async_copy(stage, out_ref.at[:, pl.ds(at, height), :], sems.at[0])
        back.start()
        back.wait()


def pair_block(choice, place, shards, right, table, out, unroll_sum=8, unroll_lag=8, pad=8):
    count = len(shards)
    height = shards[0].shape[1]
    meta = jnp.stack([choice, place]).astype(jnp.int32)
    anywhere = pl.BlockSpec(memory_space=pl.ANY)
    return pl.pallas_call(
        functools.partial(
            pair_kernel,
            count=count,
            height=height,
            unroll_sum=unroll_sum,
            unroll_lag=unroll_lag,
            pitch=height + pad,
        ),
        out_shape=jax.ShapeDtypeStruct(out.shape, out.dtype),
        grid_spec=pltpu.PrefetchScalarGridSpec(
            num_scalar_prefetch=1,
            grid=(),
            in_specs=[anywhere] * (count + 3),
            out_specs=anywhere,
            scratch_shapes=[
                pltpu.VMEM((ROWS, height, 128), jnp.bfloat16),
                pltpu.VMEM((ROWS * height, 128), jnp.float32),
                pltpu.VMEM((PAIRS, 256, 256), jnp.bfloat16),
                pltpu.VMEM((LAG_PAD, 2 * FB), jnp.bfloat16),
                pltpu.VMEM((height, FB, 256), jnp.bfloat16),
                pltpu.VMEM((LAG_PAD * (height + pad), 128), jnp.float32),
                pltpu.VMEM((LAGS, height, 128), jnp.bfloat16),
                pltpu.SemaphoreType.DMA((3,)),
            ],
        ),
        input_output_aliases={count + 3: 0},
        compiler_params=pltpu.CompilerParams(vmem_limit_bytes=60 << 20),
        cost_estimate=pl.CostEstimate(
            flops=2 * height * FB * 256 * 8 * 32 + 2 * height * 128 * 2 * FB * LAG_PAD,
            bytes_accessed=PAIRS * 256 * 256 * 2 + 2 * height * 128 * LAGS,
            transcendentals=0,
        ),
        name="pair_block",
    )(meta, *shards, right, table, out)


def make_table(band_range):
    order = jnp.arange(FB, dtype=jnp.int32)
    freq_index = (order % SEGMENTS) * ROWS + order // SEGMENTS
    lag_index = jnp.arange(LAG_PAD, dtype=jnp.int32) - LAGS // 2
    turns = jnp.mod((F0 + freq_index)[None, :] * lag_index[:, None], NFFT)
    theta = turns.astype(jnp.float32) * (2.0 * math.pi / NFFT)
    inband = ((freq_index >= band_range[0]) & (freq_index < band_range[1])).astype(jnp.float32)[None, :]
    return jnp.concatenate([inband * jnp.cos(theta), -inband * jnp.sin(theta)], axis=1).astype(jnp.bfloat16)


def relay_body(spectra, request, table, out):
    rows, sides = lax.axis_size("row"), lax.axis_size("side")
    axes = ("row", "plane", "side")
    row_id, plane, side = (lax.axis_index(name) for name in axes)
    width = spectra.shape[2]
    core, chip = row_id % 2, row_id // 2
    depth = plane - row_id
    devices = [(r, p, x) for r in range(rows) for p in range(rows) for x in range(sides)]

    def send(value, pairs):
        number = [tuple((r * rows + p) * sides + x for r, p, x in pair) for pair in pairs]
        return lax.ppermute(value, axes, number)

    def join(mine, sibling):
        first = jnp.where(core == 0, mine, sibling)
        second = jnp.where(core == 0, sibling, mine)
        return jnp.concatenate([first, second], axis=1)

    core_flip = [((r, p, x), (r ^ 1, p, x)) for r, p, x in devices]
    chip_flip = [((r, p, x), (r ^ 2, p, x)) for r, p, x in devices]

    shard = whiten(spectra, 1)[0]
    joined = join(shard, send(shard, core_flip))
    across = send(shard, chip_flip)
    joined_across = join(across, send(across, core_flip))
    offsets = jnp.stack([2 * chip * width, 2 * (1 - chip) * width]).astype(jnp.int32)
    right = weights(offsets, [joined, joined_across])

    climbed = [joined]
    for d in range(1, rows):
        hop = [((r, p, x), (r, p + 1, x)) for r, p, x in devices if p + 1 < rows and p - d + 1 >= 0 and (p - d + 1 - r) % 2 == 0]
        climbed.append(send(climbed[-1], hop))

    def to_row(d, flip_side, flip_chip):
        takers = [(r, p, x) for r, p, x in devices if p - r == d]
        return send(climbed[d], [((r ^ 2 * flip_chip, p, x ^ flip_side), (r, p, x)) for r, p, x in takers])

    held = []
    for d in range(rows):
        held.append(
            [
                climbed[d],
                to_row(d, 1, 0),
                joined_across if d == 0 else to_row(d, 0, 1),
                to_row(d, 1, 1),
            ]
        )
    for depths in ((0, 1), (2, 3)):
        wanted = (request == 1) & (depth >= depths[0]) & (depth <= depths[1])
        choice = jnp.where(wanted, depth - depths[0], -1)
        for q, (flip_side, flip_chip) in enumerate(((0, 0), (1, 0), (0, 1), (1, 1))):
            place = ((side ^ flip_side) * rows + 2 * (chip ^ flip_chip)) * width
            out = pair_block(choice, place, [held[d][q] for d in depths], right, table, out)
    return out


def gather_body(spectra, request, table, out):
    shard = whiten(spectra, 1)[0]
    width = shard.shape[1]
    rows = lax.axis_size("row")
    sides = lax.axis_size("side")
    column = lax.all_gather(shard, "row", axis=1, tiled=True)
    grouped = lax.all_gather(shard, ("plane", "side"), axis=0).reshape(rows, sides, ROWS, width, 128)
    moved = lax.all_to_all(grouped, "row", split_axis=0, concat_axis=0)
    block = jnp.transpose(moved, (2, 1, 0, 3, 4)).reshape(ROWS, sides * rows * width, 128)
    right = weights(jnp.zeros((1,), jnp.int32), [column])
    group = min(64, block.shape[1])
    for at in range(0, block.shape[1], group):
        out = pair_block(request - 1, jnp.int32(at), [block[:, at : at + group]], right, table, out)
    return out


def body(spectra, pair_mask, band_range):
    rows = lax.axis_size("row")
    sides = lax.axis_size("side")
    width = spectra.shape[2]
    request = ((pair_mask[0, 0] == 1) & (lax.axis_index("plane") >= lax.axis_index("row"))).astype(jnp.int32)
    table = make_table(band_range)
    out = jnp.zeros((LAGS, sides * rows * width, rows * width), jnp.bfloat16)
    if (rows, sides) == (4, 2) and width % 32 == 0:
        out = relay_body(spectra, request, table, out)
    else:
        out = gather_body(spectra, request, table, out)
    return jnp.transpose(out, (1, 2, 0))


def solution(mesh):
    rows, cols = mesh.devices.shape
    cut = Mesh(mesh.devices.reshape(rows, rows, cols // rows), ("row", "plane", "side"))
    return jax.shard_map(
        body,
        mesh=cut,
        in_specs=(P(None, None, ("plane", "side", "row"), None), P("row", ("plane", "side")), P()),
        out_specs=P("row", ("plane", "side"), None),
        check_vma=False,
    )
```

```python
import functools
import math

import jax
import jax.numpy as jnp
from jax import lax
from jax.experimental import pallas as pl
from jax.experimental.pallas import tpu as pltpu
from jax.sharding import Mesh
from jax.sharding import PartitionSpec as P

W = 16
FB = 512
LAGS = 201
NFFT = 15000
F0 = 60
EPS = 1e-06

SEGMENTS = 4
ROWS = FB // SEGMENTS
PAIRS = ROWS // 2
LAG_PAD = 208


def whiten_kernel(*refs, width, parts):
    x_refs, whole_ref, out_refs, scratch = refs[:SEGMENTS], refs[SEGMENTS], refs[SEGMENTS + 1 : -1], refs[-1]

    def channel(c, carry):
        tiles = [x_ref[pl.ds(c, 2 * W, stride=width), :] for x_ref in x_refs]
        total = sum(v[:W] * v[:W] + v[W:] * v[W:] for v in tiles)
        power = jnp.sum(total, axis=-1, keepdims=True) * (1.0 / FB)
        scale = lax.rsqrt(power + EPS)
        scale = jnp.concatenate([scale, scale], axis=0)
        stacked = jnp.concatenate([v * scale for v in tiles], axis=0)
        scratch[pl.ds(c, ROWS, stride=width), :] = stacked.T
        return carry

    lax.fori_loop(0, width, channel, 0, unroll=2)
    step = width // parts
    full = scratch[...].reshape(ROWS, width, 128).astype(jnp.bfloat16)
    whole_ref[...] = full
    for g, out_ref in enumerate(out_refs):
        out_ref[...] = full[:, g * step : (g + 1) * step, :]


def whiten(spectra, parts):
    width = spectra.shape[2]
    widths = [width] + ([width // parts] * parts if parts > 1 else [])
    lines = 2 * W * width
    flat = spectra.reshape(lines, FB)
    return pl.pallas_call(
        functools.partial(whiten_kernel, width=width, parts=parts),
        out_shape=[jax.ShapeDtypeStruct((ROWS, n, 128), jnp.bfloat16) for n in widths],
        grid=(1,),
        in_specs=[pl.BlockSpec((lines, ROWS), functools.partial(lambda q, i: (0, q), q)) for q in range(SEGMENTS)],
        out_specs=[pl.BlockSpec((ROWS, n, 128), lambda i: (0, 0, 0)) for n in widths],
        scratch_shapes=[pltpu.VMEM((ROWS * width, 128), jnp.float32)],
        compiler_params=pltpu.CompilerParams(vmem_limit_bytes=40 << 20),
        name="whiten",
    )(*[flat] * SEGMENTS)


def weights_kernel(offset_ref, *refs, count, step):
    in_refs, out_ref, clear_ref, scratch = refs[:count], refs[count], refs[count + 1], refs[count + 2]
    clear_ref[...] = jnp.zeros_like(clear_ref)
    for i in range(count):
        at = pl.multiple_of(offset_ref[i], step)
        scratch[:, pl.ds(at, step), :] = in_refs[i][...].astype(jnp.float32)

    def row(t, carry):
        for s in range(2):
            real = scratch[2 * t + s].T
            pieces = []
            for q in range(SEGMENTS):
                lo = q * 2 * W
                pieces += [-real[lo + W : lo + 2 * W], real[lo : lo + W]]
            imag = jnp.concatenate(pieces, axis=0)
            both = jnp.concatenate([real, imag], axis=1).astype(jnp.bfloat16)
            out_ref[t, s * 128 : (s + 1) * 128, :] = both
        return carry

    lax.fori_loop(0, out_ref.shape[0], row, 0, unroll=2)


def weights(offsets, shards, height):
    count = len(shards)
    step = shards[0].shape[1]
    tiles = 4
    return pl.pallas_call(
        functools.partial(weights_kernel, count=count, step=step),
        out_shape=[
            jax.ShapeDtypeStruct((PAIRS, 256, 256), jnp.bfloat16),
            jax.ShapeDtypeStruct((LAGS, height, count * step), jnp.bfloat16),
        ],
        grid_spec=pltpu.PrefetchScalarGridSpec(
            num_scalar_prefetch=1,
            grid=(tiles,),
            in_specs=[pl.BlockSpec((ROWS // tiles, step, 128), lambda i, o: (i, 0, 0))] * count,
            out_specs=[
                pl.BlockSpec((PAIRS // tiles, 256, 256), lambda i, o: (i, 0, 0)),
                pl.BlockSpec((LAGS, height // tiles, count * step), lambda i, o: (0, i, 0)),
            ],
            scratch_shapes=[pltpu.VMEM((ROWS // tiles, count * step, 128), jnp.float32)],
        ),
        compiler_params=pltpu.CompilerParams(vmem_limit_bytes=40 << 20),
        name="weights",
    )(offsets, *shards)


def pair_kernel(meta_ref, *refs, count, height, unroll_sum, unroll_lag, pitch):
    x_refs = refs[:count]
    w_ref, t_ref, _, out_ref = refs[count : count + 4]
    xbuf, wide, wbuf, tbuf, cross, lags, stage, sems = refs[count + 4 :]

    @pl.when(meta_ref[0] >= 0)
    def _():
        for i in range(count):

            @pl.when(meta_ref[0] == i)
            def _(i=i):
                pltpu.make_async_copy(x_refs[i], xbuf, sems.at[0]).start()

        others = [
            pltpu.make_async_copy(w_ref, wbuf, sems.at[1]),
            pltpu.make_async_copy(t_ref, tbuf, sems.at[2]),
        ]
        for copy in others:
            copy.start()
        pltpu.make_async_copy(x_refs[0], xbuf, sems.at[0]).wait()
        wide[...] = xbuf[...].astype(jnp.float32).reshape(ROWS * height, 128)
        for copy in others:
            copy.wait()

        sub = lax.broadcasted_iota(jnp.int32, (8, 128), 0)
        segment = lax.broadcasted_iota(jnp.int32, (8, 128), 1) // (2 * W)
        masks = (segment == sub, segment == sub - SEGMENTS)

        def window_sums(h, carry):
            halves = []
            for u in range(2):
                pair = 2 * h + u
                rows = []
                for a in range(height):
                    halves_of_k = [
                        jnp.where(masks[s], wide[pl.ds((2 * pair + s) * height + a, 8, stride=0), :], 0.0)
                        for s in range(2)
                    ]
                    rows.append(jnp.concatenate(halves_of_k, axis=1))
                left = jnp.concatenate(rows, axis=0).astype(jnp.bfloat16)
                sums = jnp.dot(left, wbuf[pair], preferred_element_type=jnp.float32)
                halves.append(sums.reshape(height, 8, 256))
            both = jnp.concatenate(halves, axis=1).astype(jnp.bfloat16)
            cross[:, pl.ds(pl.multiple_of(h * 16, 16), 16), :] = both
            return carry

        lax.fori_loop(0, PAIRS // 2, window_sums, 0, unroll=unroll_sum)

        def lag_sums(h, carry):
            first, second = cross[2 * h], cross[2 * h + 1]
            real = jnp.concatenate([first[:, :128], second[:, :128]], axis=1)
            imag = jnp.concatenate([first[:, 128:], second[:, 128:]], axis=1)
            right = jnp.concatenate([real, imag], axis=0)
            out = jnp.dot(tbuf[...], right, preferred_element_type=jnp.float32)
            out = out * (1.0 / math.sqrt(W * FB))
            lags[pl.ds(2 * h, LAG_PAD, stride=pitch), :] = out[:, :128]
            lags[pl.ds(2 * h + 1, LAG_PAD, stride=pitch), :] = out[:, 128:]
            return carry

        lax.fori_loop(0, height // 2, lag_sums, 0, unroll=unroll_lag)
        stage[...] = lags[...].reshape(LAG_PAD, pitch, 128)[:LAGS, :height].astype(jnp.bfloat16)
        at = pl.multiple_of(meta_ref[1], height)
        back = pltpu.make_async_copy(stage, out_ref.at[:, pl.ds(at, height), :], sems.at[0])
        back.start()
        back.wait()


def pair_block(choice, place, shards, right, table, out, unroll_sum=8, unroll_lag=8, pad=8):
    count = len(shards)
    height = shards[0].shape[1]
    meta = jnp.stack([choice, place]).astype(jnp.int32)
    anywhere = pl.BlockSpec(memory_space=pl.ANY)
    return pl.pallas_call(
        functools.partial(
            pair_kernel,
            count=count,
            height=height,
            unroll_sum=unroll_sum,
            unroll_lag=unroll_lag,
            pitch=height + pad,
        ),
        out_shape=jax.ShapeDtypeStruct(out.shape, out.dtype),
        grid_spec=pltpu.PrefetchScalarGridSpec(
            num_scalar_prefetch=1,
            grid=(),
            in_specs=[anywhere] * (count + 3),
            out_specs=anywhere,
            scratch_shapes=[
                pltpu.VMEM((ROWS, height, 128), jnp.bfloat16),
                pltpu.VMEM((ROWS * height, 128), jnp.float32),
                pltpu.VMEM((PAIRS, 256, 256), jnp.bfloat16),
                pltpu.VMEM((LAG_PAD, 2 * FB), jnp.bfloat16),
                pltpu.VMEM((height, FB, 256), jnp.bfloat16),
                pltpu.VMEM((LAG_PAD * (height + pad), 128), jnp.float32),
                pltpu.VMEM((LAGS, height, 128), jnp.bfloat16),
                pltpu.SemaphoreType.DMA((3,)),
            ],
        ),
        input_output_aliases={count + 3: 0},
        compiler_params=pltpu.CompilerParams(vmem_limit_bytes=60 << 20),
        cost_estimate=pl.CostEstimate(
            flops=2 * height * FB * 256 * 8 * 32 + 2 * height * 128 * 2 * FB * LAG_PAD,
            bytes_accessed=PAIRS * 256 * 256 * 2 + 2 * height * 128 * LAGS,
            transcendentals=0,
        ),
        name="pair_block",
    )(meta, *shards, right, table, out)


def make_table(band_range):
    order = jnp.arange(FB, dtype=jnp.int32)
    freq_index = (order % SEGMENTS) * ROWS + order // SEGMENTS
    lag_index = jnp.arange(LAG_PAD, dtype=jnp.int32) - LAGS // 2
    turns = jnp.mod((F0 + freq_index)[None, :] * lag_index[:, None], NFFT)
    theta = turns.astype(jnp.float32) * (2.0 * math.pi / NFFT)
    inband = ((freq_index >= band_range[0]) & (freq_index < band_range[1])).astype(jnp.float32)[None, :]
    return jnp.concatenate([inband * jnp.cos(theta), -inband * jnp.sin(theta)], axis=1).astype(jnp.bfloat16)


def relay_body(spectra, request, table):
    rows, sides = lax.axis_size("row"), lax.axis_size("side")
    axes = ("row", "plane", "side")
    row_id, plane, side = (lax.axis_index(name) for name in axes)
    width = spectra.shape[2]
    core, chip = row_id % 2, row_id // 2
    depth = plane - row_id
    devices = [(r, p, x) for r in range(rows) for p in range(rows) for x in range(sides)]

    def send(value, pairs):
        number = [tuple((r * rows + p) * sides + x for r, p, x in pair) for pair in pairs]
        return lax.ppermute(value, axes, number)

    def join(mine, sibling):
        first = jnp.where(core == 0, mine, sibling)
        second = jnp.where(core == 0, sibling, mine)
        return jnp.concatenate([first, second], axis=1)

    core_flip = [((r, p, x), (r ^ 1, p, x)) for r, p, x in devices]
    chip_flip = [((r, p, x), (r ^ 2, p, x)) for r, p, x in devices]

    shard = whiten(spectra, 1)[0]
    joined = join(shard, send(shard, core_flip))
    across = send(shard, chip_flip)
    joined_across = join(across, send(across, core_flip))
    offsets = jnp.stack([2 * chip * width, 2 * (1 - chip) * width]).astype(jnp.int32)
    right, out = weights(offsets, [joined, joined_across], sides * rows * width)

    def climb(value, d):
        return send(
            value,
            [
                ((r, p, x), (r, p + 1, x))
                for r, p, x in devices
                if p + 1 < rows and p - d + 1 >= 0 and (p - d + 1 - r) % 2 == 0
            ],
        )

    def to_row(value, depths, flip_side, flip_chip):
        takers = [(r, p, x) for r, p, x in devices if p - r in depths]
        return send(value, [((r ^ 2 * flip_chip, p, x ^ flip_side), (r, p, x)) for r, p, x in takers])

    after = lax.optimization_barrier
    once = climb(joined, 1)
    twice = climb(once, 2)
    side_early = to_row(jnp.where(depth == 0, joined, once), (0, 1), 1, 0)
    chip_one = to_row(once, (1,), 0, 1)
    both_early = to_row(jnp.where(plane == (row_id ^ 2), joined, once), (0, 1), 1, 1)
    twice, side_early, right, table = after((twice, side_early, right, table))
    thrice = climb(twice, 3)
    side_two = to_row(twice, (2,), 1, 0)
    chip_two = to_row(twice, (2,), 0, 1)
    thrice, chip_one, both_early, side_two, chip_two, twice = after(
        (thrice, chip_one, both_early, side_two, chip_two, twice)
    )
    chip_three = to_row(thrice, (3,), 0, 1)
    side_three = to_row(thrice, (3,), 1, 0)
    both_two = to_row(twice, (2,), 1, 1)

    wanted = request == 1
    by_depth = jnp.where(wanted, depth, -1)
    by_late = jnp.where(wanted, jnp.maximum(depth - 1, 0), -1)

    def place(flip_side, flip_chip):
        return ((side ^ flip_side) * rows + 2 * (chip ^ flip_chip)) * width

    out = pair_block(by_depth, place(0, 0), [joined, once, twice, thrice], right, table, out)
    chip_three, out = after((chip_three, out))
    both_three = to_row(chip_three, (3,), 1, 0)
    out = pair_block(by_late, place(1, 0), [side_early, side_two, side_three], right, table, out)
    out = pair_block(by_depth, place(0, 1), [joined_across, chip_one, chip_two, chip_three], right, table, out)
    return pair_block(by_late, place(1, 1), [both_early, both_two, both_three], right, table, out)


def gather_body(spectra, request, table):
    shard = whiten(spectra, 1)[0]
    width = shard.shape[1]
    rows = lax.axis_size("row")
    sides = lax.axis_size("side")
    column = lax.all_gather(shard, "row", axis=1, tiled=True)
    grouped = lax.all_gather(shard, ("plane", "side"), axis=0).reshape(rows, sides, ROWS, width, 128)
    moved = lax.all_to_all(grouped, "row", split_axis=0, concat_axis=0)
    block = jnp.transpose(moved, (2, 1, 0, 3, 4)).reshape(ROWS, sides * rows * width, 128)
    right, out = weights(jnp.zeros((1,), jnp.int32), [column], block.shape[1])
    group = min(64, block.shape[1])
    for at in range(0, block.shape[1], group):
        out = pair_block(request - 1, jnp.int32(at), [block[:, at : at + group]], right, table, out)
    return out


def body(spectra, pair_mask, band_range):
    rows = lax.axis_size("row")
    sides = lax.axis_size("side")
    width = spectra.shape[2]
    request = ((pair_mask[0, 0] == 1) & (lax.axis_index("plane") >= lax.axis_index("row"))).astype(jnp.int32)
    table = make_table(band_range)
    if (rows, sides) == (4, 2) and width % 32 == 0:
        out = relay_body(spectra, request, table)
    else:
        out = gather_body(spectra, request, table)
    return jnp.transpose(out, (1, 2, 0))


def solution(mesh):
    rows, cols = mesh.devices.shape
    cut = Mesh(mesh.devices.reshape(rows, rows, cols // rows), ("row", "plane", "side"))
    return jax.shard_map(
        body,
        mesh=cut,
        in_specs=(P(None, None, ("plane", "side", "row"), None), P("row", ("plane", "side")), P()),
        out_specs=P("row", ("plane", "side"), None),
        check_vma=False,
    )
```

```python
import functools
import math

import jax
import jax.numpy as jnp
from jax import lax
from jax.experimental import pallas as pl
from jax.experimental.pallas import tpu as pltpu
from jax.sharding import Mesh
from jax.sharding import PartitionSpec as P

W = 16
FB = 512
LAGS = 201
NFFT = 15000
F0 = 60
EPS = 1e-06

SEGMENTS = 4
ROWS = FB // SEGMENTS
PAIRS = ROWS // 2
LAG_PAD = 208


def whiten_kernel(*refs, width, parts):
    x_refs, whole_ref, out_refs, scratch = refs[:SEGMENTS], refs[SEGMENTS], refs[SEGMENTS + 1 : -1], refs[-1]

    def channel(c, carry):
        tiles = [x_ref[pl.ds(c, 2 * W, stride=width), :] for x_ref in x_refs]
        total = sum(v[:W] * v[:W] + v[W:] * v[W:] for v in tiles)
        power = jnp.sum(total, axis=-1, keepdims=True) * (1.0 / FB)
        scale = lax.rsqrt(power + EPS)
        scale = jnp.concatenate([scale, scale], axis=0)
        stacked = jnp.concatenate([v * scale for v in tiles], axis=0)
        scratch[pl.ds(c, ROWS, stride=width), :] = stacked.T
        return carry

    lax.fori_loop(0, width, channel, 0, unroll=2)
    step = width // parts
    full = scratch[...].reshape(ROWS, width, 128).astype(jnp.bfloat16)
    whole_ref[...] = full
    for g, out_ref in enumerate(out_refs):
        out_ref[...] = full[:, g * step : (g + 1) * step, :]


def whiten(spectra, parts):
    width = spectra.shape[2]
    widths = [width] + ([width // parts] * parts if parts > 1 else [])
    lines = 2 * W * width
    flat = spectra.reshape(lines, FB)
    return pl.pallas_call(
        functools.partial(whiten_kernel, width=width, parts=parts),
        out_shape=[jax.ShapeDtypeStruct((ROWS, n, 128), jnp.bfloat16) for n in widths],
        grid=(1,),
        in_specs=[pl.BlockSpec((lines, ROWS), functools.partial(lambda q, i: (0, q), q)) for q in range(SEGMENTS)],
        out_specs=[pl.BlockSpec((ROWS, n, 128), lambda i: (0, 0, 0)) for n in widths],
        scratch_shapes=[pltpu.VMEM((ROWS * width, 128), jnp.float32)],
        compiler_params=pltpu.CompilerParams(vmem_limit_bytes=40 << 20),
        name="whiten",
    )(*[flat] * SEGMENTS)


def weights_kernel(offset_ref, *refs, count, step):
    in_refs, out_ref, clear_ref, scratch = refs[:count], refs[count], refs[count + 1], refs[count + 2]
    clear_ref[...] = jnp.zeros_like(clear_ref)
    for i in range(count):
        at = pl.multiple_of(offset_ref[i], step)
        scratch[:, pl.ds(at, step), :] = in_refs[i][...].astype(jnp.float32)

    def row(t, carry):
        for s in range(2):
            real = scratch[2 * t + s].T
            pieces = []
            for q in range(SEGMENTS):
                lo = q * 2 * W
                pieces += [-real[lo + W : lo + 2 * W], real[lo : lo + W]]
            imag = jnp.concatenate(pieces, axis=0)
            both = jnp.concatenate([real, imag], axis=1).astype(jnp.bfloat16)
            out_ref[t, s * 128 : (s + 1) * 128, :] = both
        return carry

    lax.fori_loop(0, out_ref.shape[0], row, 0, unroll=2)


def weights(offsets, shards, height):
    count = len(shards)
    step = shards[0].shape[1]
    tiles = 4
    return pl.pallas_call(
        functools.partial(weights_kernel, count=count, step=step),
        out_shape=[
            jax.ShapeDtypeStruct((PAIRS, 256, 256), jnp.bfloat16),
            jax.ShapeDtypeStruct((LAGS, height, count * step), jnp.bfloat16),
        ],
        grid_spec=pltpu.PrefetchScalarGridSpec(
            num_scalar_prefetch=1,
            grid=(tiles,),
            in_specs=[pl.BlockSpec((ROWS // tiles, step, 128), lambda i, o: (i, 0, 0))] * count,
            out_specs=[
                pl.BlockSpec((PAIRS // tiles, 256, 256), lambda i, o: (i, 0, 0)),
                pl.BlockSpec((LAGS, height // tiles, count * step), lambda i, o: (0, i, 0)),
            ],
            scratch_shapes=[pltpu.VMEM((ROWS // tiles, count * step, 128), jnp.float32)],
        ),
        compiler_params=pltpu.CompilerParams(vmem_limit_bytes=40 << 20),
        name="weights",
    )(offsets, *shards)


def pair_kernel(meta_ref, *refs, count, height, unroll_sum, unroll_lag, pitch):
    x_refs = refs[:count]
    w_ref, t_ref, _, out_ref = refs[count : count + 4]
    xbuf, wide, wbuf, tbuf, cross, lags, stage, sems = refs[count + 4 :]

    @pl.when(meta_ref[0] >= 0)
    def _():
        for i in range(count):

            @pl.when(meta_ref[0] == i)
            def _(i=i):
                pltpu.make_async_copy(x_refs[i], xbuf, sems.at[0]).start()

        others = [
            pltpu.make_async_copy(w_ref, wbuf, sems.at[1]),
            pltpu.make_async_copy(t_ref, tbuf, sems.at[2]),
        ]
        for copy in others:
            copy.start()
        pltpu.make_async_copy(x_refs[0], xbuf, sems.at[0]).wait()
        wide[...] = xbuf[...].astype(jnp.float32).reshape(ROWS * height, 128)
        for copy in others:
            copy.wait()

        sub = lax.broadcasted_iota(jnp.int32, (8, 128), 0)
        segment = lax.broadcasted_iota(jnp.int32, (8, 128), 1) // (2 * W)
        masks = (segment == sub, segment == sub - SEGMENTS)

        def window_sums(h, carry):
            halves = []
            for u in range(2):
                pair = 2 * h + u
                rows = []
                for a in range(height):
                    halves_of_k = [
                        jnp.where(masks[s], wide[pl.ds((2 * pair + s) * height + a, 8, stride=0), :], 0.0)
                        for s in range(2)
                    ]
                    rows.append(jnp.concatenate(halves_of_k, axis=1))
                left = jnp.concatenate(rows, axis=0).astype(jnp.bfloat16)
                sums = jnp.dot(left, wbuf[pair], preferred_element_type=jnp.float32)
                halves.append(sums.reshape(height, 8, 256))
            both = jnp.concatenate(halves, axis=1).astype(jnp.bfloat16)
            cross[:, pl.ds(pl.multiple_of(h * 16, 16), 16), :] = both
            return carry

        lax.fori_loop(0, PAIRS // 2, window_sums, 0, unroll=unroll_sum)

        def lag_sums(h, carry):
            first, second = cross[2 * h], cross[2 * h + 1]
            real = jnp.concatenate([first[:, :128], second[:, :128]], axis=1)
            imag = jnp.concatenate([first[:, 128:], second[:, 128:]], axis=1)
            right = jnp.concatenate([real, imag], axis=0)
            out = jnp.dot(tbuf[...], right, preferred_element_type=jnp.float32)
            out = out * (1.0 / math.sqrt(W * FB))
            lags[pl.ds(2 * h, LAG_PAD, stride=pitch), :] = out[:, :128]
            lags[pl.ds(2 * h + 1, LAG_PAD, stride=pitch), :] = out[:, 128:]
            return carry

        lax.fori_loop(0, height // 2, lag_sums, 0, unroll=unroll_lag)
        stage[...] = lags[...].reshape(LAG_PAD, pitch, 128)[:LAGS, :height].astype(jnp.bfloat16)
        at = pl.multiple_of(meta_ref[1], height)
        back = pltpu.make_async_copy(stage, out_ref.at[:, pl.ds(at, height), :], sems.at[0])
        back.start()
        back.wait()


def pair_block(choice, place, shards, right, table, out, unroll_sum=8, unroll_lag=8, pad=8):
    count = len(shards)
    height = shards[0].shape[1]
    meta = jnp.stack([choice, place]).astype(jnp.int32)
    anywhere = pl.BlockSpec(memory_space=pl.ANY)
    return pl.pallas_call(
        functools.partial(
            pair_kernel,
            count=count,
            height=height,
            unroll_sum=unroll_sum,
            unroll_lag=unroll_lag,
            pitch=height + pad,
        ),
        out_shape=jax.ShapeDtypeStruct(out.shape, out.dtype),
        grid_spec=pltpu.PrefetchScalarGridSpec(
            num_scalar_prefetch=1,
            grid=(),
            in_specs=[anywhere] * (count + 3),
            out_specs=anywhere,
            scratch_shapes=[
                pltpu.VMEM((ROWS, height, 128), jnp.bfloat16),
                pltpu.VMEM((ROWS * height, 128), jnp.float32),
                pltpu.VMEM((PAIRS, 256, 256), jnp.bfloat16),
                pltpu.VMEM((LAG_PAD, 2 * FB), jnp.bfloat16),
                pltpu.VMEM((height, FB, 256), jnp.bfloat16),
                pltpu.VMEM((LAG_PAD * (height + pad), 128), jnp.float32),
                pltpu.VMEM((LAGS, height, 128), jnp.bfloat16),
                pltpu.SemaphoreType.DMA((3,)),
            ],
        ),
        input_output_aliases={count + 3: 0},
        compiler_params=pltpu.CompilerParams(vmem_limit_bytes=60 << 20),
        cost_estimate=pl.CostEstimate(
            flops=2 * height * FB * 256 * 8 * 32 + 2 * height * 128 * 2 * FB * LAG_PAD,
            bytes_accessed=PAIRS * 256 * 256 * 2 + 2 * height * 128 * LAGS,
            transcendentals=0,
        ),
        name="pair_block",
    )(meta, *shards, right, table, out)


def make_table(band_range):
    order = jnp.arange(FB, dtype=jnp.int32)
    freq_index = (order % SEGMENTS) * ROWS + order // SEGMENTS
    lag_index = jnp.arange(LAG_PAD, dtype=jnp.int32) - LAGS // 2
    turns = jnp.mod((F0 + freq_index)[None, :] * lag_index[:, None], NFFT)
    theta = turns.astype(jnp.float32) * (2.0 * math.pi / NFFT)
    inband = ((freq_index >= band_range[0]) & (freq_index < band_range[1])).astype(jnp.float32)[None, :]
    return jnp.concatenate([inband * jnp.cos(theta), -inband * jnp.sin(theta)], axis=1).astype(jnp.bfloat16)


def relay_body(spectra, request, table):
    rows, sides = lax.axis_size("row"), lax.axis_size("side")
    axes = ("row", "plane", "side")
    row_id, plane, side = (lax.axis_index(name) for name in axes)
    width = spectra.shape[2]
    core, chip = row_id % 2, row_id // 2
    depth = plane - row_id
    devices = [(r, p, x) for r in range(rows) for p in range(rows) for x in range(sides)]

    def send(value, pairs):
        number = [tuple((r * rows + p) * sides + x for r, p, x in pair) for pair in pairs]
        return lax.ppermute(value, axes, number)

    def join(mine, sibling):
        first = jnp.where(core == 0, mine, sibling)
        second = jnp.where(core == 0, sibling, mine)
        return jnp.concatenate([first, second], axis=1)

    core_flip = [((r, p, x), (r ^ 1, p, x)) for r, p, x in devices]
    chip_flip = [((r, p, x), (r ^ 2, p, x)) for r, p, x in devices]

    shard = whiten(spectra, 1)[0]
    joined = join(shard, send(shard, core_flip))
    across = send(shard, chip_flip)
    joined_across = join(across, send(across, core_flip))
    offsets = jnp.stack([2 * chip * width, 2 * (1 - chip) * width]).astype(jnp.int32)
    right, out = weights(offsets, [joined, joined_across], sides * rows * width)

    def climb(value, d):
        return send(
            value,
            [
                ((r, p, x), (r, p + 1, x))
                for r, p, x in devices
                if p + 1 < rows and p - d + 1 >= 0 and (p - d + 1 - r) % 2 == 0
            ],
        )

    def to_row(value, d, flip_side, flip_chip):
        takers = [(r, p, x) for r, p, x in devices if p - r == d]
        return send(value, [((r ^ 2 * flip_chip, p, x ^ flip_side), (r, p, x)) for r, p, x in takers])

    after = lax.optimization_barrier
    once = climb(joined, 1)
    side_zero = to_row(joined, 0, 1, 0)
    both_zero = to_row(joined_across, 0, 1, 0)
    twice = climb(once, 2)
    chip_one = to_row(once, 1, 0, 1)
    side_one = to_row(once, 1, 1, 0)
    twice, side_zero, both_zero, chip_one, right, table = after((twice, side_zero, both_zero, chip_one, right, table))
    thrice = climb(twice, 3)
    chip_two = to_row(twice, 2, 0, 1)
    side_two = to_row(twice, 2, 1, 0)
    both_one = to_row(chip_one, 1, 1, 0)
    thrice, side_one, side_two, chip_two, twice = after((thrice, side_one, side_two, chip_two, twice))
    chip_three = to_row(thrice, 3, 0, 1)
    side_three = to_row(thrice, 3, 1, 0)
    both_two = to_row(twice, 2, 1, 1)

    by_depth = jnp.where(request == 1, depth, -1)

    def place(flip_side, flip_chip):
        return ((side ^ flip_side) * rows + 2 * (chip ^ flip_chip)) * width

    out = pair_block(by_depth, place(0, 0), [joined, once, twice, thrice], right, table, out)
    chip_three, out = after((chip_three, out))
    both_three = to_row(chip_three, 3, 1, 0)
    out = pair_block(by_depth, place(1, 0), [side_zero, side_one, side_two, side_three], right, table, out)
    out = pair_block(by_depth, place(0, 1), [joined_across, chip_one, chip_two, chip_three], right, table, out)
    return pair_block(by_depth, place(1, 1), [both_zero, both_one, both_two, both_three], right, table, out)


def gather_body(spectra, request, table):
    shard = whiten(spectra, 1)[0]
    width = shard.shape[1]
    rows = lax.axis_size("row")
    sides = lax.axis_size("side")
    column = lax.all_gather(shard, "row", axis=1, tiled=True)
    grouped = lax.all_gather(shard, ("plane", "side"), axis=0).reshape(rows, sides, ROWS, width, 128)
    moved = lax.all_to_all(grouped, "row", split_axis=0, concat_axis=0)
    block = jnp.transpose(moved, (2, 1, 0, 3, 4)).reshape(ROWS, sides * rows * width, 128)
    right, out = weights(jnp.zeros((1,), jnp.int32), [column], block.shape[1])
    group = min(64, block.shape[1])
    for at in range(0, block.shape[1], group):
        out = pair_block(request - 1, jnp.int32(at), [block[:, at : at + group]], right, table, out)
    return out


def body(spectra, pair_mask, band_range):
    rows = lax.axis_size("row")
    sides = lax.axis_size("side")
    width = spectra.shape[2]
    request = ((pair_mask[0, 0] == 1) & (lax.axis_index("plane") >= lax.axis_index("row"))).astype(jnp.int32)
    table = make_table(band_range)
    if (rows, sides) == (4, 2) and width % 32 == 0:
        out = relay_body(spectra, request, table)
    else:
        out = gather_body(spectra, request, table)
    return jnp.transpose(out, (1, 2, 0))


def solution(mesh):
    rows, cols = mesh.devices.shape
    cut = Mesh(mesh.devices.reshape(rows, rows, cols // rows), ("row", "plane", "side"))
    return jax.shard_map(
        body,
        mesh=cut,
        in_specs=(P(None, None, ("plane", "side", "row"), None), P("row", ("plane", "side")), P()),
        out_specs=P("row", ("plane", "side"), None),
        check_vma=False,
    )
```

```python
import functools
import math

import jax
import jax.numpy as jnp
from jax import lax
from jax.experimental import pallas as pl
from jax.experimental.pallas import tpu as pltpu
from jax.sharding import Mesh
from jax.sharding import PartitionSpec as P

W = 16
FB = 512
LAGS = 201
NFFT = 15000
F0 = 60
EPS = 1e-06

SEGMENTS = 4
ROWS = FB // SEGMENTS
PAIRS = ROWS // 2
LAG_PAD = 208


def whiten_kernel(*refs, width, parts):
    x_refs, whole_ref, out_refs, scratch = refs[:SEGMENTS], refs[SEGMENTS], refs[SEGMENTS + 1 : -1], refs[-1]

    def channel(c, carry):
        tiles = [x_ref[pl.ds(c, 2 * W, stride=width), :] for x_ref in x_refs]
        total = sum(v[:W] * v[:W] + v[W:] * v[W:] for v in tiles)
        power = jnp.sum(total, axis=-1, keepdims=True) * (1.0 / FB)
        scale = lax.rsqrt(power + EPS)
        scale = jnp.concatenate([scale, scale], axis=0)
        stacked = jnp.concatenate([v * scale for v in tiles], axis=0)
        scratch[pl.ds(c, ROWS, stride=width), :] = stacked.T
        return carry

    lax.fori_loop(0, width, channel, 0, unroll=2)
    step = width // parts
    full = scratch[...].reshape(ROWS, width, 128).astype(jnp.bfloat16)
    whole_ref[...] = full
    for g, out_ref in enumerate(out_refs):
        out_ref[...] = full[:, g * step : (g + 1) * step, :]


def whiten(spectra, parts):
    width = spectra.shape[2]
    widths = [width] + ([width // parts] * parts if parts > 1 else [])
    lines = 2 * W * width
    flat = spectra.reshape(lines, FB)
    return pl.pallas_call(
        functools.partial(whiten_kernel, width=width, parts=parts),
        out_shape=[jax.ShapeDtypeStruct((ROWS, n, 128), jnp.bfloat16) for n in widths],
        grid=(1,),
        in_specs=[pl.BlockSpec((lines, ROWS), functools.partial(lambda q, i: (0, q), q)) for q in range(SEGMENTS)],
        out_specs=[pl.BlockSpec((ROWS, n, 128), lambda i: (0, 0, 0)) for n in widths],
        scratch_shapes=[pltpu.VMEM((ROWS * width, 128), jnp.float32)],
        compiler_params=pltpu.CompilerParams(vmem_limit_bytes=40 << 20),
        name="whiten",
    )(*[flat] * SEGMENTS)


def weights_kernel(offset_ref, *refs, count, step):
    in_refs, out_ref, clear_ref, scratch = refs[:count], refs[count], refs[count + 1], refs[count + 2]
    clear_ref[...] = jnp.zeros_like(clear_ref)
    for i in range(count):
        at = pl.multiple_of(offset_ref[i], step)
        scratch[:, pl.ds(at, step), :] = in_refs[i][...].astype(jnp.float32)

    def row(t, carry):
        for s in range(2):
            real = scratch[2 * t + s].T
            pieces = []
            for q in range(SEGMENTS):
                lo = q * 2 * W
                pieces += [-real[lo + W : lo + 2 * W], real[lo : lo + W]]
            imag = jnp.concatenate(pieces, axis=0)
            both = jnp.concatenate([real, imag], axis=1).astype(jnp.bfloat16)
            out_ref[t, s * 128 : (s + 1) * 128, :] = both
        return carry

    lax.fori_loop(0, out_ref.shape[0], row, 0, unroll=2)


def weights(offsets, shards, height):
    count = len(shards)
    step = shards[0].shape[1]
    tiles = 4
    return pl.pallas_call(
        functools.partial(weights_kernel, count=count, step=step),
        out_shape=[
            jax.ShapeDtypeStruct((PAIRS, 256, 256), jnp.bfloat16),
            jax.ShapeDtypeStruct((LAGS, height, count * step), jnp.bfloat16),
        ],
        grid_spec=pltpu.PrefetchScalarGridSpec(
            num_scalar_prefetch=1,
            grid=(tiles,),
            in_specs=[pl.BlockSpec((ROWS // tiles, step, 128), lambda i, o: (i, 0, 0))] * count,
            out_specs=[
                pl.BlockSpec((PAIRS // tiles, 256, 256), lambda i, o: (i, 0, 0)),
                pl.BlockSpec((LAGS, height // tiles, count * step), lambda i, o: (0, i, 0)),
            ],
            scratch_shapes=[pltpu.VMEM((ROWS // tiles, count * step, 128), jnp.float32)],
        ),
        compiler_params=pltpu.CompilerParams(vmem_limit_bytes=40 << 20),
        name="weights",
    )(offsets, *shards)


def pair_kernel(meta_ref, *refs, count, height, unroll_sum, unroll_lag, pitch):
    x_refs = refs[:count]
    w_ref, t_ref, _, out_ref = refs[count : count + 4]
    xbuf, wide, wbuf, tbuf, cross, lags, stage, sems = refs[count + 4 :]

    @pl.when(meta_ref[0] >= 0)
    def _():
        for i in range(count):

            @pl.when(meta_ref[0] == i)
            def _(i=i):
                pltpu.make_async_copy(x_refs[i], xbuf, sems.at[0]).start()

        others = [
            pltpu.make_async_copy(w_ref, wbuf, sems.at[1]),
            pltpu.make_async_copy(t_ref, tbuf, sems.at[2]),
        ]
        for copy in others:
            copy.start()
        pltpu.make_async_copy(x_refs[0], xbuf, sems.at[0]).wait()
        wide[...] = xbuf[...].astype(jnp.float32).reshape(ROWS * height, 128)
        for copy in others:
            copy.wait()

        sub = lax.broadcasted_iota(jnp.int32, (8, 128), 0)
        segment = lax.broadcasted_iota(jnp.int32, (8, 128), 1) // (2 * W)
        masks = (segment == sub, segment == sub - SEGMENTS)

        def window_sums(h, carry):
            halves = []
            for u in range(2):
                pair = 2 * h + u
                rows = []
                for a in range(height):
                    halves_of_k = [
                        jnp.where(masks[s], wide[pl.ds((2 * pair + s) * height + a, 8, stride=0), :], 0.0)
                        for s in range(2)
                    ]
                    rows.append(jnp.concatenate(halves_of_k, axis=1))
                left = jnp.concatenate(rows, axis=0).astype(jnp.bfloat16)
                sums = jnp.dot(left, wbuf[pair], preferred_element_type=jnp.float32)
                halves.append(sums.reshape(height, 8, 256))
            both = jnp.concatenate(halves, axis=1).astype(jnp.bfloat16)
            cross[:, pl.ds(pl.multiple_of(h * 16, 16), 16), :] = both
            return carry

        lax.fori_loop(0, PAIRS // 2, window_sums, 0, unroll=unroll_sum)

        def lag_sums(h, carry):
            first, second = cross[2 * h], cross[2 * h + 1]
            real = jnp.concatenate([first[:, :128], second[:, :128]], axis=1)
            imag = jnp.concatenate([first[:, 128:], second[:, 128:]], axis=1)
            right = jnp.concatenate([real, imag], axis=0)
            out = jnp.dot(tbuf[...], right, preferred_element_type=jnp.float32)
            out = out * (1.0 / math.sqrt(W * FB))
            lags[pl.ds(2 * h, LAG_PAD, stride=pitch), :] = out[:, :128]
            lags[pl.ds(2 * h + 1, LAG_PAD, stride=pitch), :] = out[:, 128:]
            return carry

        lax.fori_loop(0, height // 2, lag_sums, 0, unroll=unroll_lag)
        stage[...] = lags[...].reshape(LAG_PAD, pitch, 128)[:LAGS, :height].astype(jnp.bfloat16)
        at = pl.multiple_of(meta_ref[1], height)
        back = pltpu.make_async_copy(stage, out_ref.at[:, pl.ds(at, height), :], sems.at[0])
        back.start()
        back.wait()


def pair_block(choice, place, shards, right, table, out, unroll_sum=8, unroll_lag=8, pad=8):
    count = len(shards)
    height = shards[0].shape[1]
    meta = jnp.stack([choice, place]).astype(jnp.int32)
    anywhere = pl.BlockSpec(memory_space=pl.ANY)
    return pl.pallas_call(
        functools.partial(
            pair_kernel,
            count=count,
            height=height,
            unroll_sum=unroll_sum,
            unroll_lag=unroll_lag,
            pitch=height + pad,
        ),
        out_shape=jax.ShapeDtypeStruct(out.shape, out.dtype),
        grid_spec=pltpu.PrefetchScalarGridSpec(
            num_scalar_prefetch=1,
            grid=(),
            in_specs=[anywhere] * (count + 3),
            out_specs=anywhere,
            scratch_shapes=[
                pltpu.VMEM((ROWS, height, 128), jnp.bfloat16),
                pltpu.VMEM((ROWS * height, 128), jnp.float32),
                pltpu.VMEM((PAIRS, 256, 256), jnp.bfloat16),
                pltpu.VMEM((LAG_PAD, 2 * FB), jnp.bfloat16),
                pltpu.VMEM((height, FB, 256), jnp.bfloat16),
                pltpu.VMEM((LAG_PAD * (height + pad), 128), jnp.float32),
                pltpu.VMEM((LAGS, height, 128), jnp.bfloat16),
                pltpu.SemaphoreType.DMA((3,)),
            ],
        ),
        input_output_aliases={count + 3: 0},
        compiler_params=pltpu.CompilerParams(vmem_limit_bytes=60 << 20),
        cost_estimate=pl.CostEstimate(
            flops=2 * height * FB * 256 * 8 * 32 + 2 * height * 128 * 2 * FB * LAG_PAD,
            bytes_accessed=PAIRS * 256 * 256 * 2 + 2 * height * 128 * LAGS,
            transcendentals=0,
        ),
        name="pair_block",
    )(meta, *shards, right, table, out)


def make_table(band_range):
    order = jnp.arange(FB, dtype=jnp.int32)
    freq_index = (order % SEGMENTS) * ROWS + order // SEGMENTS
    lag_index = jnp.arange(LAG_PAD, dtype=jnp.int32) - LAGS // 2
    turns = jnp.mod((F0 + freq_index)[None, :] * lag_index[:, None], NFFT)
    theta = turns.astype(jnp.float32) * (2.0 * math.pi / NFFT)
    inband = ((freq_index >= band_range[0]) & (freq_index < band_range[1])).astype(jnp.float32)[None, :]
    return jnp.concatenate([inband * jnp.cos(theta), -inband * jnp.sin(theta)], axis=1).astype(jnp.bfloat16)


def relay_body(spectra, request, table):
    rows, sides = lax.axis_size("row"), lax.axis_size("side")
    axes = ("row", "plane", "side")
    row_id, plane, side = (lax.axis_index(name) for name in axes)
    width = spectra.shape[2]
    core, chip = row_id % 2, row_id // 2
    depth = plane - row_id
    devices = [(r, p, x) for r in range(rows) for p in range(rows) for x in range(sides)]

    def send(value, pairs):
        number = [tuple((r * rows + p) * sides + x for r, p, x in pair) for pair in pairs]
        return lax.ppermute(value, axes, number)

    def join(mine, sibling):
        first = jnp.where(core == 0, mine, sibling)
        second = jnp.where(core == 0, sibling, mine)
        return jnp.concatenate([first, second], axis=1)

    core_flip = [((r, p, x), (r ^ 1, p, x)) for r, p, x in devices]
    chip_flip = [((r, p, x), (r ^ 2, p, x)) for r, p, x in devices]

    shard = whiten(spectra, 1)[0]
    joined = join(shard, send(shard, core_flip))
    across = send(shard, chip_flip)
    joined_across = join(across, send(across, core_flip))
    offsets = jnp.stack([2 * chip * width, 2 * (1 - chip) * width]).astype(jnp.int32)
    right, out = weights(offsets, [joined, joined_across], sides * rows * width)

    def climb(value, d):
        return send(
            value,
            [
                ((r, p, x), (r, p + 1, x))
                for r, p, x in devices
                if p + 1 < rows and p - d + 1 >= 0 and (p - d + 1 - r) % 2 == 0
            ],
        )

    def to_row(value, d, flip_side, flip_chip):
        takers = [(r, p, x) for r, p, x in devices if p - r == d]
        return send(value, [((r ^ 2 * flip_chip, p, x ^ flip_side), (r, p, x)) for r, p, x in takers])

    after = lax.optimization_barrier
    once = climb(joined, 1)
    side_zero = to_row(joined, 0, 1, 0)
    both_zero = to_row(joined, 0, 1, 1)
    twice = climb(once, 2)
    chip_one = to_row(once, 1, 0, 1)
    side_one = to_row(once, 1, 1, 0)
    twice, side_zero, both_zero, right, table = after((twice, side_zero, both_zero, right, table))
    thrice = climb(twice, 3)
    chip_two = to_row(twice, 2, 0, 1)
    side_two = to_row(twice, 2, 1, 0)
    thrice, chip_one, side_one, chip_two, side_two, twice = after(
        (thrice, chip_one, side_one, chip_two, side_two, twice)
    )
    both_one = to_row(chip_one, 1, 1, 0)
    chip_three = to_row(thrice, 3, 0, 1)
    side_three = to_row(thrice, 3, 1, 0)
    both_two = to_row(twice, 2, 1, 1)

    by_depth = jnp.where(request == 1, depth, -1)

    def place(flip_side, flip_chip):
        return ((side ^ flip_side) * rows + 2 * (chip ^ flip_chip)) * width

    out = pair_block(by_depth, place(0, 0), [joined, once, twice, thrice], right, table, out)
    chip_three, out = after((chip_three, out))
    both_three = to_row(chip_three, 3, 1, 0)
    out = pair_block(by_depth, place(1, 0), [side_zero, side_one, side_two, side_three], right, table, out)
    out = pair_block(by_depth, place(0, 1), [joined_across, chip_one, chip_two, chip_three], right, table, out)
    return pair_block(by_depth, place(1, 1), [both_zero, both_one, both_two, both_three], right, table, out)


def gather_body(spectra, request, table):
    shard = whiten(spectra, 1)[0]
    width = shard.shape[1]
    rows = lax.axis_size("row")
    sides = lax.axis_size("side")
    column = lax.all_gather(shard, "row", axis=1, tiled=True)
    grouped = lax.all_gather(shard, ("plane", "side"), axis=0).reshape(rows, sides, ROWS, width, 128)
    moved = lax.all_to_all(grouped, "row", split_axis=0, concat_axis=0)
    block = jnp.transpose(moved, (2, 1, 0, 3, 4)).reshape(ROWS, sides * rows * width, 128)
    right, out = weights(jnp.zeros((1,), jnp.int32), [column], block.shape[1])
    group = min(64, block.shape[1])
    for at in range(0, block.shape[1], group):
        out = pair_block(request - 1, jnp.int32(at), [block[:, at : at + group]], right, table, out)
    return out


def body(spectra, pair_mask, band_range):
    rows = lax.axis_size("row")
    sides = lax.axis_size("side")
    width = spectra.shape[2]
    request = ((pair_mask[0, 0] == 1) & (lax.axis_index("plane") >= lax.axis_index("row"))).astype(jnp.int32)
    table = make_table(band_range)
    if (rows, sides) == (4, 2) and width % 32 == 0:
        out = relay_body(spectra, request, table)
    else:
        out = gather_body(spectra, request, table)
    return jnp.transpose(out, (1, 2, 0))


def solution(mesh):
    rows, cols = mesh.devices.shape
    cut = Mesh(mesh.devices.reshape(rows, rows, cols // rows), ("row", "plane", "side"))
    return jax.shard_map(
        body,
        mesh=cut,
        in_specs=(P(None, None, ("plane", "side", "row"), None), P("row", ("plane", "side")), P()),
        out_specs=P("row", ("plane", "side"), None),
        check_vma=False,
    )
```

```python
import functools
import math

import jax
import jax.numpy as jnp
from jax import lax
from jax.experimental import pallas as pl
from jax.experimental.pallas import tpu as pltpu
from jax.sharding import Mesh
from jax.sharding import PartitionSpec as P

W = 16
FB = 512
LAGS = 201
NFFT = 15000
F0 = 60
EPS = 1e-06

SEGMENTS = 4
ROWS = FB // SEGMENTS
PAIRS = ROWS // 2
LAG_PAD = 208


def whiten_kernel(*refs, width, parts):
    x_refs, whole_ref, out_refs, scratch = refs[:SEGMENTS], refs[SEGMENTS], refs[SEGMENTS + 1 : -1], refs[-1]

    def channel(c, carry):
        tiles = [x_ref[pl.ds(c, 2 * W, stride=width), :] for x_ref in x_refs]
        total = sum(v[:W] * v[:W] + v[W:] * v[W:] for v in tiles)
        power = jnp.sum(total, axis=-1, keepdims=True) * (1.0 / FB)
        scale = lax.rsqrt(power + EPS)
        scale = jnp.concatenate([scale, scale], axis=0)
        stacked = jnp.concatenate([v * scale for v in tiles], axis=0)
        scratch[pl.ds(c, ROWS, stride=width), :] = stacked.T
        return carry

    lax.fori_loop(0, width, channel, 0, unroll=2)
    step = width // parts
    full = scratch[...].reshape(ROWS, width, 128).astype(jnp.bfloat16)
    whole_ref[...] = full
    for g, out_ref in enumerate(out_refs):
        out_ref[...] = full[:, g * step : (g + 1) * step, :]


def whiten(spectra, parts):
    width = spectra.shape[2]
    widths = [width] + ([width // parts] * parts if parts > 1 else [])
    lines = 2 * W * width
    flat = spectra.reshape(lines, FB)
    return pl.pallas_call(
        functools.partial(whiten_kernel, width=width, parts=parts),
        out_shape=[jax.ShapeDtypeStruct((ROWS, n, 128), jnp.bfloat16) for n in widths],
        grid=(1,),
        in_specs=[pl.BlockSpec((lines, ROWS), functools.partial(lambda q, i: (0, q), q)) for q in range(SEGMENTS)],
        out_specs=[pl.BlockSpec((ROWS, n, 128), lambda i: (0, 0, 0)) for n in widths],
        scratch_shapes=[pltpu.VMEM((ROWS * width, 128), jnp.float32)],
        compiler_params=pltpu.CompilerParams(vmem_limit_bytes=40 << 20),
        name="whiten",
    )(*[flat] * SEGMENTS)


def weights_kernel(offset_ref, *refs, count, step):
    in_refs, out_ref, clear_ref, scratch = refs[:count], refs[count], refs[count + 1], refs[count + 2]
    clear_ref[...] = jnp.zeros_like(clear_ref)
    for i in range(count):
        at = pl.multiple_of(offset_ref[i], step)
        scratch[:, pl.ds(at, step), :] = in_refs[i][...].astype(jnp.float32)

    def row(t, carry):
        for s in range(2):
            real = scratch[2 * t + s].T
            pieces = []
            for q in range(SEGMENTS):
                lo = q * 2 * W
                pieces += [-real[lo + W : lo + 2 * W], real[lo : lo + W]]
            imag = jnp.concatenate(pieces, axis=0)
            both = jnp.concatenate([real, imag], axis=1).astype(jnp.bfloat16)
            out_ref[t, s * 128 : (s + 1) * 128, :] = both
        return carry

    lax.fori_loop(0, out_ref.shape[0], row, 0, unroll=2)


def weights(offsets, shards, height):
    count = len(shards)
    step = shards[0].shape[1]
    tiles = 4
    return pl.pallas_call(
        functools.partial(weights_kernel, count=count, step=step),
        out_shape=[
            jax.ShapeDtypeStruct((PAIRS, 256, 256), jnp.bfloat16),
            jax.ShapeDtypeStruct((LAGS, height, count * step), jnp.bfloat16),
        ],
        grid_spec=pltpu.PrefetchScalarGridSpec(
            num_scalar_prefetch=1,
            grid=(tiles,),
            in_specs=[pl.BlockSpec((ROWS // tiles, step, 128), lambda i, o: (i, 0, 0))] * count,
            out_specs=[
                pl.BlockSpec((PAIRS // tiles, 256, 256), lambda i, o: (i, 0, 0)),
                pl.BlockSpec((LAGS, height // tiles, count * step), lambda i, o: (0, i, 0)),
            ],
            scratch_shapes=[pltpu.VMEM((ROWS // tiles, count * step, 128), jnp.float32)],
        ),
        compiler_params=pltpu.CompilerParams(vmem_limit_bytes=40 << 20),
        name="weights",
    )(offsets, *shards)


def pair_kernel(meta_ref, *refs, count, height, unroll_sum, unroll_lag, pitch):
    x_refs = refs[:count]
    w_ref, t_ref, _, out_ref = refs[count : count + 4]
    xbuf, wide, wbuf, tbuf, cross, lags, stage, sems = refs[count + 4 :]

    @pl.when(meta_ref[0] >= 0)
    def _():
        for i in range(count):

            @pl.when(meta_ref[0] == i)
            def _(i=i):
                pltpu.make_async_copy(x_refs[i], xbuf, sems.at[0]).start()

        others = [
            pltpu.make_async_copy(w_ref, wbuf, sems.at[1]),
            pltpu.make_async_copy(t_ref, tbuf, sems.at[2]),
        ]
        for copy in others:
            copy.start()
        pltpu.make_async_copy(x_refs[0], xbuf, sems.at[0]).wait()
        wide[...] = xbuf[...].astype(jnp.float32).reshape(ROWS * height, 128)
        for copy in others:
            copy.wait()

        sub = lax.broadcasted_iota(jnp.int32, (8, 128), 0)
        segment = lax.broadcasted_iota(jnp.int32, (8, 128), 1) // (2 * W)
        masks = (segment == sub, segment == sub - SEGMENTS)

        def window_sums(h, carry):
            halves = []
            for u in range(2):
                pair = 2 * h + u
                rows = []
                for a in range(height):
                    halves_of_k = [
                        jnp.where(masks[s], wide[pl.ds((2 * pair + s) * height + a, 8, stride=0), :], 0.0)
                        for s in range(2)
                    ]
                    rows.append(jnp.concatenate(halves_of_k, axis=1))
                left = jnp.concatenate(rows, axis=0).astype(jnp.bfloat16)
                sums = jnp.dot(left, wbuf[pair], preferred_element_type=jnp.float32)
                halves.append(sums.reshape(height, 8, 256))
            both = jnp.concatenate(halves, axis=1).astype(jnp.bfloat16)
            cross[:, pl.ds(pl.multiple_of(h * 16, 16), 16), :] = both
            return carry

        lax.fori_loop(0, PAIRS // 2, window_sums, 0, unroll=unroll_sum)

        def lag_sums(h, carry):
            first, second = cross[2 * h], cross[2 * h + 1]
            real = jnp.concatenate([first[:, :128], second[:, :128]], axis=1)
            imag = jnp.concatenate([first[:, 128:], second[:, 128:]], axis=1)
            right = jnp.concatenate([real, imag], axis=0)
            out = jnp.dot(tbuf[...], right, preferred_element_type=jnp.float32)
            out = out * (1.0 / math.sqrt(W * FB))
            lags[pl.ds(2 * h, LAG_PAD, stride=pitch), :] = out[:, :128]
            lags[pl.ds(2 * h + 1, LAG_PAD, stride=pitch), :] = out[:, 128:]
            return carry

        lax.fori_loop(0, height // 2, lag_sums, 0, unroll=unroll_lag)
        stage[...] = lags[...].reshape(LAG_PAD, pitch, 128)[:LAGS, :height].astype(jnp.bfloat16)
        at = pl.multiple_of(meta_ref[1], height)
        back = pltpu.make_async_copy(stage, out_ref.at[:, pl.ds(at, height), :], sems.at[0])
        back.start()
        back.wait()


def pair_block(choice, place, shards, right, table, out, unroll_sum=8, unroll_lag=8, pad=8):
    count = len(shards)
    height = shards[0].shape[1]
    meta = jnp.stack([choice, place]).astype(jnp.int32)
    anywhere = pl.BlockSpec(memory_space=pl.ANY)
    return pl.pallas_call(
        functools.partial(
            pair_kernel,
            count=count,
            height=height,
            unroll_sum=unroll_sum,
            unroll_lag=unroll_lag,
            pitch=height + pad,
        ),
        out_shape=jax.ShapeDtypeStruct(out.shape, out.dtype),
        grid_spec=pltpu.PrefetchScalarGridSpec(
            num_scalar_prefetch=1,
            grid=(),
            in_specs=[anywhere] * (count + 3),
            out_specs=anywhere,
            scratch_shapes=[
                pltpu.VMEM((ROWS, height, 128), jnp.bfloat16),
                pltpu.VMEM((ROWS * height, 128), jnp.float32),
                pltpu.VMEM((PAIRS, 256, 256), jnp.bfloat16),
                pltpu.VMEM((LAG_PAD, 2 * FB), jnp.bfloat16),
                pltpu.VMEM((height, FB, 256), jnp.bfloat16),
                pltpu.VMEM((LAG_PAD * (height + pad), 128), jnp.float32),
                pltpu.VMEM((LAGS, height, 128), jnp.bfloat16),
                pltpu.SemaphoreType.DMA((3,)),
            ],
        ),
        input_output_aliases={count + 3: 0},
        compiler_params=pltpu.CompilerParams(vmem_limit_bytes=60 << 20),
        cost_estimate=pl.CostEstimate(
            flops=2 * height * FB * 256 * 8 * 32 + 2 * height * 128 * 2 * FB * LAG_PAD,
            bytes_accessed=PAIRS * 256 * 256 * 2 + 2 * height * 128 * LAGS,
            transcendentals=0,
        ),
        name="pair_block",
    )(meta, *shards, right, table, out)


def make_table(band_range):
    order = jnp.arange(FB, dtype=jnp.int32)
    freq_index = (order % SEGMENTS) * ROWS + order // SEGMENTS
    lag_index = jnp.arange(LAG_PAD, dtype=jnp.int32) - LAGS // 2
    turns = jnp.mod((F0 + freq_index)[None, :] * lag_index[:, None], NFFT)
    theta = turns.astype(jnp.float32) * (2.0 * math.pi / NFFT)
    inband = ((freq_index >= band_range[0]) & (freq_index < band_range[1])).astype(jnp.float32)[None, :]
    return jnp.concatenate([inband * jnp.cos(theta), -inband * jnp.sin(theta)], axis=1).astype(jnp.bfloat16)


def relay_body(spectra, request, table):
    rows, sides = lax.axis_size("row"), lax.axis_size("side")
    axes = ("row", "plane", "side")
    row_id, plane, side = (lax.axis_index(name) for name in axes)
    width = spectra.shape[2]
    core, chip = row_id % 2, row_id // 2
    depth = plane - row_id
    devices = [(r, p, x) for r in range(rows) for p in range(rows) for x in range(sides)]

    def send(value, pairs):
        number = [tuple((r * rows + p) * sides + x for r, p, x in pair) for pair in pairs]
        return lax.ppermute(value, axes, number)

    def join(mine, sibling):
        first = jnp.where(core == 0, mine, sibling)
        second = jnp.where(core == 0, sibling, mine)
        return jnp.concatenate([first, second], axis=1)

    core_flip = [((r, p, x), (r ^ 1, p, x)) for r, p, x in devices]
    chip_flip = [((r, p, x), (r ^ 2, p, x)) for r, p, x in devices]

    shard = whiten(spectra, 1)[0]
    joined = join(shard, send(shard, core_flip))
    across = send(shard, chip_flip)
    def climb(value, d):
        return send(
            value,
            [
                ((r, p, x), (r, p + 1, x))
                for r, p, x in devices
                if p + 1 < rows and p - d + 1 >= 0 and (p - d + 1 - r) % 2 == 0
            ],
        )

    def to_row(value, d, flip_side, flip_chip):
        takers = [(r, p, x) for r, p, x in devices if p - r == d]
        return send(value, [((r ^ 2 * flip_chip, p, x ^ flip_side), (r, p, x)) for r, p, x in takers])

    after = lax.optimization_barrier
    once = climb(joined, 1)
    side_zero = to_row(joined, 0, 1, 0)
    both_zero = to_row(joined, 0, 1, 1)
    once, table, across = after((once, table, across))
    twice = climb(once, 2)
    joined_across = join(across, send(across, core_flip))
    offsets = jnp.stack([2 * chip * width, 2 * (1 - chip) * width]).astype(jnp.int32)
    right, out = weights(offsets, [joined, joined_across], sides * rows * width)
    chip_one = to_row(once, 1, 0, 1)
    side_one = to_row(once, 1, 1, 0)
    twice, side_zero, both_zero = after((twice, side_zero, both_zero))
    thrice = climb(twice, 3)
    chip_two = to_row(twice, 2, 0, 1)
    side_two = to_row(twice, 2, 1, 0)
    thrice, chip_one, side_one, chip_two, side_two, twice, right, out = after(
        (thrice, chip_one, side_one, chip_two, side_two, twice, right, out)
    )
    both_one = to_row(chip_one, 1, 1, 0)
    chip_three = to_row(thrice, 3, 0, 1)
    side_three = to_row(thrice, 3, 1, 0)

    by_depth = jnp.where(request == 1, depth, -1)

    def place(flip_side, flip_chip):
        return ((side ^ flip_side) * rows + 2 * (chip ^ flip_chip)) * width

    out = pair_block(by_depth, place(0, 0), [joined, once, twice, thrice], right, table, out)
    chip_three, twice, out = after((chip_three, twice, out))
    both_two = to_row(twice, 2, 1, 1)
    both_three = to_row(chip_three, 3, 1, 0)
    out = pair_block(by_depth, place(1, 0), [side_zero, side_one, side_two, side_three], right, table, out)
    out = pair_block(by_depth, place(0, 1), [joined_across, chip_one, chip_two, chip_three], right, table, out)
    return pair_block(by_depth, place(1, 1), [both_zero, both_one, both_two, both_three], right, table, out)


def gather_body(spectra, request, table):
    shard = whiten(spectra, 1)[0]
    width = shard.shape[1]
    rows = lax.axis_size("row")
    sides = lax.axis_size("side")
    column = lax.all_gather(shard, "row", axis=1, tiled=True)
    grouped = lax.all_gather(shard, ("plane", "side"), axis=0).reshape(rows, sides, ROWS, width, 128)
    moved = lax.all_to_all(grouped, "row", split_axis=0, concat_axis=0)
    block = jnp.transpose(moved, (2, 1, 0, 3, 4)).reshape(ROWS, sides * rows * width, 128)
    right, out = weights(jnp.zeros((1,), jnp.int32), [column], block.shape[1])
    group = min(64, block.shape[1])
    for at in range(0, block.shape[1], group):
        out = pair_block(request - 1, jnp.int32(at), [block[:, at : at + group]], right, table, out)
    return out


def body(spectra, pair_mask, band_range):
    rows = lax.axis_size("row")
    sides = lax.axis_size("side")
    width = spectra.shape[2]
    request = ((pair_mask[0, 0] == 1) & (lax.axis_index("plane") >= lax.axis_index("row"))).astype(jnp.int32)
    table = make_table(band_range)
    if (rows, sides) == (4, 2) and width % 32 == 0:
        out = relay_body(spectra, request, table)
    else:
        out = gather_body(spectra, request, table)
    return jnp.transpose(out, (1, 2, 0))


def solution(mesh):
    rows, cols = mesh.devices.shape
    cut = Mesh(mesh.devices.reshape(rows, rows, cols // rows), ("row", "plane", "side"))
    return jax.shard_map(
        body,
        mesh=cut,
        in_specs=(P(None, None, ("plane", "side", "row"), None), P("row", ("plane", "side")), P()),
        out_specs=P("row", ("plane", "side"), None),
        check_vma=False,
    )
```

```python
import functools
import math

import jax
import jax.numpy as jnp
from jax import lax
from jax.experimental import pallas as pl
from jax.experimental.pallas import tpu as pltpu
from jax.sharding import Mesh
from jax.sharding import PartitionSpec as P

W = 16
FB = 512
LAGS = 201
NFFT = 15000
F0 = 60
EPS = 1e-06

SEGMENTS = 4
ROWS = FB // SEGMENTS
PAIRS = ROWS // 2
LAG_PAD = 208


def whiten_kernel(*refs, width, parts):
    x_refs, whole_ref, out_refs, scratch = refs[:SEGMENTS], refs[SEGMENTS], refs[SEGMENTS + 1 : -1], refs[-1]

    def channel(c, carry):
        tiles = [x_ref[pl.ds(c, 2 * W, stride=width), :] for x_ref in x_refs]
        total = sum(v[:W] * v[:W] + v[W:] * v[W:] for v in tiles)
        power = jnp.sum(total, axis=-1, keepdims=True) * (1.0 / FB)
        scale = lax.rsqrt(power + EPS)
        scale = jnp.concatenate([scale, scale], axis=0)
        stacked = jnp.concatenate([v * scale for v in tiles], axis=0)
        scratch[pl.ds(c, ROWS, stride=width), :] = stacked.T
        return carry

    lax.fori_loop(0, width, channel, 0, unroll=2)
    step = width // parts
    full = scratch[...].reshape(ROWS, width, 128).astype(jnp.bfloat16)
    whole_ref[...] = full
    for g, out_ref in enumerate(out_refs):
        out_ref[...] = full[:, g * step : (g + 1) * step, :]


def whiten(spectra, parts):
    width = spectra.shape[2]
    widths = [width] + ([width // parts] * parts if parts > 1 else [])
    lines = 2 * W * width
    flat = spectra.reshape(lines, FB)
    return pl.pallas_call(
        functools.partial(whiten_kernel, width=width, parts=parts),
        out_shape=[jax.ShapeDtypeStruct((ROWS, n, 128), jnp.bfloat16) for n in widths],
        grid=(1,),
        in_specs=[pl.BlockSpec((lines, ROWS), functools.partial(lambda q, i: (0, q), q)) for q in range(SEGMENTS)],
        out_specs=[pl.BlockSpec((ROWS, n, 128), lambda i: (0, 0, 0)) for n in widths],
        scratch_shapes=[pltpu.VMEM((ROWS * width, 128), jnp.float32)],
        compiler_params=pltpu.CompilerParams(vmem_limit_bytes=40 << 20),
        name="whiten",
    )(*[flat] * SEGMENTS)


def weights_kernel(offset_ref, *refs, count, step):
    in_refs, out_ref, clear_ref, scratch = refs[:count], refs[count], refs[count + 1], refs[count + 2]
    clear_ref[...] = jnp.zeros_like(clear_ref)
    for i in range(count):
        at = pl.multiple_of(offset_ref[i], step)
        scratch[:, pl.ds(at, step), :] = in_refs[i][...].astype(jnp.float32)

    def row(t, carry):
        for s in range(2):
            real = scratch[2 * t + s].T
            pieces = []
            for q in range(SEGMENTS):
                lo = q * 2 * W
                pieces += [-real[lo + W : lo + 2 * W], real[lo : lo + W]]
            imag = jnp.concatenate(pieces, axis=0)
            both = jnp.concatenate([real, imag], axis=1).astype(jnp.bfloat16)
            out_ref[t, s * 128 : (s + 1) * 128, :] = both
        return carry

    lax.fori_loop(0, out_ref.shape[0], row, 0, unroll=2)


def weights(offsets, shards, height):
    count = len(shards)
    step = shards[0].shape[1]
    tiles = 4
    return pl.pallas_call(
        functools.partial(weights_kernel, count=count, step=step),
        out_shape=[
            jax.ShapeDtypeStruct((PAIRS, 256, 256), jnp.bfloat16),
            jax.ShapeDtypeStruct((LAGS, height, count * step), jnp.bfloat16),
        ],
        grid_spec=pltpu.PrefetchScalarGridSpec(
            num_scalar_prefetch=1,
            grid=(tiles,),
            in_specs=[pl.BlockSpec((ROWS // tiles, step, 128), lambda i, o: (i, 0, 0))] * count,
            out_specs=[
                pl.BlockSpec((PAIRS // tiles, 256, 256), lambda i, o: (i, 0, 0)),
                pl.BlockSpec((LAGS, height // tiles, count * step), lambda i, o: (0, i, 0)),
            ],
            scratch_shapes=[pltpu.VMEM((ROWS // tiles, count * step, 128), jnp.float32)],
        ),
        compiler_params=pltpu.CompilerParams(vmem_limit_bytes=40 << 20),
        name="weights",
    )(offsets, *shards)


def pair_kernel(meta_ref, *refs, count, height, unroll_sum, unroll_lag, pitch):
    x_refs = refs[:count]
    w_ref, t_ref, _, out_ref = refs[count : count + 4]
    xbuf, wide, wbuf, tbuf, cross, lags, stage, sems = refs[count + 4 :]

    @pl.when(meta_ref[0] >= 0)
    def _():
        for i in range(count):

            @pl.when(meta_ref[0] == i)
            def _(i=i):
                pltpu.make_async_copy(x_refs[i], xbuf, sems.at[0]).start()

        others = [
            pltpu.make_async_copy(w_ref, wbuf, sems.at[1]),
            pltpu.make_async_copy(t_ref, tbuf, sems.at[2]),
        ]
        for copy in others:
            copy.start()
        pltpu.make_async_copy(x_refs[0], xbuf, sems.at[0]).wait()
        wide[...] = xbuf[...].astype(jnp.float32).reshape(ROWS * height, 128)
        for copy in others:
            copy.wait()

        sub = lax.broadcasted_iota(jnp.int32, (8, 128), 0)
        segment = lax.broadcasted_iota(jnp.int32, (8, 128), 1) // (2 * W)
        masks = (segment == sub, segment == sub - SEGMENTS)

        def window_sums(h, carry):
            halves = []
            for u in range(2):
                pair = 2 * h + u
                rows = []
                for a in range(height):
                    halves_of_k = [
                        jnp.where(masks[s], wide[pl.ds((2 * pair + s) * height + a, 8, stride=0), :], 0.0)
                        for s in range(2)
                    ]
                    rows.append(jnp.concatenate(halves_of_k, axis=1))
                left = jnp.concatenate(rows, axis=0).astype(jnp.bfloat16)
                sums = jnp.dot(left, wbuf[pair], preferred_element_type=jnp.float32)
                halves.append(sums.reshape(height, 8, 256))
            both = jnp.concatenate(halves, axis=1).astype(jnp.bfloat16)
            cross[:, pl.ds(pl.multiple_of(h * 16, 16), 16), :] = both
            return carry

        lax.fori_loop(0, PAIRS // 2, window_sums, 0, unroll=unroll_sum)

        def lag_sums(h, carry):
            first, second = cross[2 * h], cross[2 * h + 1]
            real = jnp.concatenate([first[:, :128], second[:, :128]], axis=1)
            imag = jnp.concatenate([first[:, 128:], second[:, 128:]], axis=1)
            right = jnp.concatenate([real, imag], axis=0)
            out = jnp.dot(tbuf[...], right, preferred_element_type=jnp.float32)
            out = out * (1.0 / math.sqrt(W * FB))
            lags[pl.ds(2 * h, LAG_PAD, stride=pitch), :] = out[:, :128]
            lags[pl.ds(2 * h + 1, LAG_PAD, stride=pitch), :] = out[:, 128:]
            return carry

        lax.fori_loop(0, height // 2, lag_sums, 0, unroll=unroll_lag)
        stage[...] = lags[...].reshape(LAG_PAD, pitch, 128)[:LAGS, :height].astype(jnp.bfloat16)
        at = pl.multiple_of(meta_ref[1], height)
        back = pltpu.make_async_copy(stage, out_ref.at[:, pl.ds(at, height), :], sems.at[0])
        back.start()
        back.wait()


def pair_block(choice, place, shards, right, table, out, unroll_sum=8, unroll_lag=8, pad=8):
    count = len(shards)
    height = shards[0].shape[1]
    meta = jnp.stack([choice, place]).astype(jnp.int32)
    anywhere = pl.BlockSpec(memory_space=pl.ANY)
    return pl.pallas_call(
        functools.partial(
            pair_kernel,
            count=count,
            height=height,
            unroll_sum=unroll_sum,
            unroll_lag=unroll_lag,
            pitch=height + pad,
        ),
        out_shape=jax.ShapeDtypeStruct(out.shape, out.dtype),
        grid_spec=pltpu.PrefetchScalarGridSpec(
            num_scalar_prefetch=1,
            grid=(),
            in_specs=[anywhere] * (count + 3),
            out_specs=anywhere,
            scratch_shapes=[
                pltpu.VMEM((ROWS, height, 128), jnp.bfloat16),
                pltpu.VMEM((ROWS * height, 128), jnp.float32),
                pltpu.VMEM((PAIRS, 256, 256), jnp.bfloat16),
                pltpu.VMEM((LAG_PAD, 2 * FB), jnp.bfloat16),
                pltpu.VMEM((height, FB, 256), jnp.bfloat16),
                pltpu.VMEM((LAG_PAD * (height + pad), 128), jnp.float32),
                pltpu.VMEM((LAGS, height, 128), jnp.bfloat16),
                pltpu.SemaphoreType.DMA((3,)),
            ],
        ),
        input_output_aliases={count + 3: 0},
        compiler_params=pltpu.CompilerParams(vmem_limit_bytes=60 << 20),
        cost_estimate=pl.CostEstimate(
            flops=2 * height * FB * 256 * 8 * 32 + 2 * height * 128 * 2 * FB * LAG_PAD,
            bytes_accessed=PAIRS * 256 * 256 * 2 + 2 * height * 128 * LAGS,
            transcendentals=0,
        ),
        name="pair_block",
    )(meta, *shards, right, table, out)


def make_table(band_range):
    order = jnp.arange(FB, dtype=jnp.int32)
    freq_index = (order % SEGMENTS) * ROWS + order // SEGMENTS
    lag_index = jnp.arange(LAG_PAD, dtype=jnp.int32) - LAGS // 2
    turns = jnp.mod((F0 + freq_index)[None, :] * lag_index[:, None], NFFT)
    theta = turns.astype(jnp.float32) * (2.0 * math.pi / NFFT)
    inband = ((freq_index >= band_range[0]) & (freq_index < band_range[1])).astype(jnp.float32)[None, :]
    return jnp.concatenate([inband * jnp.cos(theta), -inband * jnp.sin(theta)], axis=1).astype(jnp.bfloat16)


def relay_body(spectra, request, table):
    rows, sides = lax.axis_size("row"), lax.axis_size("side")
    axes = ("row", "plane", "side")
    row_id, plane, side = (lax.axis_index(name) for name in axes)
    width = spectra.shape[2]
    core, chip = row_id % 2, row_id // 2
    depth = plane - row_id
    devices = [(r, p, x) for r in range(rows) for p in range(rows) for x in range(sides)]

    def send(value, pairs):
        number = [tuple((r * rows + p) * sides + x for r, p, x in pair) for pair in pairs]
        return lax.ppermute(value, axes, number)

    def join(mine, sibling):
        first = jnp.where(core == 0, mine, sibling)
        second = jnp.where(core == 0, sibling, mine)
        return jnp.concatenate([first, second], axis=1)

    core_flip = [((r, p, x), (r ^ 1, p, x)) for r, p, x in devices]
    chip_flip = [((r, p, x), (r ^ 2, p, x)) for r, p, x in devices]

    shard = whiten(spectra, 1)[0]
    joined = join(shard, send(shard, core_flip))
    across = send(shard, chip_flip)
    def climb(value, d):
        return send(
            value,
            [
                ((r, p, x), (r, p + 1, x))
                for r, p, x in devices
                if p + 1 < rows and p - d + 1 >= 0 and (p - d + 1 - r) % 2 == 0
            ],
        )

    def to_row(value, d, flip_side, flip_chip):
        takers = [(r, p, x) for r, p, x in devices if p - r == d]
        return send(value, [((r ^ 2 * flip_chip, p, x ^ flip_side), (r, p, x)) for r, p, x in takers])

    after = lax.optimization_barrier
    once = climb(joined, 1)
    side_zero = to_row(joined, 0, 1, 0)
    once, table, across, kept = after((once, table, across, joined))
    twice = climb(once, 2)
    joined_across = join(across, send(across, core_flip))
    offsets = jnp.stack([2 * chip * width, 2 * (1 - chip) * width]).astype(jnp.int32)
    right, out = weights(offsets, [joined, joined_across], sides * rows * width)
    chip_one = to_row(once, 1, 0, 1)
    side_one = to_row(once, 1, 1, 0)
    both_zero = to_row(kept, 0, 1, 1)
    twice, side_zero, side_one = after((twice, side_zero, side_one))
    thrice = climb(twice, 3)
    chip_two = to_row(twice, 2, 0, 1)
    side_two = to_row(twice, 2, 1, 0)
    thrice, chip_one, both_zero, chip_two, side_two, twice, right, out = after(
        (thrice, chip_one, both_zero, chip_two, side_two, twice, right, out)
    )
    both_one = to_row(chip_one, 1, 1, 0)
    chip_three = to_row(thrice, 3, 0, 1)
    side_three = to_row(thrice, 3, 1, 0)

    by_depth = jnp.where(request == 1, depth, -1)

    def place(flip_side, flip_chip):
        return ((side ^ flip_side) * rows + 2 * (chip ^ flip_chip)) * width

    out = pair_block(by_depth, place(0, 0), [joined, once, twice, thrice], right, table, out)
    chip_three, twice, out = after((chip_three, twice, out))
    both_two = to_row(twice, 2, 1, 1)
    both_three = to_row(chip_three, 3, 1, 0)
    out = pair_block(by_depth, place(1, 0), [side_zero, side_one, side_two, side_three], right, table, out)
    out = pair_block(by_depth, place(0, 1), [joined_across, chip_one, chip_two, chip_three], right, table, out)
    return pair_block(by_depth, place(1, 1), [both_zero, both_one, both_two, both_three], right, table, out)


def gather_body(spectra, request, table):
    shard = whiten(spectra, 1)[0]
    width = shard.shape[1]
    rows = lax.axis_size("row")
    sides = lax.axis_size("side")
    column = lax.all_gather(shard, "row", axis=1, tiled=True)
    grouped = lax.all_gather(shard, ("plane", "side"), axis=0).reshape(rows, sides, ROWS, width, 128)
    moved = lax.all_to_all(grouped, "row", split_axis=0, concat_axis=0)
    block = jnp.transpose(moved, (2, 1, 0, 3, 4)).reshape(ROWS, sides * rows * width, 128)
    right, out = weights(jnp.zeros((1,), jnp.int32), [column], block.shape[1])
    group = min(64, block.shape[1])
    for at in range(0, block.shape[1], group):
        out = pair_block(request - 1, jnp.int32(at), [block[:, at : at + group]], right, table, out)
    return out


def body(spectra, pair_mask, band_range):
    rows = lax.axis_size("row")
    sides = lax.axis_size("side")
    width = spectra.shape[2]
    request = ((pair_mask[0, 0] == 1) & (lax.axis_index("plane") >= lax.axis_index("row"))).astype(jnp.int32)
    table = make_table(band_range)
    if (rows, sides) == (4, 2) and width % 32 == 0:
        out = relay_body(spectra, request, table)
    else:
        out = gather_body(spectra, request, table)
    return jnp.transpose(out, (1, 2, 0))


def solution(mesh):
    rows, cols = mesh.devices.shape
    cut = Mesh(mesh.devices.reshape(rows, rows, cols // rows), ("row", "plane", "side"))
    return jax.shard_map(
        body,
        mesh=cut,
        in_specs=(P(None, None, ("plane", "side", "row"), None), P("row", ("plane", "side")), P()),
        out_specs=P("row", ("plane", "side"), None),
        check_vma=False,
    )
```

```python
import functools
import math

import jax
import jax.numpy as jnp
from jax import lax
from jax.experimental import pallas as pl
from jax.experimental.pallas import tpu as pltpu
from jax.sharding import Mesh
from jax.sharding import PartitionSpec as P

W = 16
FB = 512
LAGS = 201
NFFT = 15000
F0 = 60
EPS = 1e-06

SEGMENTS = 4
ROWS = FB // SEGMENTS
PAIRS = ROWS // 2
LAG_PAD = 208


def whiten_kernel(*refs, width, parts):
    x_refs, whole_ref, out_refs, scratch = refs[:SEGMENTS], refs[SEGMENTS], refs[SEGMENTS + 1 : -1], refs[-1]

    def channel(c, carry):
        tiles = [x_ref[pl.ds(c, 2 * W, stride=width), :] for x_ref in x_refs]
        total = sum(v[:W] * v[:W] + v[W:] * v[W:] for v in tiles)
        power = jnp.sum(total, axis=-1, keepdims=True) * (1.0 / FB)
        scale = lax.rsqrt(power + EPS)
        scale = jnp.concatenate([scale, scale], axis=0)
        stacked = jnp.concatenate([v * scale for v in tiles], axis=0)
        scratch[pl.ds(c, ROWS, stride=width), :] = stacked.T
        return carry

    lax.fori_loop(0, width, channel, 0, unroll=2)
    step = width // parts
    full = scratch[...].reshape(ROWS, width, 128).astype(jnp.bfloat16)
    whole_ref[...] = full
    for g, out_ref in enumerate(out_refs):
        out_ref[...] = full[:, g * step : (g + 1) * step, :]


def whiten(spectra, parts):
    width = spectra.shape[2]
    widths = [width] + ([width // parts] * parts if parts > 1 else [])
    lines = 2 * W * width
    flat = spectra.reshape(lines, FB)
    return pl.pallas_call(
        functools.partial(whiten_kernel, width=width, parts=parts),
        out_shape=[jax.ShapeDtypeStruct((ROWS, n, 128), jnp.bfloat16) for n in widths],
        grid=(1,),
        in_specs=[pl.BlockSpec((lines, ROWS), functools.partial(lambda q, i: (0, q), q)) for q in range(SEGMENTS)],
        out_specs=[pl.BlockSpec((ROWS, n, 128), lambda i: (0, 0, 0)) for n in widths],
        scratch_shapes=[pltpu.VMEM((ROWS * width, 128), jnp.float32)],
        compiler_params=pltpu.CompilerParams(vmem_limit_bytes=40 << 20),
        name="whiten",
    )(*[flat] * SEGMENTS)


def weights_kernel(offset_ref, *refs, count, step):
    in_refs, out_ref, clear_ref, scratch = refs[:count], refs[count], refs[count + 1], refs[count + 2]
    clear_ref[...] = jnp.zeros_like(clear_ref)
    for i in range(count):
        at = pl.multiple_of(offset_ref[i], step)
        scratch[:, pl.ds(at, step), :] = in_refs[i][...].astype(jnp.float32)

    def row(t, carry):
        for s in range(2):
            real = scratch[2 * t + s].T
            pieces = []
            for q in range(SEGMENTS):
                lo = q * 2 * W
                pieces += [-real[lo + W : lo + 2 * W], real[lo : lo + W]]
            imag = jnp.concatenate(pieces, axis=0)
            both = jnp.concatenate([real, imag], axis=1).astype(jnp.bfloat16)
            out_ref[t, s * 128 : (s + 1) * 128, :] = both
        return carry

    lax.fori_loop(0, out_ref.shape[0], row, 0, unroll=2)


def weights(offsets, shards, height):
    count = len(shards)
    step = shards[0].shape[1]
    tiles = 4
    return pl.pallas_call(
        functools.partial(weights_kernel, count=count, step=step),
        out_shape=[
            jax.ShapeDtypeStruct((PAIRS, 256, 256), jnp.bfloat16),
            jax.ShapeDtypeStruct((LAGS, height, count * step), jnp.bfloat16),
        ],
        grid_spec=pltpu.PrefetchScalarGridSpec(
            num_scalar_prefetch=1,
            grid=(tiles,),
            in_specs=[pl.BlockSpec((ROWS // tiles, step, 128), lambda i, o: (i, 0, 0))] * count,
            out_specs=[
                pl.BlockSpec((PAIRS // tiles, 256, 256), lambda i, o: (i, 0, 0)),
                pl.BlockSpec((LAGS, height // tiles, count * step), lambda i, o: (0, i, 0)),
            ],
            scratch_shapes=[pltpu.VMEM((ROWS // tiles, count * step, 128), jnp.float32)],
        ),
        compiler_params=pltpu.CompilerParams(vmem_limit_bytes=40 << 20),
        name="weights",
    )(offsets, *shards)


def pair_kernel(meta_ref, *refs, groups, height, unroll_sum, unroll_lag, pitch):
    count = sum(groups)
    x_refs = refs[:count]
    w_ref, t_ref, _, out_ref = refs[count : count + 4]
    xbuf, wide, wbuf, tbuf, cross, lags, stage, sems = refs[count + 4 :]

    def one_group(g):
        sub = lax.broadcasted_iota(jnp.int32, (8, 128), 0)
        segment = lax.broadcasted_iota(jnp.int32, (8, 128), 1) // (2 * W)
        masks = (segment == sub, segment == sub - SEGMENTS)

        def window_sums(h, carry):
            halves = []
            for u in range(2):
                pair = 2 * h + u
                rows = []
                for a in range(height):
                    halves_of_k = [
                        jnp.where(masks[s], wide[pl.ds((2 * pair + s) * height + a, 8, stride=0), :], 0.0)
                        for s in range(2)
                    ]
                    rows.append(jnp.concatenate(halves_of_k, axis=1))
                left = jnp.concatenate(rows, axis=0).astype(jnp.bfloat16)
                sums = jnp.dot(left, wbuf[pair], preferred_element_type=jnp.float32)
                halves.append(sums.reshape(height, 8, 256))
            both = jnp.concatenate(halves, axis=1).astype(jnp.bfloat16)
            cross[:, pl.ds(pl.multiple_of(h * 16, 16), 16), :] = both
            return carry

        lax.fori_loop(0, PAIRS // 2, window_sums, 0, unroll=unroll_sum)

        def lag_sums(h, carry):
            first, second = cross[2 * h], cross[2 * h + 1]
            real = jnp.concatenate([first[:, :128], second[:, :128]], axis=1)
            imag = jnp.concatenate([first[:, 128:], second[:, 128:]], axis=1)
            right = jnp.concatenate([real, imag], axis=0)
            out = jnp.dot(tbuf[...], right, preferred_element_type=jnp.float32)
            out = out * (1.0 / math.sqrt(W * FB))
            lags[pl.ds(2 * h, LAG_PAD, stride=pitch), :] = out[:, :128]
            lags[pl.ds(2 * h + 1, LAG_PAD, stride=pitch), :] = out[:, 128:]
            return carry

        lax.fori_loop(0, height // 2, lag_sums, 0, unroll=unroll_lag)
        at = pl.multiple_of(meta_ref[1 + g], height)
        back = pltpu.make_async_copy(stage, out_ref.at[:, pl.ds(at, height), :], sems.at[0])
        if g:
            pltpu.make_async_copy(stage, out_ref.at[:, pl.ds(0, height), :], sems.at[0]).wait()
        stage[...] = lags[...].reshape(LAG_PAD, pitch, 128)[:LAGS, :height].astype(jnp.bfloat16)
        back.start()
        if g == len(groups) - 1:
            back.wait()

    @pl.when(meta_ref[0] >= 0)
    def _():
        first = 0
        for g, size in enumerate(groups):
            for i in range(size):

                @pl.when(meta_ref[0] == i)
                def _(g=g, ref=x_refs[first + i]):
                    pltpu.make_async_copy(ref, xbuf.at[g], sems.at[3 + g]).start()

            first += size
            if g == 0:
                others = [
                    pltpu.make_async_copy(w_ref, wbuf, sems.at[1]),
                    pltpu.make_async_copy(t_ref, tbuf, sems.at[2]),
                ]
                for copy in others:
                    copy.start()
        for g in range(len(groups)):
            pltpu.make_async_copy(x_refs[0], xbuf.at[g], sems.at[3 + g]).wait()
            wide[...] = xbuf[g].astype(jnp.float32).reshape(ROWS * height, 128)
            if g == 0:
                for copy in others:
                    copy.wait()
            one_group(g)


def pair_block(choice, members, right, table, out, unroll_sum=8, unroll_lag=8, pad=8):
    groups = [len(shards) for _, shards in members]
    shards = [shard for _, some in members for shard in some]
    count = len(shards)
    height = shards[0].shape[1]
    meta = jnp.stack([choice] + [place for place, _ in members]).astype(jnp.int32)
    anywhere = pl.BlockSpec(memory_space=pl.ANY)
    return pl.pallas_call(
        functools.partial(
            pair_kernel,
            groups=groups,
            height=height,
            unroll_sum=unroll_sum,
            unroll_lag=unroll_lag,
            pitch=height + pad,
        ),
        out_shape=jax.ShapeDtypeStruct(out.shape, out.dtype),
        grid_spec=pltpu.PrefetchScalarGridSpec(
            num_scalar_prefetch=1,
            grid=(),
            in_specs=[anywhere] * (count + 3),
            out_specs=anywhere,
            scratch_shapes=[
                pltpu.VMEM((len(groups), ROWS, height, 128), jnp.bfloat16),
                pltpu.VMEM((ROWS * height, 128), jnp.float32),
                pltpu.VMEM((PAIRS, 256, 256), jnp.bfloat16),
                pltpu.VMEM((LAG_PAD, 2 * FB), jnp.bfloat16),
                pltpu.VMEM((height, FB, 256), jnp.bfloat16),
                pltpu.VMEM((LAG_PAD * (height + pad), 128), jnp.float32),
                pltpu.VMEM((LAGS, height, 128), jnp.bfloat16),
                pltpu.SemaphoreType.DMA((3 + len(groups),)),
            ],
        ),
        input_output_aliases={count + 3: 0},
        compiler_params=pltpu.CompilerParams(vmem_limit_bytes=60 << 20),
        cost_estimate=pl.CostEstimate(
            flops=len(groups) * (2 * height * FB * 256 * 8 * 32 + 2 * height * 128 * 2 * FB * LAG_PAD),
            bytes_accessed=PAIRS * 256 * 256 * 2 + 2 * len(groups) * height * 128 * LAGS,
            transcendentals=0,
        ),
        name="pair_block",
    )(meta, *shards, right, table, out)


def make_table(band_range):
    order = jnp.arange(FB, dtype=jnp.int32)
    freq_index = (order % SEGMENTS) * ROWS + order // SEGMENTS
    lag_index = jnp.arange(LAG_PAD, dtype=jnp.int32) - LAGS // 2
    turns = jnp.mod((F0 + freq_index)[None, :] * lag_index[:, None], NFFT)
    theta = turns.astype(jnp.float32) * (2.0 * math.pi / NFFT)
    inband = ((freq_index >= band_range[0]) & (freq_index < band_range[1])).astype(jnp.float32)[None, :]
    return jnp.concatenate([inband * jnp.cos(theta), -inband * jnp.sin(theta)], axis=1).astype(jnp.bfloat16)


def relay_body(spectra, request, table):
    rows, sides = lax.axis_size("row"), lax.axis_size("side")
    axes = ("row", "plane", "side")
    row_id, plane, side = (lax.axis_index(name) for name in axes)
    width = spectra.shape[2]
    core, chip = row_id % 2, row_id // 2
    depth = plane - row_id
    devices = [(r, p, x) for r in range(rows) for p in range(rows) for x in range(sides)]

    def send(value, pairs):
        number = [tuple((r * rows + p) * sides + x for r, p, x in pair) for pair in pairs]
        return lax.ppermute(value, axes, number)

    def join(mine, sibling):
        first = jnp.where(core == 0, mine, sibling)
        second = jnp.where(core == 0, sibling, mine)
        return jnp.concatenate([first, second], axis=1)

    core_flip = [((r, p, x), (r ^ 1, p, x)) for r, p, x in devices]
    chip_flip = [((r, p, x), (r ^ 2, p, x)) for r, p, x in devices]

    shard = whiten(spectra, 1)[0]
    joined = join(shard, send(shard, core_flip))
    across = send(shard, chip_flip)
    def climb(value, d):
        return send(
            value,
            [
                ((r, p, x), (r, p + 1, x))
                for r, p, x in devices
                if p + 1 < rows and p - d + 1 >= 0 and (p - d + 1 - r) % 2 == 0
            ],
        )

    def to_row(value, d, flip_side, flip_chip):
        takers = [(r, p, x) for r, p, x in devices if p - r == d]
        return send(value, [((r ^ 2 * flip_chip, p, x ^ flip_side), (r, p, x)) for r, p, x in takers])

    after = lax.optimization_barrier
    once = climb(joined, 1)
    side_zero = to_row(joined, 0, 1, 0)
    once, table, across = after((once, table, across))
    twice = climb(once, 2)
    joined_across = join(across, send(across, core_flip))
    offsets = jnp.stack([2 * chip * width, 2 * (1 - chip) * width]).astype(jnp.int32)
    right, out = weights(offsets, [joined, joined_across], sides * rows * width)
    chip_one = to_row(once, 1, 0, 1)
    side_one = to_row(once, 1, 1, 0)
    twice, side_zero, side_one, joined_across = after((twice, side_zero, side_one, joined_across))
    both_zero = to_row(joined_across, 0, 1, 0)
    thrice = climb(twice, 3)
    chip_two = to_row(twice, 2, 0, 1)
    side_two = to_row(twice, 2, 1, 0)
    thrice, chip_one, both_zero, chip_two, side_two, twice, right, out = after(
        (thrice, chip_one, both_zero, chip_two, side_two, twice, right, out)
    )
    both_one = to_row(chip_one, 1, 1, 0)
    chip_three = to_row(thrice, 3, 0, 1)
    side_three = to_row(thrice, 3, 1, 0)

    by_depth = jnp.where(request == 1, depth, -1)

    def place(flip_side, flip_chip):
        return ((side ^ flip_side) * rows + 2 * (chip ^ flip_chip)) * width

    out = pair_block(by_depth, [(place(0, 0), [joined, once, twice, thrice])], right, table, out)
    chip_three, twice, out = after((chip_three, twice, out))
    both_two = to_row(twice, 2, 1, 1)
    both_three = to_row(chip_three, 3, 1, 0)
    sides_of = (place(1, 0), [side_zero, side_one, side_two, side_three])
    chips_of = (place(0, 1), [joined_across, chip_one, chip_two, chip_three])
    out = pair_block(by_depth, [sides_of, chips_of], right, table, out)
    return pair_block(by_depth, [(place(1, 1), [both_zero, both_one, both_two, both_three])], right, table, out)


def gather_body(spectra, request, table):
    shard = whiten(spectra, 1)[0]
    width = shard.shape[1]
    rows = lax.axis_size("row")
    sides = lax.axis_size("side")
    column = lax.all_gather(shard, "row", axis=1, tiled=True)
    grouped = lax.all_gather(shard, ("plane", "side"), axis=0).reshape(rows, sides, ROWS, width, 128)
    moved = lax.all_to_all(grouped, "row", split_axis=0, concat_axis=0)
    block = jnp.transpose(moved, (2, 1, 0, 3, 4)).reshape(ROWS, sides * rows * width, 128)
    right, out = weights(jnp.zeros((1,), jnp.int32), [column], block.shape[1])
    group = min(64, block.shape[1])
    for at in range(0, block.shape[1], group):
        out = pair_block(request - 1, [(jnp.int32(at), [block[:, at : at + group]])], right, table, out)
    return out


def body(spectra, pair_mask, band_range):
    rows = lax.axis_size("row")
    sides = lax.axis_size("side")
    width = spectra.shape[2]
    request = ((pair_mask[0, 0] == 1) & (lax.axis_index("plane") >= lax.axis_index("row"))).astype(jnp.int32)
    table = make_table(band_range)
    if (rows, sides) == (4, 2) and width % 32 == 0:
        out = relay_body(spectra, request, table)
    else:
        out = gather_body(spectra, request, table)
    return jnp.transpose(out, (1, 2, 0))


def solution(mesh):
    rows, cols = mesh.devices.shape
    cut = Mesh(mesh.devices.reshape(rows, rows, cols // rows), ("row", "plane", "side"))
    return jax.shard_map(
        body,
        mesh=cut,
        in_specs=(P(None, None, ("plane", "side", "row"), None), P("row", ("plane", "side")), P()),
        out_specs=P("row", ("plane", "side"), None),
        check_vma=False,
    )
```

```python
import functools
import math

import jax
import jax.numpy as jnp
from jax import lax
from jax.experimental import pallas as pl
from jax.experimental.pallas import tpu as pltpu
from jax.sharding import Mesh
from jax.sharding import PartitionSpec as P

W = 16
FB = 512
LAGS = 201
NFFT = 15000
F0 = 60
EPS = 1e-06

SEGMENTS = 4
ROWS = FB // SEGMENTS
PAIRS = ROWS // 2
LAG_PAD = 208


def whiten_kernel(*refs, width, parts):
    x_refs, whole_ref, out_refs, scratch = refs[:SEGMENTS], refs[SEGMENTS], refs[SEGMENTS + 1 : -1], refs[-1]

    def channel(c, carry):
        tiles = [x_ref[pl.ds(c, 2 * W, stride=width), :] for x_ref in x_refs]
        total = sum(v[:W] * v[:W] + v[W:] * v[W:] for v in tiles)
        power = jnp.sum(total, axis=-1, keepdims=True) * (1.0 / FB)
        scale = lax.rsqrt(power + EPS)
        scale = jnp.concatenate([scale, scale], axis=0)
        stacked = jnp.concatenate([v * scale for v in tiles], axis=0)
        scratch[pl.ds(c, ROWS, stride=width), :] = stacked.T
        return carry

    lax.fori_loop(0, width, channel, 0, unroll=2)
    step = width // parts
    full = scratch[...].reshape(ROWS, width, 128).astype(jnp.bfloat16)
    whole_ref[...] = full
    for g, out_ref in enumerate(out_refs):
        out_ref[...] = full[:, g * step : (g + 1) * step, :]


def whiten(spectra, parts):
    width = spectra.shape[2]
    widths = [width] + ([width // parts] * parts if parts > 1 else [])
    lines = 2 * W * width
    flat = spectra.reshape(lines, FB)
    return pl.pallas_call(
        functools.partial(whiten_kernel, width=width, parts=parts),
        out_shape=[jax.ShapeDtypeStruct((ROWS, n, 128), jnp.bfloat16) for n in widths],
        grid=(1,),
        in_specs=[pl.BlockSpec((lines, ROWS), functools.partial(lambda q, i: (0, q), q)) for q in range(SEGMENTS)],
        out_specs=[pl.BlockSpec((ROWS, n, 128), lambda i: (0, 0, 0)) for n in widths],
        scratch_shapes=[pltpu.VMEM((ROWS * width, 128), jnp.float32)],
        compiler_params=pltpu.CompilerParams(vmem_limit_bytes=40 << 20),
        name="whiten",
    )(*[flat] * SEGMENTS)


def weights_kernel(offset_ref, *refs, count, step):
    in_refs, out_ref, clear_ref, scratch = refs[:count], refs[count], refs[count + 1], refs[count + 2]
    clear_ref[...] = jnp.zeros_like(clear_ref)
    for i in range(count):
        at = pl.multiple_of(offset_ref[i], step)
        scratch[:, pl.ds(at, step), :] = in_refs[i][...].astype(jnp.float32)

    def row(t, carry):
        for s in range(2):
            real = scratch[2 * t + s].T
            pieces = []
            for q in range(SEGMENTS):
                lo = q * 2 * W
                pieces += [-real[lo + W : lo + 2 * W], real[lo : lo + W]]
            imag = jnp.concatenate(pieces, axis=0)
            both = jnp.concatenate([real, imag], axis=1).astype(jnp.bfloat16)
            out_ref[t, s * 128 : (s + 1) * 128, :] = both
        return carry

    lax.fori_loop(0, out_ref.shape[0], row, 0, unroll=2)


def weights(offsets, shards, height):
    count = len(shards)
    step = shards[0].shape[1]
    tiles = 4
    return pl.pallas_call(
        functools.partial(weights_kernel, count=count, step=step),
        out_shape=[
            jax.ShapeDtypeStruct((PAIRS, 256, 256), jnp.bfloat16),
            jax.ShapeDtypeStruct((LAGS, height, count * step), jnp.bfloat16),
        ],
        grid_spec=pltpu.PrefetchScalarGridSpec(
            num_scalar_prefetch=1,
            grid=(tiles,),
            in_specs=[pl.BlockSpec((ROWS // tiles, step, 128), lambda i, o: (i, 0, 0))] * count,
            out_specs=[
                pl.BlockSpec((PAIRS // tiles, 256, 256), lambda i, o: (i, 0, 0)),
                pl.BlockSpec((LAGS, height // tiles, count * step), lambda i, o: (0, i, 0)),
            ],
            scratch_shapes=[pltpu.VMEM((ROWS // tiles, count * step, 128), jnp.float32)],
        ),
        compiler_params=pltpu.CompilerParams(vmem_limit_bytes=40 << 20),
        name="weights",
    )(offsets, *shards)


def pair_kernel(meta_ref, *refs, groups, height, unroll_sum, unroll_lag, pitch):
    count = sum(groups)
    x_refs = refs[:count]
    w_ref, t_ref, _, out_ref = refs[count : count + 4]
    xbuf, wide, wbuf, tbuf, cross, lags, stage, sems = refs[count + 4 :]

    def one_group(g):
        sub = lax.broadcasted_iota(jnp.int32, (8, 128), 0)
        segment = lax.broadcasted_iota(jnp.int32, (8, 128), 1) // (2 * W)
        masks = (segment == sub, segment == sub - SEGMENTS)

        def window_sums(h, carry):
            halves = []
            for u in range(2):
                pair = 2 * h + u
                rows = []
                for a in range(height):
                    halves_of_k = [
                        jnp.where(masks[s], wide[pl.ds((2 * pair + s) * height + a, 8, stride=0), :], 0.0)
                        for s in range(2)
                    ]
                    rows.append(jnp.concatenate(halves_of_k, axis=1))
                left = jnp.concatenate(rows, axis=0).astype(jnp.bfloat16)
                sums = jnp.dot(left, wbuf[pair], preferred_element_type=jnp.float32)
                halves.append(sums.reshape(height, 8, 256))
            both = jnp.concatenate(halves, axis=1).astype(jnp.bfloat16)
            cross[:, pl.ds(pl.multiple_of(h * 16, 16), 16), :] = both
            return carry

        lax.fori_loop(0, PAIRS // 2, window_sums, 0, unroll=unroll_sum)

        def lag_sums(h, carry):
            first, second = cross[2 * h], cross[2 * h + 1]
            real = jnp.concatenate([first[:, :128], second[:, :128]], axis=1)
            imag = jnp.concatenate([first[:, 128:], second[:, 128:]], axis=1)
            right = jnp.concatenate([real, imag], axis=0)
            out = jnp.dot(tbuf[...], right, preferred_element_type=jnp.float32)
            out = out * (1.0 / math.sqrt(W * FB))
            lags[pl.ds(2 * h, LAG_PAD, stride=pitch), :] = out[:, :128]
            lags[pl.ds(2 * h + 1, LAG_PAD, stride=pitch), :] = out[:, 128:]
            return carry

        lax.fori_loop(0, height // 2, lag_sums, 0, unroll=unroll_lag)
        at = pl.multiple_of(meta_ref[1 + g], height)
        back = pltpu.make_async_copy(stage, out_ref.at[:, pl.ds(at, height), :], sems.at[0])
        if g:
            pltpu.make_async_copy(stage, out_ref.at[:, pl.ds(0, height), :], sems.at[0]).wait()
        stage[...] = lags[...].reshape(LAG_PAD, pitch, 128)[:LAGS, :height].astype(jnp.bfloat16)
        back.start()
        if g == len(groups) - 1:
            back.wait()

    @pl.when(meta_ref[0] >= 0)
    def _():
        first = 0
        for g, size in enumerate(groups):
            for i in range(size):

                @pl.when(meta_ref[0] == i)
                def _(g=g, ref=x_refs[first + i]):
                    pltpu.make_async_copy(ref, xbuf.at[g], sems.at[3 + g]).start()

            first += size
            if g == 0:
                others = [
                    pltpu.make_async_copy(w_ref, wbuf, sems.at[1]),
                    pltpu.make_async_copy(t_ref, tbuf, sems.at[2]),
                ]
                for copy in others:
                    copy.start()
        for g in range(len(groups)):
            pltpu.make_async_copy(x_refs[0], xbuf.at[g], sems.at[3 + g]).wait()
            wide[...] = xbuf[g].astype(jnp.float32).reshape(ROWS * height, 128)
            if g == 0:
                for copy in others:
                    copy.wait()
            one_group(g)


def pair_block(choice, members, right, table, out, unroll_sum=8, unroll_lag=8, pad=8):
    groups = [len(shards) for _, shards in members]
    shards = [shard for _, some in members for shard in some]
    count = len(shards)
    height = shards[0].shape[1]
    meta = jnp.stack([choice] + [place for place, _ in members]).astype(jnp.int32)
    anywhere = pl.BlockSpec(memory_space=pl.ANY)
    return pl.pallas_call(
        functools.partial(
            pair_kernel,
            groups=groups,
            height=height,
            unroll_sum=unroll_sum,
            unroll_lag=unroll_lag,
            pitch=height + pad,
        ),
        out_shape=jax.ShapeDtypeStruct(out.shape, out.dtype),
        grid_spec=pltpu.PrefetchScalarGridSpec(
            num_scalar_prefetch=1,
            grid=(),
            in_specs=[anywhere] * (count + 3),
            out_specs=anywhere,
            scratch_shapes=[
                pltpu.VMEM((len(groups), ROWS, height, 128), jnp.bfloat16),
                pltpu.VMEM((ROWS * height, 128), jnp.float32),
                pltpu.VMEM((PAIRS, 256, 256), jnp.bfloat16),
                pltpu.VMEM((LAG_PAD, 2 * FB), jnp.bfloat16),
                pltpu.VMEM((height, FB, 256), jnp.bfloat16),
                pltpu.VMEM((LAG_PAD * (height + pad), 128), jnp.float32),
                pltpu.VMEM((LAGS, height, 128), jnp.bfloat16),
                pltpu.SemaphoreType.DMA((3 + len(groups),)),
            ],
        ),
        input_output_aliases={count + 3: 0},
        compiler_params=pltpu.CompilerParams(vmem_limit_bytes=60 << 20),
        cost_estimate=pl.CostEstimate(
            flops=len(groups) * (2 * height * FB * 256 * 8 * 32 + 2 * height * 128 * 2 * FB * LAG_PAD),
            bytes_accessed=PAIRS * 256 * 256 * 2 + 2 * len(groups) * height * 128 * LAGS,
            transcendentals=0,
        ),
        name="pair_block",
    )(meta, *shards, right, table, out)


def make_table(band_range):
    order = jnp.arange(FB, dtype=jnp.int32)
    freq_index = (order % SEGMENTS) * ROWS + order // SEGMENTS
    lag_index = jnp.arange(LAG_PAD, dtype=jnp.int32) - LAGS // 2
    turns = jnp.mod((F0 + freq_index)[None, :] * lag_index[:, None], NFFT)
    theta = turns.astype(jnp.float32) * (2.0 * math.pi / NFFT)
    inband = ((freq_index >= band_range[0]) & (freq_index < band_range[1])).astype(jnp.float32)[None, :]
    return jnp.concatenate([inband * jnp.cos(theta), -inband * jnp.sin(theta)], axis=1).astype(jnp.bfloat16)


def relay_body(spectra, request, table):
    rows, sides = lax.axis_size("row"), lax.axis_size("side")
    axes = ("row", "plane", "side")
    row_id, plane, side = (lax.axis_index(name) for name in axes)
    width = spectra.shape[2]
    core, chip = row_id % 2, row_id // 2
    depth = plane - row_id
    devices = [(r, p, x) for r in range(rows) for p in range(rows) for x in range(sides)]

    def send(value, pairs):
        number = [tuple((r * rows + p) * sides + x for r, p, x in pair) for pair in pairs]
        return lax.ppermute(value, axes, number)

    def join(mine, sibling):
        first = jnp.where(core == 0, mine, sibling)
        second = jnp.where(core == 0, sibling, mine)
        return jnp.concatenate([first, second], axis=1)

    core_flip = [((r, p, x), (r ^ 1, p, x)) for r, p, x in devices]
    chip_flip = [((r, p, x), (r ^ 2, p, x)) for r, p, x in devices]

    shard = whiten(spectra, 1)[0]
    joined = join(shard, send(shard, core_flip))
    across = send(shard, chip_flip)
    def climb(value, d):
        return send(
            value,
            [
                ((r, p, x), (r, p + 1, x))
                for r, p, x in devices
                if p + 1 < rows and p - d + 1 >= 0 and (p - d + 1 - r) % 2 == 0
            ],
        )

    def to_row(value, d, flip_side, flip_chip):
        takers = [(r, p, x) for r, p, x in devices if p - r == d]
        return send(value, [((r ^ 2 * flip_chip, p, x ^ flip_side), (r, p, x)) for r, p, x in takers])

    after = lax.optimization_barrier
    once = climb(joined, 1)
    side_zero = to_row(joined, 0, 1, 0)
    once, table, across = after((once, table, across))
    twice = climb(once, 2)
    joined_across = join(across, send(across, core_flip))
    offsets = jnp.stack([2 * chip * width, 2 * (1 - chip) * width]).astype(jnp.int32)
    right, out = weights(offsets, [joined, joined_across], sides * rows * width)
    chip_one = to_row(once, 1, 0, 1)
    side_one = to_row(once, 1, 1, 0)
    twice, side_zero, side_one, joined_across = after((twice, side_zero, side_one, joined_across))
    both_zero = to_row(joined_across, 0, 1, 0)
    thrice = climb(twice, 3)
    chip_two = to_row(twice, 2, 0, 1)
    side_two = to_row(twice, 2, 1, 0)
    thrice, chip_one, both_zero, chip_two, side_two, right, out = after(
        (thrice, chip_one, both_zero, chip_two, side_two, right, out)
    )
    both_one = to_row(chip_one, 1, 1, 0)
    chip_three = to_row(thrice, 3, 0, 1)
    both_three = to_row(thrice, 3, 1, 1)
    side_three = to_row(thrice, 3, 1, 0)
    both_two = to_row(chip_two, 2, 1, 0)

    by_depth = jnp.where(request == 1, depth, -1)

    def place(flip_side, flip_chip):
        return ((side ^ flip_side) * rows + 2 * (chip ^ flip_chip)) * width

    own_of = (place(0, 0), [joined, once, twice, thrice])
    chips_of = (place(0, 1), [joined_across, chip_one, chip_two, chip_three])
    sides_of = (place(1, 0), [side_zero, side_one, side_two, side_three])
    boths_of = (place(1, 1), [both_zero, both_one, both_two, both_three])
    for members in ([own_of], [chips_of], [sides_of, boths_of]):
        out = pair_block(by_depth, members, right, table, out)
    return out


def gather_body(spectra, request, table):
    shard = whiten(spectra, 1)[0]
    width = shard.shape[1]
    rows = lax.axis_size("row")
    sides = lax.axis_size("side")
    column = lax.all_gather(shard, "row", axis=1, tiled=True)
    grouped = lax.all_gather(shard, ("plane", "side"), axis=0).reshape(rows, sides, ROWS, width, 128)
    moved = lax.all_to_all(grouped, "row", split_axis=0, concat_axis=0)
    block = jnp.transpose(moved, (2, 1, 0, 3, 4)).reshape(ROWS, sides * rows * width, 128)
    right, out = weights(jnp.zeros((1,), jnp.int32), [column], block.shape[1])
    group = min(64, block.shape[1])
    for at in range(0, block.shape[1], group):
        out = pair_block(request - 1, [(jnp.int32(at), [block[:, at : at + group]])], right, table, out)
    return out


def body(spectra, pair_mask, band_range):
    rows = lax.axis_size("row")
    sides = lax.axis_size("side")
    width = spectra.shape[2]
    request = ((pair_mask[0, 0] == 1) & (lax.axis_index("plane") >= lax.axis_index("row"))).astype(jnp.int32)
    table = make_table(band_range)
    if (rows, sides) == (4, 2) and width % 32 == 0:
        out = relay_body(spectra, request, table)
    else:
        out = gather_body(spectra, request, table)
    return jnp.transpose(out, (1, 2, 0))


def solution(mesh):
    rows, cols = mesh.devices.shape
    cut = Mesh(mesh.devices.reshape(rows, rows, cols // rows), ("row", "plane", "side"))
    return jax.shard_map(
        body,
        mesh=cut,
        in_specs=(P(None, None, ("plane", "side", "row"), None), P("row", ("plane", "side")), P()),
        out_specs=P("row", ("plane", "side"), None),
        check_vma=False,
    )
```

```python
import functools
import math

import jax
import jax.numpy as jnp
from jax import lax
from jax.experimental import pallas as pl
from jax.experimental.pallas import tpu as pltpu
from jax.sharding import Mesh
from jax.sharding import PartitionSpec as P

W = 16
FB = 512
LAGS = 201
NFFT = 15000
F0 = 60
EPS = 1e-06

SEGMENTS = 4
ROWS = FB // SEGMENTS
PAIRS = ROWS // 2
LAG_PAD = 208


def whiten_kernel(*refs, width, parts):
    x_refs, whole_ref, out_refs, scratch = refs[:SEGMENTS], refs[SEGMENTS], refs[SEGMENTS + 1 : -1], refs[-1]

    def channel(c, carry):
        tiles = [x_ref[pl.ds(c, 2 * W, stride=width), :] for x_ref in x_refs]
        total = sum(v[:W] * v[:W] + v[W:] * v[W:] for v in tiles)
        power = jnp.sum(total, axis=-1, keepdims=True) * (1.0 / FB)
        scale = lax.rsqrt(power + EPS)
        scale = jnp.concatenate([scale, scale], axis=0)
        stacked = jnp.concatenate([v * scale for v in tiles], axis=0)
        scratch[pl.ds(c, ROWS, stride=width), :] = stacked.T
        return carry

    lax.fori_loop(0, width, channel, 0, unroll=2)
    step = width // parts
    full = scratch[...].reshape(ROWS, width, 128).astype(jnp.bfloat16)
    whole_ref[...] = full
    for g, out_ref in enumerate(out_refs):
        out_ref[...] = full[:, g * step : (g + 1) * step, :]


def whiten(spectra, parts):
    width = spectra.shape[2]
    widths = [width] + ([width // parts] * parts if parts > 1 else [])
    lines = 2 * W * width
    flat = spectra.reshape(lines, FB)
    return pl.pallas_call(
        functools.partial(whiten_kernel, width=width, parts=parts),
        out_shape=[jax.ShapeDtypeStruct((ROWS, n, 128), jnp.bfloat16) for n in widths],
        grid=(1,),
        in_specs=[pl.BlockSpec((lines, ROWS), functools.partial(lambda q, i: (0, q), q)) for q in range(SEGMENTS)],
        out_specs=[pl.BlockSpec((ROWS, n, 128), lambda i: (0, 0, 0)) for n in widths],
        scratch_shapes=[pltpu.VMEM((ROWS * width, 128), jnp.float32)],
        compiler_params=pltpu.CompilerParams(vmem_limit_bytes=40 << 20),
        name="whiten",
    )(*[flat] * SEGMENTS)


def weights_kernel(offset_ref, *refs, count, step):
    in_refs, out_ref, clear_ref, scratch = refs[:count], refs[count], refs[count + 1], refs[count + 2]
    clear_ref[...] = jnp.zeros_like(clear_ref)
    for i in range(count):
        at = pl.multiple_of(offset_ref[i], step)
        scratch[:, pl.ds(at, step), :] = in_refs[i][...].astype(jnp.float32)

    def row(t, carry):
        for s in range(2):
            real = scratch[2 * t + s].T
            pieces = []
            for q in range(SEGMENTS):
                lo = q * 2 * W
                pieces += [-real[lo + W : lo + 2 * W], real[lo : lo + W]]
            imag = jnp.concatenate(pieces, axis=0)
            both = jnp.concatenate([real, imag], axis=1).astype(jnp.bfloat16)
            out_ref[t, s * 128 : (s + 1) * 128, :] = both
        return carry

    lax.fori_loop(0, out_ref.shape[0], row, 0, unroll=2)


def weights(offsets, shards, height):
    count = len(shards)
    step = shards[0].shape[1]
    tiles = 4
    return pl.pallas_call(
        functools.partial(weights_kernel, count=count, step=step),
        out_shape=[
            jax.ShapeDtypeStruct((PAIRS, 256, 256), jnp.bfloat16),
            jax.ShapeDtypeStruct((LAGS, height, count * step), jnp.bfloat16),
        ],
        grid_spec=pltpu.PrefetchScalarGridSpec(
            num_scalar_prefetch=1,
            grid=(tiles,),
            in_specs=[pl.BlockSpec((ROWS // tiles, step, 128), lambda i, o: (i, 0, 0))] * count,
            out_specs=[
                pl.BlockSpec((PAIRS // tiles, 256, 256), lambda i, o: (i, 0, 0)),
                pl.BlockSpec((LAGS, height // tiles, count * step), lambda i, o: (0, i, 0)),
            ],
            scratch_shapes=[pltpu.VMEM((ROWS // tiles, count * step, 128), jnp.float32)],
        ),
        compiler_params=pltpu.CompilerParams(vmem_limit_bytes=40 << 20),
        name="weights",
    )(offsets, *shards)


def pair_kernel(meta_ref, *refs, groups, height, unroll_sum, unroll_lag, pitch):
    count = sum(groups)
    x_refs = refs[:count]
    w_ref, t_ref, _, out_ref = refs[count : count + 4]
    xbuf, wide, wbuf, tbuf, cross, lags, stage, sems = refs[count + 4 :]
    cut = 2 * unroll_sum

    def one_group(g):
        sub = lax.broadcasted_iota(jnp.int32, (8, 128), 0)
        segment = lax.broadcasted_iota(jnp.int32, (8, 128), 1) // (2 * W)
        masks = (segment == sub, segment == sub - SEGMENTS)

        def window_sums(h, carry):
            halves = []
            for u in range(2):
                pair = 2 * h + u
                rows = []
                for a in range(height):
                    halves_of_k = [
                        jnp.where(masks[s], wide[pl.ds((2 * pair + s) * height + a, 8, stride=0), :], 0.0)
                        for s in range(2)
                    ]
                    rows.append(jnp.concatenate(halves_of_k, axis=1))
                left = jnp.concatenate(rows, axis=0).astype(jnp.bfloat16)
                sums = jnp.dot(left, wbuf[pair], preferred_element_type=jnp.float32)
                halves.append(sums.reshape(height, 8, 256))
            both = jnp.concatenate(halves, axis=1).astype(jnp.bfloat16)
            cross[:, pl.ds(pl.multiple_of(h * 16, 16), 16), :] = both
            return carry

        def slice_sums(j, carry):
            if g == 0:
                pltpu.make_async_copy(w_ref.at[pl.ds(0, cut)], wbuf.at[pl.ds(0, cut)], sems.at[2 + len(groups) + j]).wait()
            for v in range(unroll_sum):
                window_sums(j * unroll_sum + v, 0)
            return carry

        lax.fori_loop(0, PAIRS // (2 * unroll_sum), slice_sums, 0)

        if g == 0:
            pltpu.make_async_copy(t_ref, tbuf, sems.at[1]).wait()

        def lag_sums(h, carry):
            first, second = cross[2 * h], cross[2 * h + 1]
            real = jnp.concatenate([first[:, :128], second[:, :128]], axis=1)
            imag = jnp.concatenate([first[:, 128:], second[:, 128:]], axis=1)
            right = jnp.concatenate([real, imag], axis=0)
            out = jnp.dot(tbuf[...], right, preferred_element_type=jnp.float32)
            out = out * (1.0 / math.sqrt(W * FB))
            lags[pl.ds(2 * h, LAG_PAD, stride=pitch), :] = out[:, :128]
            lags[pl.ds(2 * h + 1, LAG_PAD, stride=pitch), :] = out[:, 128:]
            return carry

        lax.fori_loop(0, height // 2, lag_sums, 0, unroll=unroll_lag)
        at = pl.multiple_of(meta_ref[1 + g], height)
        back = pltpu.make_async_copy(stage, out_ref.at[:, pl.ds(at, height), :], sems.at[0])
        if g:
            pltpu.make_async_copy(stage, out_ref.at[:, pl.ds(0, height), :], sems.at[0]).wait()
        stage[...] = lags[...].reshape(LAG_PAD, pitch, 128)[:LAGS, :height].astype(jnp.bfloat16)
        back.start()
        if g == len(groups) - 1:
            back.wait()

    @pl.when(meta_ref[0] >= 0)
    def _():
        first = 0
        for g, size in enumerate(groups):
            for i in range(size):

                @pl.when(meta_ref[0] == i)
                def _(g=g, ref=x_refs[first + i]):
                    pltpu.make_async_copy(ref, xbuf.at[g], sems.at[2 + g]).start()

            first += size
            if g == 0:
                for j in range(PAIRS // cut):
                    at = pl.ds(j * cut, cut)
                    pltpu.make_async_copy(w_ref.at[at], wbuf.at[at], sems.at[2 + len(groups) + j]).start()
                pltpu.make_async_copy(t_ref, tbuf, sems.at[1]).start()
        for g in range(len(groups)):
            pltpu.make_async_copy(x_refs[0], xbuf.at[g], sems.at[2 + g]).wait()
            wide[...] = xbuf[g].astype(jnp.float32).reshape(ROWS * height, 128)
            one_group(g)


def pair_block(choice, members, right, table, out, unroll_sum=8, unroll_lag=8, pad=8):
    groups = [len(shards) for _, shards in members]
    shards = [shard for _, some in members for shard in some]
    count = len(shards)
    height = shards[0].shape[1]
    meta = jnp.stack([choice] + [place for place, _ in members]).astype(jnp.int32)
    anywhere = pl.BlockSpec(memory_space=pl.ANY)
    return pl.pallas_call(
        functools.partial(
            pair_kernel,
            groups=groups,
            height=height,
            unroll_sum=unroll_sum,
            unroll_lag=unroll_lag,
            pitch=height + pad,
        ),
        out_shape=jax.ShapeDtypeStruct(out.shape, out.dtype),
        grid_spec=pltpu.PrefetchScalarGridSpec(
            num_scalar_prefetch=1,
            grid=(),
            in_specs=[anywhere] * (count + 3),
            out_specs=anywhere,
            scratch_shapes=[
                pltpu.VMEM((len(groups), ROWS, height, 128), jnp.bfloat16),
                pltpu.VMEM((ROWS * height, 128), jnp.float32),
                pltpu.VMEM((PAIRS, 256, 256), jnp.bfloat16),
                pltpu.VMEM((LAG_PAD, 2 * FB), jnp.bfloat16),
                pltpu.VMEM((height, FB, 256), jnp.bfloat16),
                pltpu.VMEM((LAG_PAD * (height + pad), 128), jnp.float32),
                pltpu.VMEM((LAGS, height, 128), jnp.bfloat16),
                pltpu.SemaphoreType.DMA((2 + len(groups) + PAIRS // (2 * unroll_sum),)),
            ],
        ),
        input_output_aliases={count + 3: 0},
        compiler_params=pltpu.CompilerParams(vmem_limit_bytes=60 << 20),
        cost_estimate=pl.CostEstimate(
            flops=len(groups) * (2 * height * FB * 256 * 8 * 32 + 2 * height * 128 * 2 * FB * LAG_PAD),
            bytes_accessed=PAIRS * 256 * 256 * 2 + 2 * len(groups) * height * 128 * LAGS,
            transcendentals=0,
        ),
        name="pair_block",
    )(meta, *shards, right, table, out)


def make_table(band_range):
    order = jnp.arange(FB, dtype=jnp.int32)
    freq_index = (order % SEGMENTS) * ROWS + order // SEGMENTS
    lag_index = jnp.arange(LAG_PAD, dtype=jnp.int32) - LAGS // 2
    turns = jnp.mod((F0 + freq_index)[None, :] * lag_index[:, None], NFFT)
    theta = turns.astype(jnp.float32) * (2.0 * math.pi / NFFT)
    inband = ((freq_index >= band_range[0]) & (freq_index < band_range[1])).astype(jnp.float32)[None, :]
    return jnp.concatenate([inband * jnp.cos(theta), -inband * jnp.sin(theta)], axis=1).astype(jnp.bfloat16)


def relay_body(spectra, request, table):
    rows, sides = lax.axis_size("row"), lax.axis_size("side")
    axes = ("row", "plane", "side")
    row_id, plane, side = (lax.axis_index(name) for name in axes)
    width = spectra.shape[2]
    core, chip = row_id % 2, row_id // 2
    depth = plane - row_id
    devices = [(r, p, x) for r in range(rows) for p in range(rows) for x in range(sides)]

    def send(value, pairs):
        number = [tuple((r * rows + p) * sides + x for r, p, x in pair) for pair in pairs]
        return lax.ppermute(value, axes, number)

    def join(mine, sibling):
        first = jnp.where(core == 0, mine, sibling)
        second = jnp.where(core == 0, sibling, mine)
        return jnp.concatenate([first, second], axis=1)

    core_flip = [((r, p, x), (r ^ 1, p, x)) for r, p, x in devices]
    chip_flip = [((r, p, x), (r ^ 2, p, x)) for r, p, x in devices]

    shard = whiten(spectra, 1)[0]
    joined = join(shard, send(shard, core_flip))
    across = send(shard, chip_flip)
    def climb(value, d):
        return send(
            value,
            [
                ((r, p, x), (r, p + 1, x))
                for r, p, x in devices
                if p + 1 < rows and p - d + 1 >= 0 and (p - d + 1 - r) % 2 == 0
            ],
        )

    def to_row(value, d, flip_side, flip_chip):
        takers = [(r, p, x) for r, p, x in devices if p - r == d]
        return send(value, [((r ^ 2 * flip_chip, p, x ^ flip_side), (r, p, x)) for r, p, x in takers])

    after = lax.optimization_barrier
    once = climb(joined, 1)
    side_zero = to_row(joined, 0, 1, 0)
    once, table, across = after((once, table, across))
    twice = climb(once, 2)
    joined_across = join(across, send(across, core_flip))
    offsets = jnp.stack([2 * chip * width, 2 * (1 - chip) * width]).astype(jnp.int32)
    right, out = weights(offsets, [joined, joined_across], sides * rows * width)
    chip_one = to_row(once, 1, 0, 1)
    side_one = to_row(once, 1, 1, 0)
    twice, side_zero, side_one, chip_one, joined_across = after((twice, side_zero, side_one, chip_one, joined_across))
    both_one = to_row(chip_one, 1, 1, 0)
    thrice = climb(twice, 3)
    both_zero = to_row(joined_across, 0, 1, 0)
    chip_two = to_row(twice, 2, 0, 1)
    side_two = to_row(twice, 2, 1, 0)
    both_zero, both_one, thrice, chip_two, side_two, right, out = after(
        (both_zero, both_one, thrice, chip_two, side_two, right, out)
    )
    chip_three = to_row(thrice, 3, 0, 1)
    both_three = to_row(thrice, 3, 1, 1)
    side_three = to_row(thrice, 3, 1, 0)
    both_two = to_row(chip_two, 2, 1, 0)

    by_depth = jnp.where(request == 1, depth, -1)

    def place(flip_side, flip_chip):
        return ((side ^ flip_side) * rows + 2 * (chip ^ flip_chip)) * width

    own_of = (place(0, 0), [joined, once, twice, thrice])
    chips_of = (place(0, 1), [joined_across, chip_one, chip_two, chip_three])
    sides_of = (place(1, 0), [side_zero, side_one, side_two, side_three])
    boths_of = (place(1, 1), [both_zero, both_one, both_two, both_three])
    for members in ([own_of], [chips_of], [sides_of, boths_of]):
        out = pair_block(by_depth, members, right, table, out)
    return out


def gather_body(spectra, request, table):
    shard = whiten(spectra, 1)[0]
    width = shard.shape[1]
    rows = lax.axis_size("row")
    sides = lax.axis_size("side")
    column = lax.all_gather(shard, "row", axis=1, tiled=True)
    grouped = lax.all_gather(shard, ("plane", "side"), axis=0).reshape(rows, sides, ROWS, width, 128)
    moved = lax.all_to_all(grouped, "row", split_axis=0, concat_axis=0)
    block = jnp.transpose(moved, (2, 1, 0, 3, 4)).reshape(ROWS, sides * rows * width, 128)
    right, out = weights(jnp.zeros((1,), jnp.int32), [column], block.shape[1])
    group = min(64, block.shape[1])
    for at in range(0, block.shape[1], group):
        out = pair_block(request - 1, [(jnp.int32(at), [block[:, at : at + group]])], right, table, out)
    return out


def body(spectra, pair_mask, band_range):
    rows = lax.axis_size("row")
    sides = lax.axis_size("side")
    width = spectra.shape[2]
    request = ((pair_mask[0, 0] == 1) & (lax.axis_index("plane") >= lax.axis_index("row"))).astype(jnp.int32)
    table = make_table(band_range)
    if (rows, sides) == (4, 2) and width % 32 == 0:
        out = relay_body(spectra, request, table)
    else:
        out = gather_body(spectra, request, table)
    return jnp.transpose(out, (1, 2, 0))


def solution(mesh):
    rows, cols = mesh.devices.shape
    cut = Mesh(mesh.devices.reshape(rows, rows, cols // rows), ("row", "plane", "side"))
    return jax.shard_map(
        body,
        mesh=cut,
        in_specs=(P(None, None, ("plane", "side", "row"), None), P("row", ("plane", "side")), P()),
        out_specs=P("row", ("plane", "side"), None),
        check_vma=False,
    )
```

```python
import functools
import math

import jax
import jax.numpy as jnp
from jax import lax
from jax.experimental import pallas as pl
from jax.experimental.pallas import tpu as pltpu
from jax.sharding import Mesh
from jax.sharding import PartitionSpec as P

W = 16
FB = 512
LAGS = 201
NFFT = 15000
F0 = 60
EPS = 1e-06

SEGMENTS = 4
ROWS = FB // SEGMENTS
PAIRS = ROWS // 2
LAG_PAD = 208


def whiten_kernel(*refs, width, parts):
    x_refs, whole_ref, out_refs, scratch = refs[:SEGMENTS], refs[SEGMENTS], refs[SEGMENTS + 1 : -1], refs[-1]

    def channel(c, carry):
        tiles = [x_ref[pl.ds(c, 2 * W, stride=width), :] for x_ref in x_refs]
        total = sum(v[:W] * v[:W] + v[W:] * v[W:] for v in tiles)
        power = jnp.sum(total, axis=-1, keepdims=True) * (1.0 / FB)
        scale = lax.rsqrt(power + EPS)
        scale = jnp.concatenate([scale, scale], axis=0)
        stacked = jnp.concatenate([v * scale for v in tiles], axis=0)
        scratch[pl.ds(c, ROWS, stride=width), :] = stacked.T
        return carry

    lax.fori_loop(0, width, channel, 0, unroll=2)
    step = width // parts
    full = scratch[...].reshape(ROWS, width, 128).astype(jnp.bfloat16)
    whole_ref[...] = full
    for g, out_ref in enumerate(out_refs):
        out_ref[...] = full[:, g * step : (g + 1) * step, :]


def whiten(spectra, parts):
    width = spectra.shape[2]
    widths = [width] + ([width // parts] * parts if parts > 1 else [])
    lines = 2 * W * width
    flat = spectra.reshape(lines, FB)
    return pl.pallas_call(
        functools.partial(whiten_kernel, width=width, parts=parts),
        out_shape=[jax.ShapeDtypeStruct((ROWS, n, 128), jnp.bfloat16) for n in widths],
        grid=(1,),
        in_specs=[pl.BlockSpec((lines, ROWS), functools.partial(lambda q, i: (0, q), q)) for q in range(SEGMENTS)],
        out_specs=[pl.BlockSpec((ROWS, n, 128), lambda i: (0, 0, 0)) for n in widths],
        scratch_shapes=[pltpu.VMEM((ROWS * width, 128), jnp.float32)],
        compiler_params=pltpu.CompilerParams(vmem_limit_bytes=40 << 20),
        name="whiten",
    )(*[flat] * SEGMENTS)


def weights_kernel(offset_ref, *refs, count, step):
    in_refs, out_ref, clear_ref, scratch = refs[:count], refs[count], refs[count + 1], refs[count + 2]
    clear_ref[...] = jnp.zeros_like(clear_ref)
    for i in range(count):
        at = pl.multiple_of(offset_ref[i], step)
        scratch[:, pl.ds(at, step), :] = in_refs[i][...].astype(jnp.float32)

    def row(t, carry):
        for s in range(2):
            real = scratch[2 * t + s].T
            pieces = []
            for q in range(SEGMENTS):
                lo = q * 2 * W
                pieces += [-real[lo + W : lo + 2 * W], real[lo : lo + W]]
            imag = jnp.concatenate(pieces, axis=0)
            both = jnp.concatenate([real, imag], axis=1).astype(jnp.bfloat16)
            out_ref[t, s * 128 : (s + 1) * 128, :] = both
        return carry

    lax.fori_loop(0, out_ref.shape[0], row, 0, unroll=2)


def weights(offsets, shards, height):
    count = len(shards)
    step = shards[0].shape[1]
    tiles = 4
    return pl.pallas_call(
        functools.partial(weights_kernel, count=count, step=step),
        out_shape=[
            jax.ShapeDtypeStruct((PAIRS, 256, 256), jnp.bfloat16),
            jax.ShapeDtypeStruct((LAGS, height, count * step), jnp.bfloat16),
        ],
        grid_spec=pltpu.PrefetchScalarGridSpec(
            num_scalar_prefetch=1,
            grid=(tiles,),
            in_specs=[pl.BlockSpec((ROWS // tiles, step, 128), lambda i, o: (i, 0, 0))] * count,
            out_specs=[
                pl.BlockSpec((PAIRS // tiles, 256, 256), lambda i, o: (i, 0, 0)),
                pl.BlockSpec((LAGS, height // tiles, count * step), lambda i, o: (0, i, 0)),
            ],
            scratch_shapes=[pltpu.VMEM((ROWS // tiles, count * step, 128), jnp.float32)],
        ),
        compiler_params=pltpu.CompilerParams(vmem_limit_bytes=40 << 20),
        name="weights",
    )(offsets, *shards)


def pair_kernel(meta_ref, *refs, groups, height, unroll_sum, unroll_lag, pitch):
    count = sum(groups)
    x_refs = refs[:count]
    w_ref, t_ref, _, out_ref = refs[count : count + 4]
    xbuf, wide, wbuf, tbuf, cross, lags, stage, sems = refs[count + 4 :]
    cut = 2 * unroll_sum

    def one_group(g):
        sub = lax.broadcasted_iota(jnp.int32, (8, 128), 0)
        segment = lax.broadcasted_iota(jnp.int32, (8, 128), 1) // (2 * W)
        masks = (segment == sub, segment == sub - SEGMENTS)

        def window_sums(h, carry):
            halves = []
            for u in range(2):
                pair = 2 * h + u
                rows = []
                for a in range(height):
                    halves_of_k = [
                        jnp.where(masks[s], wide[pl.ds((2 * pair + s) * height + a, 8, stride=0), :], 0.0)
                        for s in range(2)
                    ]
                    rows.append(jnp.concatenate(halves_of_k, axis=1))
                left = jnp.concatenate(rows, axis=0).astype(jnp.bfloat16)
                sums = jnp.dot(left, wbuf[pair], preferred_element_type=jnp.float32)
                halves.append(sums.reshape(height, 8, 256))
            both = jnp.concatenate(halves, axis=1).astype(jnp.bfloat16)
            cross[:, pl.ds(pl.multiple_of(h * 16, 16), 16), :] = both
            return carry

        def slice_sums(j, carry):
            if g == 0:
                pltpu.make_async_copy(w_ref.at[pl.ds(0, cut)], wbuf.at[pl.ds(0, cut)], sems.at[2 + len(groups) + j]).wait()
            for v in range(unroll_sum):
                window_sums(j * unroll_sum + v, 0)
            return carry

        lax.fori_loop(0, PAIRS // (2 * unroll_sum), slice_sums, 0)

        if g == 0:
            pltpu.make_async_copy(t_ref, tbuf, sems.at[1]).wait()

        def lag_sums(h, carry):
            first, second = cross[2 * h], cross[2 * h + 1]
            real = jnp.concatenate([first[:, :128], second[:, :128]], axis=1)
            imag = jnp.concatenate([first[:, 128:], second[:, 128:]], axis=1)
            right = jnp.concatenate([real, imag], axis=0)
            out = jnp.dot(tbuf[...], right, preferred_element_type=jnp.float32)
            out = out * (1.0 / math.sqrt(W * FB))
            lags[pl.ds(2 * h, LAG_PAD, stride=pitch), :] = out[:, :128]
            lags[pl.ds(2 * h + 1, LAG_PAD, stride=pitch), :] = out[:, 128:]
            return carry

        lax.fori_loop(0, height // 2, lag_sums, 0, unroll=unroll_lag)
        at = pl.multiple_of(meta_ref[1 + g], height)
        back = pltpu.make_async_copy(stage, out_ref.at[:, pl.ds(at, height), :], sems.at[0])
        if g:
            pltpu.make_async_copy(stage, out_ref.at[:, pl.ds(0, height), :], sems.at[0]).wait()
        stage[...] = lags[...].reshape(LAG_PAD, pitch, 128)[:LAGS, :height].astype(jnp.bfloat16)
        back.start()
        if g == len(groups) - 1:
            back.wait()

    @pl.when(meta_ref[0] >= 0)
    def _():
        first = 0
        for g, size in enumerate(groups):
            for i in range(size):

                @pl.when(meta_ref[0] == i)
                def _(g=g, ref=x_refs[first + i]):
                    pltpu.make_async_copy(ref, xbuf.at[g], sems.at[2 + g]).start()

            first += size
            if g == 0:
                for j in range(PAIRS // cut):
                    at = pl.ds(j * cut, cut)
                    pltpu.make_async_copy(w_ref.at[at], wbuf.at[at], sems.at[2 + len(groups) + j]).start()
                pltpu.make_async_copy(t_ref, tbuf, sems.at[1]).start()
        for g in range(len(groups)):
            pltpu.make_async_copy(x_refs[0], xbuf.at[g], sems.at[2 + g]).wait()
            wide[...] = xbuf[g].astype(jnp.float32).reshape(ROWS * height, 128)
            one_group(g)


def pair_block(choice, members, right, table, out, unroll_sum=8, unroll_lag=8, pad=8):
    groups = [len(shards) for _, shards in members]
    shards = [shard for _, some in members for shard in some]
    count = len(shards)
    height = shards[0].shape[1]
    meta = jnp.stack([choice] + [place for place, _ in members]).astype(jnp.int32)
    anywhere = pl.BlockSpec(memory_space=pl.ANY)
    return pl.pallas_call(
        functools.partial(
            pair_kernel,
            groups=groups,
            height=height,
            unroll_sum=unroll_sum,
            unroll_lag=unroll_lag,
            pitch=height + pad,
        ),
        out_shape=jax.ShapeDtypeStruct(out.shape, out.dtype),
        grid_spec=pltpu.PrefetchScalarGridSpec(
            num_scalar_prefetch=1,
            grid=(),
            in_specs=[anywhere] * (count + 3),
            out_specs=anywhere,
            scratch_shapes=[
                pltpu.VMEM((len(groups), ROWS, height, 128), jnp.bfloat16),
                pltpu.VMEM((ROWS * height, 128), jnp.float32),
                pltpu.VMEM((PAIRS, 256, 256), jnp.bfloat16),
                pltpu.VMEM((LAG_PAD, 2 * FB), jnp.bfloat16),
                pltpu.VMEM((height, FB, 256), jnp.bfloat16),
                pltpu.VMEM((LAG_PAD * (height + pad), 128), jnp.float32),
                pltpu.VMEM((LAGS, height, 128), jnp.bfloat16),
                pltpu.SemaphoreType.DMA((2 + len(groups) + PAIRS // (2 * unroll_sum),)),
            ],
        ),
        input_output_aliases={count + 3: 0},
        compiler_params=pltpu.CompilerParams(vmem_limit_bytes=60 << 20),
        cost_estimate=pl.CostEstimate(
            flops=len(groups) * (2 * height * FB * 256 * 8 * 32 + 2 * height * 128 * 2 * FB * LAG_PAD),
            bytes_accessed=PAIRS * 256 * 256 * 2 + 2 * len(groups) * height * 128 * LAGS,
            transcendentals=0,
        ),
        name="pair_block",
    )(meta, *shards, right, table, out)


def make_table(band_range):
    order = jnp.arange(FB, dtype=jnp.int32)
    freq_index = (order % SEGMENTS) * ROWS + order // SEGMENTS
    lag_index = jnp.arange(LAG_PAD, dtype=jnp.int32) - LAGS // 2
    turns = jnp.mod((F0 + freq_index)[None, :] * lag_index[:, None], NFFT)
    theta = turns.astype(jnp.float32) * (2.0 * math.pi / NFFT)
    inband = ((freq_index >= band_range[0]) & (freq_index < band_range[1])).astype(jnp.float32)[None, :]
    return jnp.concatenate([inband * jnp.cos(theta), -inband * jnp.sin(theta)], axis=1).astype(jnp.bfloat16)


def relay_body(spectra, request, table):
    rows, sides = lax.axis_size("row"), lax.axis_size("side")
    axes = ("row", "plane", "side")
    row_id, plane, side = (lax.axis_index(name) for name in axes)
    width = spectra.shape[2]
    core, chip = row_id % 2, row_id // 2
    depth = plane - row_id
    devices = [(r, p, x) for r in range(rows) for p in range(rows) for x in range(sides)]

    def send(value, pairs):
        number = [tuple((r * rows + p) * sides + x for r, p, x in pair) for pair in pairs]
        return lax.ppermute(value, axes, number)

    def join(mine, sibling):
        first = jnp.where(core == 0, mine, sibling)
        second = jnp.where(core == 0, sibling, mine)
        return jnp.concatenate([first, second], axis=1)

    core_flip = [((r, p, x), (r ^ 1, p, x)) for r, p, x in devices]
    chip_flip = [((r, p, x), (r ^ 2, p, x)) for r, p, x in devices]

    shard = whiten(spectra, 1)[0]
    joined = join(shard, send(shard, core_flip))
    across = send(shard, chip_flip)
    def climb(value, d):
        return send(
            value,
            [
                ((r, p, x), (r, p + 1, x))
                for r, p, x in devices
                if p + 1 < rows and p - d + 1 >= 0 and (p - d + 1 - r) % 2 == 0
            ],
        )

    def to_row(value, d, flip_side, flip_chip):
        takers = [(r, p, x) for r, p, x in devices if p - r == d]
        return send(value, [((r ^ 2 * flip_chip, p, x ^ flip_side), (r, p, x)) for r, p, x in takers])

    after = lax.optimization_barrier
    once = climb(joined, 1)
    side_zero = to_row(joined, 0, 1, 0)
    once, table, across = after((once, table, across))
    twice = climb(once, 2)
    joined_across = join(across, send(across, core_flip))
    offsets = jnp.stack([2 * chip * width, 2 * (1 - chip) * width]).astype(jnp.int32)
    right, out = weights(offsets, [joined, joined_across], sides * rows * width)
    chip_one = to_row(once, 1, 0, 1)
    side_one = to_row(once, 1, 1, 0)
    twice, side_zero, side_one, joined_across = after((twice, side_zero, side_one, joined_across))
    thrice = climb(twice, 3)
    both_zero = to_row(joined_across, 0, 1, 0)
    chip_two = to_row(twice, 2, 0, 1)
    side_two = to_row(twice, 2, 1, 0)
    both_zero, chip_two, side_two, thrice, chip_one, right, out = after(
        (both_zero, chip_two, side_two, thrice, chip_one, right, out)
    )
    both_one = to_row(chip_one, 1, 1, 0)
    chip_three = to_row(thrice, 3, 0, 1)
    both_three = to_row(thrice, 3, 1, 1)
    side_three = to_row(thrice, 3, 1, 0)
    both_two = to_row(chip_two, 2, 1, 0)

    by_depth = jnp.where(request == 1, depth, -1)

    def place(flip_side, flip_chip):
        return ((side ^ flip_side) * rows + 2 * (chip ^ flip_chip)) * width

    own_of = (place(0, 0), [joined, once, twice, thrice])
    chips_of = (place(0, 1), [joined_across, chip_one, chip_two, chip_three])
    sides_of = (place(1, 0), [side_zero, side_one, side_two, side_three])
    boths_of = (place(1, 1), [both_zero, both_one, both_two, both_three])
    for members in ([own_of], [chips_of], [sides_of, boths_of]):
        out = pair_block(by_depth, members, right, table, out)
    return out


def gather_body(spectra, request, table):
    shard = whiten(spectra, 1)[0]
    width = shard.shape[1]
    rows = lax.axis_size("row")
    sides = lax.axis_size("side")
    column = lax.all_gather(shard, "row", axis=1, tiled=True)
    grouped = lax.all_gather(shard, ("plane", "side"), axis=0).reshape(rows, sides, ROWS, width, 128)
    moved = lax.all_to_all(grouped, "row", split_axis=0, concat_axis=0)
    block = jnp.transpose(moved, (2, 1, 0, 3, 4)).reshape(ROWS, sides * rows * width, 128)
    right, out = weights(jnp.zeros((1,), jnp.int32), [column], block.shape[1])
    group = min(64, block.shape[1])
    for at in range(0, block.shape[1], group):
        out = pair_block(request - 1, [(jnp.int32(at), [block[:, at : at + group]])], right, table, out)
    return out


def body(spectra, pair_mask, band_range):
    rows = lax.axis_size("row")
    sides = lax.axis_size("side")
    width = spectra.shape[2]
    request = ((pair_mask[0, 0] == 1) & (lax.axis_index("plane") >= lax.axis_index("row"))).astype(jnp.int32)
    table = make_table(band_range)
    if (rows, sides) == (4, 2) and width % 32 == 0:
        out = relay_body(spectra, request, table)
    else:
        out = gather_body(spectra, request, table)
    return jnp.transpose(out, (1, 2, 0))


def solution(mesh):
    rows, cols = mesh.devices.shape
    cut = Mesh(mesh.devices.reshape(rows, rows, cols // rows), ("row", "plane", "side"))
    return jax.shard_map(
        body,
        mesh=cut,
        in_specs=(P(None, None, ("plane", "side", "row"), None), P("row", ("plane", "side")), P()),
        out_specs=P("row", ("plane", "side"), None),
        check_vma=False,
    )
```

```python
import functools
import math

import jax
import jax.numpy as jnp
from jax import lax
from jax.experimental import pallas as pl
from jax.experimental.pallas import tpu as pltpu
from jax.sharding import Mesh
from jax.sharding import PartitionSpec as P

W = 16
FB = 512
LAGS = 201
NFFT = 15000
F0 = 60
EPS = 1e-06

SEGMENTS = 4
ROWS = FB // SEGMENTS
PAIRS = ROWS // 2
LAG_PAD = 208


def whiten_kernel(*refs, width, parts):
    x_refs, whole_ref, out_refs, scratch = refs[:SEGMENTS], refs[SEGMENTS], refs[SEGMENTS + 1 : -1], refs[-1]

    def channel(c, carry):
        tiles = [x_ref[pl.ds(c, 2 * W, stride=width), :] for x_ref in x_refs]
        total = sum(v[:W] * v[:W] + v[W:] * v[W:] for v in tiles)
        power = jnp.sum(total, axis=-1, keepdims=True) * (1.0 / FB)
        scale = lax.rsqrt(power + EPS)
        scale = jnp.concatenate([scale, scale], axis=0)
        stacked = jnp.concatenate([v * scale for v in tiles], axis=0)
        scratch[pl.ds(c, ROWS, stride=width), :] = stacked.T
        return carry

    lax.fori_loop(0, width, channel, 0, unroll=8)
    step = width // parts
    full = scratch[...].reshape(ROWS, width, 128).astype(jnp.bfloat16)
    whole_ref[...] = full
    for g, out_ref in enumerate(out_refs):
        out_ref[...] = full[:, g * step : (g + 1) * step, :]


def whiten(spectra, parts):
    width = spectra.shape[2]
    widths = [width] + ([width // parts] * parts if parts > 1 else [])
    lines = 2 * W * width
    flat = spectra.reshape(lines, FB)
    return pl.pallas_call(
        functools.partial(whiten_kernel, width=width, parts=parts),
        out_shape=[jax.ShapeDtypeStruct((ROWS, n, 128), jnp.bfloat16) for n in widths],
        grid=(1,),
        in_specs=[pl.BlockSpec((lines, ROWS), functools.partial(lambda q, i: (0, q), q)) for q in range(SEGMENTS)],
        out_specs=[pl.BlockSpec((ROWS, n, 128), lambda i: (0, 0, 0)) for n in widths],
        scratch_shapes=[pltpu.VMEM((ROWS * width, 128), jnp.float32)],
        compiler_params=pltpu.CompilerParams(vmem_limit_bytes=40 << 20),
        name="whiten",
    )(*[flat] * SEGMENTS)


def weights_kernel(offset_ref, *refs, count, step):
    in_refs, out_ref, clear_ref, scratch = refs[:count], refs[count], refs[count + 1], refs[count + 2]
    clear_ref[...] = jnp.zeros_like(clear_ref)
    for i in range(count):
        at = pl.multiple_of(offset_ref[i], step)
        scratch[:, pl.ds(at, step), :] = in_refs[i][...].astype(jnp.float32)

    def row(t, carry):
        for s in range(2):
            real = scratch[2 * t + s].T
            pieces = []
            for q in range(SEGMENTS):
                lo = q * 2 * W
                pieces += [-real[lo + W : lo + 2 * W], real[lo : lo + W]]
            imag = jnp.concatenate(pieces, axis=0)
            both = jnp.concatenate([real, imag], axis=1).astype(jnp.bfloat16)
            out_ref[t, s * 128 : (s + 1) * 128, :] = both
        return carry

    lax.fori_loop(0, out_ref.shape[0], row, 0, unroll=2)


def weights(offsets, shards, height):
    count = len(shards)
    step = shards[0].shape[1]
    tiles = 4
    return pl.pallas_call(
        functools.partial(weights_kernel, count=count, step=step),
        out_shape=[
            jax.ShapeDtypeStruct((PAIRS, 256, 256), jnp.bfloat16),
            jax.ShapeDtypeStruct((LAGS, height, count * step), jnp.bfloat16),
        ],
        grid_spec=pltpu.PrefetchScalarGridSpec(
            num_scalar_prefetch=1,
            grid=(tiles,),
            in_specs=[pl.BlockSpec((ROWS // tiles, step, 128), lambda i, o: (i, 0, 0))] * count,
            out_specs=[
                pl.BlockSpec((PAIRS // tiles, 256, 256), lambda i, o: (i, 0, 0)),
                pl.BlockSpec((LAGS, height // tiles, count * step), lambda i, o: (0, i, 0)),
            ],
            scratch_shapes=[pltpu.VMEM((ROWS // tiles, count * step, 128), jnp.float32)],
        ),
        compiler_params=pltpu.CompilerParams(vmem_limit_bytes=40 << 20),
        name="weights",
    )(offsets, *shards)


def pair_kernel(meta_ref, *refs, groups, height, unroll_sum, unroll_lag, pitch):
    count = sum(groups)
    x_refs = refs[:count]
    w_ref, t_ref, _, out_ref = refs[count : count + 4]
    xbuf, wide, wbuf, tbuf, cross, lags, stage, sems = refs[count + 4 :]
    cut = 2 * unroll_sum

    def one_group(g):
        sub = lax.broadcasted_iota(jnp.int32, (8, 128), 0)
        segment = lax.broadcasted_iota(jnp.int32, (8, 128), 1) // (2 * W)
        masks = (segment == sub, segment == sub - SEGMENTS)

        def window_sums(h, carry):
            halves = []
            for u in range(2):
                pair = 2 * h + u
                rows = []
                for a in range(height):
                    halves_of_k = [
                        jnp.where(masks[s], wide[pl.ds((2 * pair + s) * height + a, 8, stride=0), :], 0.0)
                        for s in range(2)
                    ]
                    rows.append(jnp.concatenate(halves_of_k, axis=1))
                left = jnp.concatenate(rows, axis=0).astype(jnp.bfloat16)
                sums = jnp.dot(left, wbuf[pair], preferred_element_type=jnp.float32)
                halves.append(sums.reshape(height, 8, 256))
            both = jnp.concatenate(halves, axis=1).astype(jnp.bfloat16)
            cross[:, pl.ds(pl.multiple_of(h * 16, 16), 16), :] = both
            return carry

        def slice_sums(j, carry):
            if g == 0:
                pltpu.make_async_copy(w_ref.at[pl.ds(0, cut)], wbuf.at[pl.ds(0, cut)], sems.at[2 + len(groups) + j]).wait()
            for v in range(unroll_sum):
                window_sums(j * unroll_sum + v, 0)
            return carry

        lax.fori_loop(0, PAIRS // (2 * unroll_sum), slice_sums, 0)

        if g == 0:
            pltpu.make_async_copy(t_ref, tbuf, sems.at[1]).wait()

        def lag_sums(h, carry):
            first, second = cross[2 * h], cross[2 * h + 1]
            real = jnp.concatenate([first[:, :128], second[:, :128]], axis=1)
            imag = jnp.concatenate([first[:, 128:], second[:, 128:]], axis=1)
            right = jnp.concatenate([real, imag], axis=0)
            out = jnp.dot(tbuf[...], right, preferred_element_type=jnp.float32)
            out = out * (1.0 / math.sqrt(W * FB))
            lags[pl.ds(2 * h, LAG_PAD, stride=pitch), :] = out[:, :128]
            lags[pl.ds(2 * h + 1, LAG_PAD, stride=pitch), :] = out[:, 128:]
            return carry

        lax.fori_loop(0, height // 2, lag_sums, 0, unroll=unroll_lag)
        at = pl.multiple_of(meta_ref[1 + g], height)
        back = pltpu.make_async_copy(stage, out_ref.at[:, pl.ds(at, height), :], sems.at[0])
        if g:
            pltpu.make_async_copy(stage, out_ref.at[:, pl.ds(0, height), :], sems.at[0]).wait()
        stage[...] = lags[...].reshape(LAG_PAD, pitch, 128)[:LAGS, :height].astype(jnp.bfloat16)
        back.start()
        if g == len(groups) - 1:
            back.wait()

    @pl.when(meta_ref[0] >= 0)
    def _():
        first = 0
        for g, size in enumerate(groups):
            for i in range(size):

                @pl.when(meta_ref[0] == i)
                def _(g=g, ref=x_refs[first + i]):
                    pltpu.make_async_copy(ref, xbuf.at[g], sems.at[2 + g]).start()

            first += size
            if g == 0:
                for j in range(PAIRS // cut):
                    at = pl.ds(j * cut, cut)
                    pltpu.make_async_copy(w_ref.at[at], wbuf.at[at], sems.at[2 + len(groups) + j]).start()
                pltpu.make_async_copy(t_ref, tbuf, sems.at[1]).start()
        for g in range(len(groups)):
            pltpu.make_async_copy(x_refs[0], xbuf.at[g], sems.at[2 + g]).wait()
            wide[...] = xbuf[g].astype(jnp.float32).reshape(ROWS * height, 128)
            one_group(g)


def pair_block(choice, members, right, table, out, unroll_sum=8, unroll_lag=16, pad=8):
    groups = [len(shards) for _, shards in members]
    shards = [shard for _, some in members for shard in some]
    count = len(shards)
    height = shards[0].shape[1]
    meta = jnp.stack([choice] + [place for place, _ in members]).astype(jnp.int32)
    anywhere = pl.BlockSpec(memory_space=pl.ANY)
    return pl.pallas_call(
        functools.partial(
            pair_kernel,
            groups=groups,
            height=height,
            unroll_sum=unroll_sum,
            unroll_lag=unroll_lag,
            pitch=height + pad,
        ),
        out_shape=jax.ShapeDtypeStruct(out.shape, out.dtype),
        grid_spec=pltpu.PrefetchScalarGridSpec(
            num_scalar_prefetch=1,
            grid=(),
            in_specs=[anywhere] * (count + 3),
            out_specs=anywhere,
            scratch_shapes=[
                pltpu.VMEM((len(groups), ROWS, height, 128), jnp.bfloat16),
                pltpu.VMEM((ROWS * height, 128), jnp.float32),
                pltpu.VMEM((PAIRS, 256, 256), jnp.bfloat16),
                pltpu.VMEM((LAG_PAD, 2 * FB), jnp.bfloat16),
                pltpu.VMEM((height, FB, 256), jnp.bfloat16),
                pltpu.VMEM((LAG_PAD * (height + pad), 128), jnp.float32),
                pltpu.VMEM((LAGS, height, 128), jnp.bfloat16),
                pltpu.SemaphoreType.DMA((2 + len(groups) + PAIRS // (2 * unroll_sum),)),
            ],
        ),
        input_output_aliases={count + 3: 0},
        compiler_params=pltpu.CompilerParams(vmem_limit_bytes=60 << 20),
        cost_estimate=pl.CostEstimate(
            flops=len(groups) * (2 * height * FB * 256 * 8 * 32 + 2 * height * 128 * 2 * FB * LAG_PAD),
            bytes_accessed=PAIRS * 256 * 256 * 2 + 2 * len(groups) * height * 128 * LAGS,
            transcendentals=0,
        ),
        name="pair_block",
    )(meta, *shards, right, table, out)


def make_table(band_range):
    order = jnp.arange(FB, dtype=jnp.int32)
    freq_index = (order % SEGMENTS) * ROWS + order // SEGMENTS
    lag_index = jnp.arange(LAG_PAD, dtype=jnp.int32) - LAGS // 2
    turns = jnp.mod((F0 + freq_index)[None, :] * lag_index[:, None], NFFT)
    theta = turns.astype(jnp.float32) * (2.0 * math.pi / NFFT)
    inband = ((freq_index >= band_range[0]) & (freq_index < band_range[1])).astype(jnp.float32)[None, :]
    return jnp.concatenate([inband * jnp.cos(theta), -inband * jnp.sin(theta)], axis=1).astype(jnp.bfloat16)


def relay_body(spectra, request, table):
    rows, sides = lax.axis_size("row"), lax.axis_size("side")
    axes = ("row", "plane", "side")
    row_id, plane, side = (lax.axis_index(name) for name in axes)
    width = spectra.shape[2]
    core, chip = row_id % 2, row_id // 2
    depth = plane - row_id
    devices = [(r, p, x) for r in range(rows) for p in range(rows) for x in range(sides)]

    def send(value, pairs):
        number = [tuple((r * rows + p) * sides + x for r, p, x in pair) for pair in pairs]
        return lax.ppermute(value, axes, number)

    def join(mine, sibling):
        first = jnp.where(core == 0, mine, sibling)
        second = jnp.where(core == 0, sibling, mine)
        return jnp.concatenate([first, second], axis=1)

    core_flip = [((r, p, x), (r ^ 1, p, x)) for r, p, x in devices]
    chip_flip = [((r, p, x), (r ^ 2, p, x)) for r, p, x in devices]

    shard = whiten(spectra, 1)[0]
    joined = join(shard, send(shard, core_flip))
    across = send(shard, chip_flip)
    def climb(value, d):
        return send(
            value,
            [
                ((r, p, x), (r, p + 1, x))
                for r, p, x in devices
                if p + 1 < rows and p - d + 1 >= 0 and (p - d + 1 - r) % 2 == 0
            ],
        )

    def to_row(value, d, flip_side, flip_chip):
        takers = [(r, p, x) for r, p, x in devices if p - r == d]
        return send(value, [((r ^ 2 * flip_chip, p, x ^ flip_side), (r, p, x)) for r, p, x in takers])

    after = lax.optimization_barrier
    once = climb(joined, 1)
    side_zero = to_row(joined, 0, 1, 0)
    once, table, across = after((once, table, across))
    twice = climb(once, 2)
    joined_across = join(across, send(across, core_flip))
    offsets = jnp.stack([2 * chip * width, 2 * (1 - chip) * width]).astype(jnp.int32)
    right, out = weights(offsets, [joined, joined_across], sides * rows * width)
    chip_one = to_row(once, 1, 0, 1)
    side_one = to_row(once, 1, 1, 0)
    twice, side_zero, side_one, joined_across = after((twice, side_zero, side_one, joined_across))
    thrice = climb(twice, 3)
    both_zero = to_row(joined_across, 0, 1, 0)
    chip_two = to_row(twice, 2, 0, 1)
    side_two = to_row(twice, 2, 1, 0)
    both_zero, chip_two, side_two, thrice, chip_one, right, out = after(
        (both_zero, chip_two, side_two, thrice, chip_one, right, out)
    )
    both_one = to_row(chip_one, 1, 1, 0)
    chip_three = to_row(thrice, 3, 0, 1)
    both_three = to_row(thrice, 3, 1, 1)
    side_three = to_row(thrice, 3, 1, 0)
    both_two = to_row(chip_two, 2, 1, 0)

    by_depth = jnp.where(request == 1, depth, -1)

    def place(flip_side, flip_chip):
        return ((side ^ flip_side) * rows + 2 * (chip ^ flip_chip)) * width

    own_of = (place(0, 0), [joined, once, twice, thrice])
    chips_of = (place(0, 1), [joined_across, chip_one, chip_two, chip_three])
    sides_of = (place(1, 0), [side_zero, side_one, side_two, side_three])
    boths_of = (place(1, 1), [both_zero, both_one, both_two, both_three])
    for members in ([own_of], [chips_of], [sides_of, boths_of]):
        out = pair_block(by_depth, members, right, table, out)
    return out


def gather_body(spectra, request, table):
    shard = whiten(spectra, 1)[0]
    width = shard.shape[1]
    rows = lax.axis_size("row")
    sides = lax.axis_size("side")
    column = lax.all_gather(shard, "row", axis=1, tiled=True)
    grouped = lax.all_gather(shard, ("plane", "side"), axis=0).reshape(rows, sides, ROWS, width, 128)
    moved = lax.all_to_all(grouped, "row", split_axis=0, concat_axis=0)
    block = jnp.transpose(moved, (2, 1, 0, 3, 4)).reshape(ROWS, sides * rows * width, 128)
    right, out = weights(jnp.zeros((1,), jnp.int32), [column], block.shape[1])
    group = min(64, block.shape[1])
    for at in range(0, block.shape[1], group):
        out = pair_block(request - 1, [(jnp.int32(at), [block[:, at : at + group]])], right, table, out)
    return out


def body(spectra, pair_mask, band_range):
    rows = lax.axis_size("row")
    sides = lax.axis_size("side")
    width = spectra.shape[2]
    request = ((pair_mask[0, 0] == 1) & (lax.axis_index("plane") >= lax.axis_index("row"))).astype(jnp.int32)
    table = make_table(band_range)
    if (rows, sides) == (4, 2) and width % 32 == 0:
        out = relay_body(spectra, request, table)
    else:
        out = gather_body(spectra, request, table)
    return jnp.transpose(out, (1, 2, 0))


def solution(mesh):
    rows, cols = mesh.devices.shape
    cut = Mesh(mesh.devices.reshape(rows, rows, cols // rows), ("row", "plane", "side"))
    return jax.shard_map(
        body,
        mesh=cut,
        in_specs=(P(None, None, ("plane", "side", "row"), None), P("row", ("plane", "side")), P()),
        out_specs=P("row", ("plane", "side"), None),
        check_vma=False,
    )
```
